32 devices in a mesh: dp: 8 (over z, y), tensor: 4 (over x, core).
Axes of the slice: x: 2, y: 2, z: 4, core: 2. Of those that a mesh axis runs over, the one named last changes fastest.
Arguments:
- text_in: bfloat16 [8192, 768], P(('dp', 'tensor')), may hold values from -6 to 6
- image_in: bfloat16 [2304, 1024], P(('dp', 'tensor')), may hold values from -6 to 6
- text_len: int32 [64], P('dp'), may hold values from 8 to 128, as said below
- region_count: int32 [64], P('dp'), may hold values from 10 to 36, as said below
- co_query_text: bfloat16 [768, 1024], P(None, 'tensor'), may hold values from -0.21875 to 0.21875
- co_kv_image: bfloat16 [2, 1024, 1024], P(None, None, 'tensor'), may hold values from -0.1875 to 0.1875
- co_out_text: bfloat16 [1024, 768], P('tensor'), may hold values from -0.75 to 0.75
- co_query_image: bfloat16 [1024, 1024], P(None, 'tensor'), may hold values from -0.1875 to 0.1875
- co_kv_text: bfloat16 [2, 768, 1024], P(None, None, 'tensor'), may hold values from -0.21875 to 0.21875
- co_out_image: bfloat16 [1024, 1024], P('tensor'), may hold values from -1.5 to 1.5
- co_ff_text_in: bfloat16 [768, 3072], P(None, 'tensor'), may hold values from -0.21875 to 0.21875
- co_ff_text_out: bfloat16 [3072, 768], P('tensor'), may hold values from -0.109375 to 0.109375
- co_ff_image_in: bfloat16 [1024, 1024], P(None, 'tensor'), may hold values from -0.1875 to 0.1875
- co_ff_image_out: bfloat16 [1024, 1024], P('tensor'), may hold values from -0.1875 to 0.1875
- self_qkv_text: bfloat16 [3, 768, 768], P(None, None, 'tensor'), may hold values from -0.21875 to 0.21875
- self_out_text: bfloat16 [768, 768], P('tensor'), may hold values from -1.75 to 1.75
- self_ff_text_in: bfloat16 [768, 3072], P(None, 'tensor'), may hold values from -0.21875 to 0.21875
- self_ff_text_out: bfloat16 [3072, 768], P('tensor'), may hold values from -0.109375 to 0.109375
- self_qkv_image: bfloat16 [3, 1024, 1024], P(None, None, 'tensor'), may hold values from -0.1875 to 0.1875
- self_out_image: bfloat16 [1024, 1024], P('tensor'), may hold values from -0.75 to 0.75
- self_ff_image_in: bfloat16 [1024, 1024], P(None, 'tensor'), may hold values from -0.1875 to 0.1875
- self_ff_image_out: bfloat16 [1024, 1024], P('tensor'), may hold values from -0.1875 to 0.1875
- text_gains: float32 [4, 768], replicated, may hold values from 0.25 to 1.75
- text_biases: float32 [4, 768], replicated, may hold values from -3 to 3
- image_gains: float32 [4, 1024], replicated, may hold values from 0.25 to 1.75
- image_biases: float32 [4, 1024], replicated, may hold values from -3 to 3
- text_cot: bfloat16 [8192, 768], P(('dp', 'tensor')), may hold values from -6 to 6
- image_cot: bfloat16 [2304, 1024], P(('dp', 'tensor')), may hold values from -6 to 6
Outputs:
- text_out: bfloat16 [8192, 768], P(('dp', 'tensor'))
- image_out: bfloat16 [2304, 1024], P(('dp', 'tensor'))
- text_in_grad: bfloat16 [8192, 768], P(('dp', 'tensor'))
- image_in_grad: bfloat16 [2304, 1024], P(('dp', 'tensor'))
- co_query_text_grad: float32 [768, 1024], P('dp', 'tensor')
- co_kv_image_grad: float32 [2, 1024, 1024], P(None, 'dp', 'tensor')
- co_out_text_grad: float32 [1024, 768], P('tensor', 'dp')
- co_query_image_grad: float32 [1024, 1024], P('dp', 'tensor')
- co_kv_text_grad: float32 [2, 768, 1024], P(None, 'dp', 'tensor')
- co_out_image_grad: float32 [1024, 1024], P('tensor', 'dp')
- co_ff_text_in_grad: float32 [768, 3072], P('dp', 'tensor')
- co_ff_text_out_grad: float32 [3072, 768], P('tensor', 'dp')
- co_ff_image_in_grad: float32 [1024, 1024], P('dp', 'tensor')
- co_ff_image_out_grad: float32 [1024, 1024], P('tensor', 'dp')
- self_qkv_text_grad: float32 [3, 768, 768], P(None, 'dp', 'tensor')
- self_out_text_grad: float32 [768, 768], P('tensor', 'dp')
- self_ff_text_in_grad: float32 [768, 3072], P('dp', 'tensor')
- self_ff_text_out_grad: float32 [3072, 768], P('tensor', 'dp')
- self_qkv_image_grad: float32 [3, 1024, 1024], P(None, 'dp', 'tensor')
- self_out_image_grad: float32 [1024, 1024], P('tensor', 'dp')
- self_ff_image_in_grad: float32 [1024, 1024], P('dp', 'tensor')
- self_ff_image_out_grad: float32 [1024, 1024], P('tensor', 'dp')
- text_gains_grad: float32 [4, 768], replicated
- text_biases_grad: float32 [4, 768], replicated
- image_gains_grad: float32 [4, 1024], replicated
- image_biases_grad: float32 [4, 1024], replicated
The draws below stay inside these ranges and needn't reach their ends.
Inputs may be any that keep to these rules, and one draw needn't show every extreme that they name: `text_len`: caption length of each pair; text positions at or past it are padding; both 8 and 128 occur in every draw. `region_count`: regions of each pair; region slots at or past it are empty; both 10 and 36 occur in every draw.
All inputs are finite; a program needn't handle non-finite values.
Results may differ from the reference program's by a relative error of at most 0.04.
Values may be sent and summed in bfloat16 or wider, within the bound.
A program may use at most 192 MiB of HBM per device.

```python
import math
import jax
import jax.numpy as jnp
from jax import lax

DT = 768
HT = 12
KT = 64
FT = 3072
DV = 1024
HV = 8
KV = 128
FV = 1024
DC = 1024
HC = 8
KC = 128
LT = 128
RG = 36
MINLEN = 8
MINREG = 10
PAIRS = 64
TEXT_ROWS = 8192
IMAGE_ROWS = 2304


def ragged_counts(key, lowest_count, highest_count):
    key_base, key_top, key_gap = jax.random.split(key, 3)
    drawn = jax.random.randint(key_base, (PAIRS,), lowest_count, highest_count + 1)
    top_place = jax.random.randint(key_top, (), 0, PAIRS)
    low_place = (top_place + 1 + jax.random.randint(key_gap, (), 0, PAIRS - 1)) % PAIRS
    positions = jnp.arange(PAIRS, dtype=jnp.int32)
    drawn = jnp.where(positions == top_place, highest_count, drawn)
    drawn = jnp.where(positions == low_place, lowest_count, drawn)
    return drawn.astype(jnp.int32)


def draw_text_len(key, part):
    return ragged_counts(jax.random.fold_in(key, 11), MINLEN, LT)


def draw_region_count(key, part):
    return ragged_counts(jax.random.fold_in(key, 23), MINREG, RG)


def shard_levels(stream_key, dims, cuts, least, largest):
    loudness, own = 1.0, jax.random.fold_in(stream_key, 6)
    for axis_at, parts in cuts:
        heights = jnp.exp(jax.random.uniform(jax.random.fold_in(own, axis_at), (parts,), jnp.float32, least / len(cuts), largest / len(cuts)))
        loudness = loudness * jnp.repeat(heights, dims[axis_at] // parts).reshape([-1 if axis == axis_at else 1 for axis in range(len(dims))])
    return loudness


def bell_draw(key, shape, scale, limit, shards=(), kind=jnp.bfloat16):
    factor_of = shard_levels(key, shape, shards, -0.22, 0.18) if shards else 1.0
    values = jax.random.normal(key, shape, jnp.float32) * scale * factor_of
    return jnp.minimum(jnp.maximum(values, -limit), limit).astype(kind)


def setup_inputs(seed: int = 0) -> dict:
    keys = jax.random.split(jax.random.key(seed), 29)
    text_in = bell_draw(keys[0], (TEXT_ROWS, DT), 1.0, 6.0, ((0, 32),))
    image_in = bell_draw(keys[1], (IMAGE_ROWS, DV), 1.0, 6.0, ((0, 32),))
    text_len = draw_text_len(jax.random.fold_in(keys[28], 71), 0)
    region_count = draw_region_count(jax.random.fold_in(keys[28], 71), 0)
    co_query_text = bell_draw(keys[4], (DT, DC), DT ** -0.5, 0.21875, ((1, 4),))
    co_kv_image = bell_draw(keys[5], (2, DV, DC), DV ** -0.5, 0.1875, ((2, 4),))
    co_out_text = bell_draw(keys[6], (DC, DT), (DC * 2 // RG) ** -0.5, 0.75, ((0, 4),))
    co_query_image = bell_draw(keys[7], (DV, DC), DV ** -0.5, 0.1875, ((1, 4),))
    co_kv_text = bell_draw(keys[8], (2, DT, DC), DT ** -0.5, 0.21875, ((2, 4),))
    co_out_image = bell_draw(keys[9], (DC, DV), (DC * 2 // LT) ** -0.5, 1.5, ((0, 4),))
    co_ff_text_in = bell_draw(keys[10], (DT, FT), DT ** -0.5, 0.21875, ((1, 4),))
    co_ff_text_out = bell_draw(keys[11], (FT, DT), FT ** -0.5, 0.109375, ((0, 4),))
    co_ff_image_in = bell_draw(keys[12], (DV, FV), DV ** -0.5, 0.1875, ((1, 4),))
    co_ff_image_out = bell_draw(keys[13], (FV, DV), FV ** -0.5, 0.1875, ((0, 4),))
    self_qkv_text = bell_draw(keys[14], (3, DT, DT), DT ** -0.5, 0.21875, ((2, 4),))
    self_out_text = bell_draw(keys[15], (DT, DT), (DT * 2 // LT) ** -0.5, 1.75, ((0, 4),))
    self_ff_text_in = bell_draw(keys[16], (DT, FT), DT ** -0.5, 0.21875, ((1, 4),))
    self_ff_text_out = bell_draw(keys[17], (FT, DT), FT ** -0.5, 0.109375, ((0, 4),))
    self_qkv_image = bell_draw(keys[18], (3, DV, DV), DV ** -0.5, 0.1875, ((2, 4),))
    self_out_image = bell_draw(keys[19], (DV, DV), (DV * 2 // RG) ** -0.5, 0.75, ((0, 4),))
    self_ff_image_in = bell_draw(keys[20], (DV, FV), DV ** -0.5, 0.1875, ((1, 4),))
    self_ff_image_out = bell_draw(keys[21], (FV, DV), FV ** -0.5, 0.1875, ((0, 4),))
    text_gains = jnp.clip(1.0 + 0.15 * jax.random.normal(keys[22], (4, DT), jnp.float32), 0.25, 1.75)
    text_biases = bell_draw(keys[23], (4, DT), 0.5, 3.0, (), jnp.float32)
    image_gains = jnp.clip(1.0 + 0.15 * jax.random.normal(keys[24], (4, DV), jnp.float32), 0.25, 1.75)
    image_biases = bell_draw(keys[25], (4, DV), 0.5, 3.0, (), jnp.float32)
    text_cot = bell_draw(keys[26], (TEXT_ROWS, DT), 1.0, 6.0, ((0, 32),))
    image_cot = bell_draw(keys[27], (IMAGE_ROWS, DV), 1.0, 6.0, ((0, 32),))
    return {"text_in": text_in, "image_in": image_in, "text_len": text_len, "region_count": region_count, "co_query_text": co_query_text, "co_kv_image": co_kv_image, "co_out_text": co_out_text, "co_query_image": co_query_image, "co_kv_text": co_kv_text, "co_out_image": co_out_image, "co_ff_text_in": co_ff_text_in, "co_ff_text_out": co_ff_text_out, "co_ff_image_in": co_ff_image_in, "co_ff_image_out": co_ff_image_out, "self_qkv_text": self_qkv_text, "self_out_text": self_out_text, "self_ff_text_in": self_ff_text_in, "self_ff_text_out": self_ff_text_out, "self_qkv_image": self_qkv_image, "self_out_image": self_out_image, "self_ff_image_in": self_ff_image_in, "self_ff_image_out": self_ff_image_out, "text_gains": text_gains, "text_biases": text_biases, "image_gains": image_gains, "image_biases": image_biases, "text_cot": text_cot, "image_cot": image_cot}


highest = lax.Precision.HIGHEST
epsilon = 1e-05
masked_score = -1e+30

@jax.custom_vjp
def low(v):
    return lax.optimization_barrier(v.astype(jnp.bfloat16)).astype(jnp.float32)

@jax.custom_vjp
def low_back(v):
    return v

def low_keep(v):
    return (low(v), None)

def low_pass(kept, grad):
    return (grad,)

def back_keep(v):
    return (v, None)

def back_low(kept, grad):
    return (low(grad),)
low.defvjp(low_keep, low_pass)
low_back.defvjp(back_keep, back_low)

def round_both(values_in):
    return low(low_back(values_in))

def product(left, right):
    return jnp.dot(left, right, precision=highest)

def layer_norm(row_block, gain_row, bias_row):
    row_mean = lax.optimization_barrier(jnp.mean(row_block, axis=-1, keepdims=True))
    centered = row_block - row_mean
    variance = lax.optimization_barrier(jnp.mean(centered * centered, axis=-1, keepdims=True))
    return centered * lax.rsqrt(variance + epsilon) * gain_row + bias_row

def attend(query_in, keys_in, w_query, w_key, w_value, w_out, key_count, head_count, head_size):
    pair_count = key_count.shape[0]
    queries = round_both(product(query_in, w_query)).reshape(pair_count, -1, head_count, head_size)
    key_rows = round_both(product(keys_in, w_key)).reshape(pair_count, -1, head_count, head_size)
    value_rows = round_both(product(keys_in, w_value)).reshape(pair_count, -1, head_count, head_size)
    raw_scores = low_back(jnp.einsum('pqhk,pshk->phqs', queries, key_rows, precision=highest))
    scores = raw_scores * (1.0 / math.sqrt(head_size))
    valid_keys = jnp.arange(key_rows.shape[1], dtype=jnp.int32)[None, :] < key_count[:, None]
    scores = jnp.where(valid_keys[:, None, None, :], scores, masked_score)
    attn_probs = low(jax.nn.softmax(scores, axis=-1))
    mixed_heads = round_both(jnp.einsum('phqs,pshk->pqhk', attn_probs, value_rows, precision=highest))
    return low_back(product(mixed_heads.reshape(query_in.shape[0], head_count * head_size), w_out))

def feed(rows_in, w_in, w_out):
    inner_rows = low_back(product(rows_in, w_in))
    act_rows = low(jax.nn.gelu(inner_rows, approximate=False))
    return low_back(product(act_rows, w_out))

def forward(weight_set, text_x, image_x, text_count, region_total):
    co_query_text, co_kv_image, co_out_text, co_query_image, co_kv_text, co_out_image, co_ff_text_in, co_ff_text_out, co_ff_image_in, co_ff_image_out, self_qkv_text, self_out_text, self_ff_text_in, self_ff_text_out, self_qkv_image, self_out_image, self_ff_image_in, self_ff_image_out, text_gains, text_biases, image_gains, image_biases = weight_set
    text_att = attend(text_x, image_x, co_query_text, co_kv_image[0], co_kv_image[1], co_out_text, region_total, HC, KC)
    image_att = attend(image_x, text_x, co_query_image, co_kv_text[0], co_kv_text[1], co_out_image, text_count, HC, KC)
    text_one = layer_norm(text_x + text_att, text_gains[0], text_biases[0])
    image_one = layer_norm(image_x + image_att, image_gains[0], image_biases[0])
    text_two = layer_norm(text_one + feed(low(text_one), co_ff_text_in, co_ff_text_out), text_gains[1], text_biases[1])
    image_two = layer_norm(image_one + feed(low(image_one), co_ff_image_in, co_ff_image_out), image_gains[1], image_biases[1])
    text_low = low(text_two)
    image_low = low(image_two)
    text_self = attend(text_low, text_low, self_qkv_text[0], self_qkv_text[1], self_qkv_text[2], self_out_text, text_count, HT, KT)
    image_self = attend(image_low, image_low, self_qkv_image[0], self_qkv_image[1], self_qkv_image[2], self_out_image, region_total, HV, KV)
    text_three = layer_norm(text_two + text_self, text_gains[2], text_biases[2])
    image_three = layer_norm(image_two + image_self, image_gains[2], image_biases[2])
    text_four = layer_norm(text_three + feed(low(text_three), self_ff_text_in, self_ff_text_out), text_gains[3], text_biases[3])
    image_four = layer_norm(image_three + feed(low(image_three), self_ff_image_in, self_ff_image_out), image_gains[3], image_biases[3])
    return (text_four, image_four)

def reference(text_in, image_in, text_len, region_count, co_query_text, co_kv_image, co_out_text, co_query_image, co_kv_text, co_out_image, co_ff_text_in, co_ff_text_out, co_ff_image_in, co_ff_image_out, self_qkv_text, self_out_text, self_ff_text_in, self_ff_text_out, self_qkv_image, self_out_image, self_ff_image_in, self_ff_image_out, text_gains, text_biases, image_gains, image_biases, text_cot, image_cot):
    block_pairs = math.gcd(PAIRS, 16)
    block_count = PAIRS // block_pairs
    weight_set = tuple((weight.astype(jnp.float32) for weight in (co_query_text, co_kv_image, co_out_text, co_query_image, co_kv_text, co_out_image, co_ff_text_in, co_ff_text_out, co_ff_image_in, co_ff_image_out, self_qkv_text, self_out_text, self_ff_text_in, self_ff_text_out, self_qkv_image, self_out_image, self_ff_image_in, self_ff_image_out, text_gains, text_biases, image_gains, image_biases)))
    zero_grads = tuple((jnp.zeros(weight.shape, jnp.float32) for weight in weight_set))

    def scan_step(totals, inputs):
        text_x, image_x, text_count, region_total, text_grad, image_grad = inputs

        def forward_block(weight_list, text_rows, image_rows):
            return forward(weight_list, text_rows, image_rows, text_count, region_total)
        outputs, pull_back = jax.vjp(forward_block, weight_set, text_x, image_x)
        weight_grads, text_back, image_back = pull_back((text_grad, image_grad))
        totals = tuple((left + right for left, right in zip(totals, weight_grads)))
        return (totals, (outputs[0].astype(jnp.bfloat16), outputs[1].astype(jnp.bfloat16), text_back.astype(jnp.bfloat16), image_back.astype(jnp.bfloat16)))
    inputs = (text_in.astype(jnp.float32).reshape(block_count, block_pairs * LT, DT), image_in.astype(jnp.float32).reshape(block_count, block_pairs * RG, DV), text_len.reshape(block_count, block_pairs), region_count.reshape(block_count, block_pairs), text_cot.astype(jnp.float32).reshape(block_count, block_pairs * LT, DT), image_cot.astype(jnp.float32).reshape(block_count, block_pairs * RG, DV))
    totals, (text_out, image_out, text_in_grad, image_in_grad) = lax.scan(scan_step, zero_grads, inputs)
    return (text_out.reshape(TEXT_ROWS, DT), image_out.reshape(IMAGE_ROWS, DV), text_in_grad.reshape(TEXT_ROWS, DT), image_in_grad.reshape(IMAGE_ROWS, DV), totals[0], totals[1], totals[2], totals[3], totals[4], totals[5], totals[6], totals[7], totals[8], totals[9], totals[10], totals[11], totals[12], totals[13], totals[14], totals[15], totals[16], totals[17], totals[18], totals[19], totals[20], totals[21])
```

```python
import functools
import math

import jax
import jax.numpy as jnp
from jax import lax
from jax.experimental import pallas as pl
from jax.experimental.pallas import tpu as pltpu
from jax.sharding import PartitionSpec as P

KT = 64
KV = 128
KC = 128
LT = 128
RG = 36
RT = 256
RI = 72
RP = 80
DT = 768
DV = 1024

epsilon = 1e-05
masked_score = -1e30
F32 = jnp.float32
BF16 = jnp.bfloat16
MESH = pl.DeviceIdType.MESH
VM = pl.BlockSpec(memory_space=pltpu.VMEM)
SM = pl.BlockSpec(memory_space=pltpu.SMEM)
ANY = pl.BlockSpec(memory_space=pl.ANY)


def mm(a, b):
    return lax.dot_general(a, b, (((1,), (0,)), ((), ())), preferred_element_type=F32)


def mm_nt(a, b):
    return lax.dot_general(a, b, (((1,), (1,)), ((), ())), preferred_element_type=F32)


def mm_tn(a, b):
    return lax.dot_general(a, b, (((0,), (0,)), ((), ())), preferred_element_type=F32)


class Places:
    def __init__(self):
        me = lax.axis_index("tensor")
        chip, core = lax.div(me, 2), lax.rem(me, 2)
        self.me = me
        self.core_mate = 2 * chip + (1 - core)
        self.chip_mate = 2 * (1 - chip) + core
        self.far = 2 * (1 - chip) + (1 - core)

    def block(self, phase):
        return [self.me, self.core_mate, self.chip_mate, self.far][phase]

    def greet(self):
        barrier = pltpu.get_barrier_semaphore()
        for mate in (self.core_mate, self.chip_mate):
            pl.semaphore_signal(barrier, inc=1, device_id={"tensor": mate}, device_id_type=MESH)
        pl.semaphore_wait(barrier, 2)


def push(src, dst, sends, recvs, slot, mate):
    return pltpu.make_async_remote_copy(
        src_ref=src,
        dst_ref=dst,
        send_sem=sends.at[slot],
        recv_sem=recvs.at[slot],
        device_id={"tensor": mate},
        device_id_type=MESH,
    )


class Stream:
    def __init__(self, at, slots, own, near, relay, out, got_near, got_far, got_chip, sends, recvs, base):
        self.at, self.slots, self.own = at, slots, own
        self.near, self.relay, self.out = near, relay, out
        self.got_near, self.got_far, self.got_chip = got_near, got_far, got_chip
        me, cm, xm = at.me, at.core_mate, at.chip_mate
        self.g_core = push(slots.at[me], slots.at[me], sends, recvs, base + 0, cm)
        self.g_chip = push(slots.at[me], slots.at[me], sends, recvs, base + 1, xm)
        self.g_far = push(slots.at[xm], slots.at[xm], sends, recvs, base + 2, cm)
        self.s_near = push(near, got_near, sends, recvs, base + 3, cm)
        self.s_relay = push(relay, got_far, sends, recvs, base + 4, cm)
        self.s_out = push(out, got_chip, sends, recvs, base + 5, xm)

    def begin(self, rows):
        self.slots[self.at.me] = rows
        self.g_chip.start()
        self.g_core.start()

    def ready(self, phase):
        if phase == 1:
            self.g_core.wait_recv()
        if phase == 2:
            self.g_chip.wait_recv()
            self.g_far.start()
        if phase == 3:
            self.g_far.wait_recv()

    def partial(self, phase, value):
        if phase == 0:
            self.own[0] = value
        if phase == 1:
            self.near[...] = value.astype(BF16)
            self.s_near.start()
        if phase == 2:
            self.own[1] = value
        if phase == 3:
            self.relay[...] = value.astype(BF16)
            self.s_relay.start()

    def forward(self):
        self.s_relay.wait_recv()
        self.out[...] = (self.own[1] + self.got_far[...].astype(F32)).astype(BF16)
        self.s_out.start()

    def total(self):
        self.s_near.wait_recv()
        self.s_out.wait_recv()
        return self.own[0] + self.got_near[...].astype(F32) + self.got_chip[...].astype(F32)

    def end(self):
        for copy in (self.g_core, self.g_chip, self.g_far, self.s_near, self.s_relay, self.s_out):
            copy.wait_send()


def stream_scratch(rows, width):
    return [
        pltpu.VMEM((4, rows, width), BF16),
        pltpu.VMEM((2, rows, width), F32),
        pltpu.VMEM((rows, width), BF16),
        pltpu.VMEM((rows, width), BF16),
        pltpu.VMEM((rows, width), BF16),
        pltpu.VMEM((rows, width), BF16),
        pltpu.VMEM((rows, width), BF16),
        pltpu.VMEM((rows, width), BF16),
    ]


COMM_SCRATCH = (
    stream_scratch(RT, DT)
    + stream_scratch(RP, DV)
    + [pltpu.SemaphoreType.DMA((12,)), pltpu.SemaphoreType.DMA((12,))]
)


def make_streams(at, refs):
    sends, recvs = refs[16], refs[17]
    text = Stream(at, *refs[0:8], sends, recvs, 0)
    image = Stream(at, *refs[8:16], sends, recvs, 6)
    return text, image


def norm_out(pre, gain, bias, out_ref, xh_ref, rs_ref):
    mean = jnp.mean(pre, axis=-1, keepdims=True)
    centered = pre - mean
    variance = jnp.mean(centered * centered, axis=-1, keepdims=True)
    rs = lax.rsqrt(variance + epsilon)
    xh = centered * rs
    xh_ref[...] = xh
    rs_ref[...] = jnp.broadcast_to(rs, rs_ref.shape)
    out_ref[...] = (xh * gain + bias).astype(out_ref.dtype)


def norm_in(grad, xh, rs, gain, gb_ref):
    dz = grad * gain
    gb_ref[0:1, :] = jnp.sum(grad * xh, axis=0, keepdims=True)
    gb_ref[1:2, :] = jnp.sum(grad, axis=0, keepdims=True)
    m1 = jnp.mean(dz, axis=-1, keepdims=True)
    m2 = jnp.mean(dz * xh, axis=-1, keepdims=True)
    return (dz - m1 - xh * m2) * rs[:, 0:1]


def loads(pairs, sems):
    copies = [pltpu.make_async_copy(s, d, sems.at[i]) for i, (s, d) in enumerate(pairs)]
    for copy in copies:
        copy.start()
    return copies


def gelu_parts(u):
    phi = 0.5 * (1.0 + lax.erf(u * (1.0 / math.sqrt(2.0))))
    density = jnp.exp(u * u * -0.5) * (1.0 / math.sqrt(2.0 * math.pi))
    return u * phi, phi + u * density


def softmax(scores):
    top = jnp.max(scores, axis=-1, keepdims=True)
    e = jnp.exp(scores - top)
    return e / jnp.sum(e, axis=-1, keepdims=True)


def iota2(shape, dim):
    return lax.broadcasted_iota(jnp.int32, shape, dim)


def joint_mask(q_rows, q_split, k_rows, k_split, count0, count1):
    q, k = iota2((q_rows, k_rows), 0), iota2((q_rows, k_rows), 1)
    first = (q < q_split) & (k < count0)
    second = (q >= q_split) & (k >= k_split) & (k < k_split + count1)
    return first | second


def key_mask(rows, count):
    return iota2((rows, rows), 1) < count


def head_masks(rows, width, size):
    lane = iota2((rows, width), 1)
    return [(lane >= h * size) & (lane < (h + 1) * size) for h in range(width // size)]


def pick(mask, x):
    return jnp.where(mask, x, jnp.zeros_like(x))


def attn_fwd(q, k, v, mask, heads, size):
    out = []
    for h in range(heads):
        s = slice(h * size, (h + 1) * size)
        scores = mm_nt(q[:, s], k[:, s]) * (1.0 / math.sqrt(size))
        p = softmax(jnp.where(mask, scores, masked_score))
        out.append(mm(p.astype(BF16), v[:, s]).astype(BF16))
    return jnp.concatenate(out, axis=1)


def attn_bwd(q, k, v, dm, mask, heads, size):
    dq, dk, dv = [], [], []
    for h in range(heads):
        s = slice(h * size, (h + 1) * size)
        scale = 1.0 / math.sqrt(size)
        scores = mm_nt(q[:, s], k[:, s]) * scale
        p = softmax(jnp.where(mask, scores, masked_score))
        dp = mm_nt(dm[:, s], v[:, s])
        dv.append(mm_tn(p.astype(BF16), dm[:, s]).astype(BF16))
        ds = p * (dp - jnp.sum(dp * p, axis=-1, keepdims=True))
        dr = (ds * scale).astype(BF16)
        dq.append(mm(dr, k[:, s]).astype(BF16))
        dk.append(mm_tn(dr, q[:, s]).astype(BF16))
    return tuple(jnp.concatenate(x, axis=1) for x in (dq, dk, dv))


def attn_fwd_small(q, k, v, mask, hm):
    total = None
    for m in hm:
        scores = mm_nt(pick(m, q), k) * (1.0 / math.sqrt(KT))
        p = softmax(jnp.where(mask, scores, masked_score))
        part = mm(p.astype(BF16), pick(m, v))
        total = part if total is None else total + part
    return total.astype(BF16)


def attn_bwd_small(q, k, v, dm, mask, hm):
    dq = dk = dv = None
    scale = 1.0 / math.sqrt(KT)
    for m in hm:
        scores = mm_nt(pick(m, q), k) * scale
        p = softmax(jnp.where(mask, scores, masked_score))
        dmh = pick(m, dm)
        dp = mm_nt(dmh, v)
        dvp = mm_tn(p.astype(BF16), dmh)
        ds = p * (dp - jnp.sum(dp * p, axis=-1, keepdims=True))
        dr = (ds * scale).astype(BF16)
        dqp = mm(dr, pick(m, k))
        dkp = mm_tn(dr, pick(m, q))
        dq, dk, dv = (dqp, dkp, dvp) if dq is None else (dq + dqp, dk + dkp, dv + dvp)
    return dq.astype(BF16), dk.astype(BF16), dv.astype(BF16)


def ff_fwd_kernel(row, xt, xi, wti, wto, wii, wio, tg, tb, ig, ib,
                  ot, oi, xht, xhi, rst, rsi, gt, gi, at_, pt_, ai_, pi_,
                  vti, vto, vii, vio, sat, spt, sai, spi, lsem, osem, *comm):
    at = Places()
    weights = loads([(wti, vti), (wii, vii), (wto, vto), (wio, vio)], lsem)
    at.greet()
    text, image = make_streams(at, comm)
    image.begin(xi[...].astype(BF16))
    text.begin(xt[...].astype(BF16))
    for w in weights:
        w.wait()
    saves = []
    for phase in range(4):
        b = at.block(phase)
        image.ready(phase)
        act, slope = gelu_parts(mm(image.slots[b], vii[...]))
        sai[b] = act.astype(BF16)
        spi[b] = slope.astype(BF16)
        image.partial(phase, mm(sai[b], vio[...]))
        text.ready(phase)
        act, slope = gelu_parts(mm(text.slots[b], vti[...]))
        sat[b] = act.astype(BF16)
        spt[b] = slope.astype(BF16)
        text.partial(phase, mm(sat[b], vto[...]))
    image.forward()
    text.forward()
    saves = loads([(text.slots, gt), (image.slots, gi), (sat, at_), (spt, pt_), (sai, ai_), (spi, pi_)], osem)
    norm_out(xi[...] + image.total(), ig[row : row + 1, :], ib[row : row + 1, :], oi, xhi, rsi)
    norm_out(xt[...] + text.total(), tg[row : row + 1, :], tb[row : row + 1, :], ot, xht, rst)
    for c in saves:
        c.wait()
    text.end()
    image.end()


def ff_bwd_kernel(row, dt, di, xht, xhi, rst, rsi, tg, ig, gt, gi, at_, pt_, ai_, pi_, wti, wto, wii, wio,
                  ot, oi, gbt, gbi, wgt, wgi,
                  vgt, vgi, vat, vpt, vai, vpi, vti, vto, vii, vio, dut, dui, keep_t, keep_i, lsem, *comm):
    at = Places()
    ins = loads([(wto, vto), (pt_, vpt), (wti, vti), (wio, vio), (pi_, vpi), (wii, vii),
                 (gt, vgt), (gi, vgi), (at_, vat), (ai_, vai)], lsem)
    at.greet()
    text, image = make_streams(at, comm)
    keep_i[...] = norm_in(di[...], xhi[...], rsi[...], ig[row : row + 1, :], gbi)
    image.begin(keep_i[...].astype(BF16))
    keep_t[...] = norm_in(dt[...], xht[...], rst[...], tg[row : row + 1, :], gbt)
    text.begin(keep_t[...].astype(BF16))
    for c in ins:
        c.wait()
    for phase in range(4):
        b = at.block(phase)
        image.ready(phase)
        dui[b] = (mm_nt(image.slots[b], vio[...]) * vpi[b].astype(F32)).astype(BF16)
        image.partial(phase, mm_nt(dui[b], vii[...]))
        text.ready(phase)
        dut[b] = (mm_nt(text.slots[b], vto[...]) * vpt[b].astype(F32)).astype(BF16)
        text.partial(phase, mm_nt(dut[b], vti[...]))
    image.forward()
    text.forward()
    ft, fi = vti.shape[1], vii.shape[1]
    wgt[:, 0:ft] = mm_tn(vgt[...].reshape(4 * RT, DT), dut[...].reshape(4 * RT, ft)).astype(BF16)
    wgt[:, ft:] = mm_tn(text.slots[...].reshape(4 * RT, DT), vat[...].reshape(4 * RT, ft)).astype(BF16)
    wgi[:, 0:fi] = mm_tn(vgi[...].reshape(4 * RP, DV), dui[...].reshape(4 * RP, fi)).astype(BF16)
    wgi[:, fi:] = mm_tn(image.slots[...].reshape(4 * RP, DV), vai[...].reshape(4 * RP, fi)).astype(BF16)
    oi[...] = (keep_i[...] + image.total()).astype(oi.dtype)
    ot[...] = (keep_t[...] + text.total()).astype(ot.dtype)
    text.end()
    image.end()


def sds(shape, dtype=F32):
    return jax.ShapeDtypeStruct(shape, dtype)


def call(kernel, out_shape, n_vmem_in, in_specs, out_specs, scratch, cid, name, flops, args):
    return pl.pallas_call(
        kernel,
        out_shape=out_shape,
        in_specs=in_specs,
        out_specs=out_specs,
        scratch_shapes=scratch + COMM_SCRATCH,
        compiler_params=pltpu.CompilerParams(
            collective_id=cid, has_side_effects=True, vmem_limit_bytes=60 << 20
        ),
        cost_estimate=pl.CostEstimate(flops=flops, bytes_accessed=20 << 20, transcendentals=0),
        name=name,
    )(*args)


NORM_OUT = lambda dt: (
    [sds((RT, DT), dt), sds((RP, DV), dt), sds((RT, DT)), sds((RP, DV)), sds((RT, 128)), sds((RP, 128))]
)


def ff_fwd(row, xt, xi, wti, wto, wii, wio, norms, out_type):
    ft, fi = wti.shape[1], wii.shape[1]
    outs = NORM_OUT(out_type) + [
        sds((4, RT, DT), BF16), sds((4, RP, DV), BF16),
        sds((4, RT, ft), BF16), sds((4, RT, ft), BF16),
        sds((4, RP, fi), BF16), sds((4, RP, fi), BF16),
    ]
    scratch = [
        pltpu.VMEM(wti.shape, BF16), pltpu.VMEM(wto.shape, BF16),
        pltpu.VMEM(wii.shape, BF16), pltpu.VMEM(wio.shape, BF16),
        pltpu.VMEM((4, RT, ft), BF16), pltpu.VMEM((4, RT, ft), BF16),
        pltpu.VMEM((4, RP, fi), BF16), pltpu.VMEM((4, RP, fi), BF16),
        pltpu.SemaphoreType.DMA((4,)), pltpu.SemaphoreType.DMA((6,)),
    ]
    return call(functools.partial(ff_fwd_kernel, row), outs, 0,
                [VM] * 2 + [ANY] * 4 + [VM] * 4, [VM] * 6 + [ANY] * 6, scratch,
                1 + row, "ff_fwd%d" % row, 10**9, (xt, xi, wti, wto, wii, wio, *norms))


def ff_bwd(row, dt, di, saved, wti, wto, wii, wio, norms):
    ft, fi = wti.shape[1], wii.shape[1]
    xht, xhi, rst, rsi, gt, gi, at_, pt_, ai_, pi_ = saved
    outs = [
        sds((RT, DT)), sds((RP, DV)), sds((2, DT)), sds((2, DV)),
        sds((DT, 2 * ft), BF16), sds((DV, 2 * fi), BF16),
    ]
    scratch = [
        pltpu.VMEM((4, RT, DT), BF16), pltpu.VMEM((4, RP, DV), BF16),
        pltpu.VMEM((4, RT, ft), BF16), pltpu.VMEM((4, RT, ft), BF16),
        pltpu.VMEM((4, RP, fi), BF16), pltpu.VMEM((4, RP, fi), BF16),
        pltpu.VMEM(wti.shape, BF16), pltpu.VMEM(wto.shape, BF16),
        pltpu.VMEM(wii.shape, BF16), pltpu.VMEM(wio.shape, BF16),
        pltpu.VMEM((4, RT, ft), BF16), pltpu.VMEM((4, RP, fi), BF16),
        pltpu.VMEM((RT, DT), F32), pltpu.VMEM((RP, DV), F32),
        pltpu.SemaphoreType.DMA((10,)),
    ]
    tg, tb, ig, ib = norms
    return call(functools.partial(ff_bwd_kernel, row), outs, 0,
                [VM] * 8 + [ANY] * 10, [VM] * 6, scratch,
                11 + row, "ff_bwd%d" % row, 10**9,
                (dt, di, xht, xhi, rst, rsi, tg, ig, gt, gi, at_, pt_, ai_, pi_, wti, wto, wii, wio))


def co_masks(b, tl, rc):
    text_q = joint_mask(RT, LT, RP, RG, rc[2 * b], rc[2 * b + 1])
    image_q = joint_mask(RP, RG, RT, LT, tl[2 * b], tl[2 * b + 1])
    return text_q, image_q


def co_fwd_kernel(tl, rc, xt, xi, wqt, wkvi, wot, wqi, wkvt, woi, tg, tb, ig, ib,
                  ot, oi, xht, xhi, rst, rsi, gt, gi, pt_, pi_, mt_, mi_,
                  vqt, vkvi, vot, vqi, vkvt, voi, spt, spi, smt, smi, lsem, osem, *comm):
    at = Places()
    weights = loads([(wqt, vqt), (wkvi, vkvi), (wkvt, vkvt), (wqi, vqi), (wot, vot), (woi, voi)], lsem)
    at.greet()
    text, image = make_streams(at, comm)
    image.begin(xi[...])
    text.begin(xt[...])
    for w in weights:
        w.wait()
    n = vqt.shape[1]
    heads = n // KC
    for phase in range(4):
        b = at.block(phase)
        text_mask, image_mask = co_masks(b, tl, rc)
        image.ready(phase)
        x = image.slots[b]
        spi[b, :, 0:n] = mm(x, vqi[...]).astype(BF16)
        spi[b, :, n : 2 * n] = mm(x, vkvi[0]).astype(BF16)
        spi[b, :, 2 * n :] = mm(x, vkvi[1]).astype(BF16)
        text.ready(phase)
        x = text.slots[b]
        spt[b, :, 0:n] = mm(x, vqt[...]).astype(BF16)
        spt[b, :, n : 2 * n] = mm(x, vkvt[0]).astype(BF16)
        spt[b, :, 2 * n :] = mm(x, vkvt[1]).astype(BF16)
        smt[b] = attn_fwd(spt[b, :, 0:n], spi[b, :, n : 2 * n], spi[b, :, 2 * n :], text_mask, heads, KC)
        text.partial(phase, mm(smt[b], vot[...]))
        smi[b] = attn_fwd(spi[b, :, 0:n], spt[b, :, n : 2 * n], spt[b, :, 2 * n :], image_mask, heads, KC)
        image.partial(phase, mm(smi[b], voi[...]))
    text.forward()
    image.forward()
    saves = loads([(text.slots, gt), (image.slots, gi), (spt, pt_), (spi, pi_), (smt, mt_), (smi, mi_)], osem)
    norm_out(xt[...].astype(F32) + text.total(), tg[0:1, :], tb[0:1, :], ot, xht, rst)
    norm_out(xi[...].astype(F32) + image.total(), ig[0:1, :], ib[0:1, :], oi, xhi, rsi)
    for c in saves:
        c.wait()
    text.end()
    image.end()


def co_bwd_kernel(tl, rc, dt, di, xht, xhi, rst, rsi, tg, ig, gt, gi, pt_, pi_, mt_, mi_,
                  wqt, wkvi, wot, wqi, wkvt, woi,
                  ot, oi, gbt, gbi, wgt, wgi,
                  vgt, vgi, spt, spi, smt, smi, vqt, vkvi, vot, vqi, vkvt, voi,
                  dpt, dpi, keep_t, keep_i, lsem, *comm):
    at = Places()
    ins = loads([(wot, vot), (woi, voi), (pt_, spt), (pi_, spi), (wqt, vqt), (wkvi, vkvi), (wkvt, vkvt),
                 (wqi, vqi), (gt, vgt), (gi, vgi), (mt_, smt), (mi_, smi)], lsem)
    at.greet()
    text, image = make_streams(at, comm)
    keep_i[...] = norm_in(di[...], xhi[...], rsi[...], ig[0:1, :], gbi)
    image.begin(keep_i[...].astype(BF16))
    keep_t[...] = norm_in(dt[...], xht[...], rst[...], tg[0:1, :], gbt)
    text.begin(keep_t[...].astype(BF16))
    for c in ins:
        c.wait()
    n = vqt.shape[1]
    heads = n // KC
    for phase in range(4):
        b = at.block(phase)
        text_mask, image_mask = co_masks(b, tl, rc)
        image.ready(phase)
        dm = mm_nt(image.slots[b], voi[...]).astype(BF16)
        dq, dk, dv = attn_bwd(spi[b, :, 0:n], spt[b, :, n : 2 * n], spt[b, :, 2 * n :], dm, image_mask, heads, KC)
        dpi[b, :, 0:n] = dq
        dpt[b, :, n : 2 * n] = dk
        dpt[b, :, 2 * n :] = dv
        text.ready(phase)
        dm = mm_nt(text.slots[b], vot[...]).astype(BF16)
        dq, dk, dv = attn_bwd(spt[b, :, 0:n], spi[b, :, n : 2 * n], spi[b, :, 2 * n :], dm, text_mask, heads, KC)
        dpt[b, :, 0:n] = dq
        dpi[b, :, n : 2 * n] = dk
        dpi[b, :, 2 * n :] = dv
        image.partial(phase, mm_nt(dpi[b, :, 0:n], vqi[...]) + mm_nt(dpi[b, :, n : 2 * n], vkvi[0])
                      + mm_nt(dpi[b, :, 2 * n :], vkvi[1]))
        text.partial(phase, mm_nt(dpt[b, :, 0:n], vqt[...]) + mm_nt(dpt[b, :, n : 2 * n], vkvt[0])
                     + mm_nt(dpt[b, :, 2 * n :], vkvt[1]))
    image.forward()
    text.forward()
    wgt[:, 0 : 3 * n] = mm_tn(vgt[...].reshape(4 * RT, DT), dpt[...].reshape(4 * RT, 3 * n)).astype(BF16)
    wgt[:, 3 * n :] = mm_tn(text.slots[...].reshape(4 * RT, DT), smt[...].reshape(4 * RT, n)).astype(BF16)
    wgi[:, 0 : 3 * n] = mm_tn(vgi[...].reshape(4 * RP, DV), dpi[...].reshape(4 * RP, 3 * n)).astype(BF16)
    wgi[:, 3 * n :] = mm_tn(image.slots[...].reshape(4 * RP, DV), smi[...].reshape(4 * RP, n)).astype(BF16)
    oi[...] = (keep_i[...] + image.total()).astype(oi.dtype)
    ot[...] = (keep_t[...] + text.total()).astype(ot.dtype)
    text.end()
    image.end()


def self_fwd_kernel(tl, rc, xt, xi, wt, wot, wi, woi, tg, tb, ig, ib,
                    ot, oi, xht, xhi, rst, rsi, gt, gi, pt_, pi_, mt_, mi_,
                    vt, vot, vi, voi, spt, spi, smt, smi, lsem, osem, *comm):
    at = Places()
    weights = loads([(wt, vt), (wot, vot), (wi, vi), (woi, voi)], lsem)
    at.greet()
    text, image = make_streams(at, comm)
    image.begin(xi[...].astype(BF16))
    text.begin(xt[...].astype(BF16))
    for w in weights:
        w.wait()
    n = vi.shape[2]
    heads = n // KV
    hm = head_masks(LT, vt.shape[2], KT)
    for phase in range(4):
        b = at.block(phase)
        image.ready(phase)
        x = image.slots[b]
        for i in range(3):
            spi[b, :, i * n : (i + 1) * n] = mm(x, vi[i]).astype(BF16)
        mask = joint_mask(RP, RG, RP, RG, rc[2 * b], rc[2 * b + 1])
        smi[b] = attn_fwd(spi[b, :, 0:n], spi[b, :, n : 2 * n], spi[b, :, 2 * n :], mask, heads, KV)
        image.partial(phase, mm(smi[b], voi[...]))
        text.ready(phase)
        x = text.slots[b]
        for i in range(3):
            spt[i, b] = mm(x, vt[i]).astype(BF16)
        for p in range(RT // LT):
            r = slice(p * LT, (p + 1) * LT)
            smt[b, r, :] = attn_fwd_small(spt[0, b, r, :], spt[1, b, r, :], spt[2, b, r, :],
                                          key_mask(LT, tl[2 * b + p]), hm)
        text.partial(phase, mm(smt[b], vot[...]))
    image.forward()
    text.forward()
    saves = loads([(text.slots, gt), (image.slots, gi), (spt, pt_), (spi, pi_), (smt, mt_), (smi, mi_)], osem)
    norm_out(xi[...] + image.total(), ig[2:3, :], ib[2:3, :], oi, xhi, rsi)
    norm_out(xt[...] + text.total(), tg[2:3, :], tb[2:3, :], ot, xht, rst)
    for c in saves:
        c.wait()
    text.end()
    image.end()


def self_bwd_kernel(tl, rc, dt, di, xht, xhi, rst, rsi, tg, ig, gt, gi, pt_, pi_, mt_, mi_, wt, wot, wi, woi,
                    ot, oi, gbt, gbi, wgt, wgi,
                    vgt, vgi, spt, spi, smt, smi, vt, vot, vi, voi, dpt, dpi, keep_t, keep_i, lsem, *comm):
    at = Places()
    ins = loads([(woi, voi), (wot, vot), (pi_, spi), (pt_, spt), (wi, vi), (wt, vt),
                 (gt, vgt), (gi, vgi), (mt_, smt), (mi_, smi)], lsem)
    at.greet()
    text, image = make_streams(at, comm)
    keep_i[...] = norm_in(di[...], xhi[...], rsi[...], ig[2:3, :], gbi)
    image.begin(keep_i[...].astype(BF16))
    keep_t[...] = norm_in(dt[...], xht[...], rst[...], tg[2:3, :], gbt)
    text.begin(keep_t[...].astype(BF16))
    for c in ins:
        c.wait()
    n = vi.shape[2]
    heads = n // KV
    m = vt.shape[2]
    hm = head_masks(LT, m, KT)
    for phase in range(4):
        b = at.block(phase)
        image.ready(phase)
        dm = mm_nt(image.slots[b], voi[...]).astype(BF16)
        mask = joint_mask(RP, RG, RP, RG, rc[2 * b], rc[2 * b + 1])
        dq, dk, dv = attn_bwd(spi[b, :, 0:n], spi[b, :, n : 2 * n], spi[b, :, 2 * n :], dm, mask, heads, KV)
        dpi[b, :, 0:n] = dq
        dpi[b, :, n : 2 * n] = dk
        dpi[b, :, 2 * n :] = dv
        image.partial(phase, mm_nt(dpi[b, :, 0:n], vi[0]) + mm_nt(dpi[b, :, n : 2 * n], vi[1])
                      + mm_nt(dpi[b, :, 2 * n :], vi[2]))
        text.ready(phase)
        dmt = mm_nt(text.slots[b], vot[...]).astype(BF16)
        for p in range(RT // LT):
            r = slice(p * LT, (p + 1) * LT)
            dq, dk, dv = attn_bwd_small(spt[0, b, r, :], spt[1, b, r, :], spt[2, b, r, :], dmt[r, :],
                                        key_mask(LT, tl[2 * b + p]), hm)
            dpt[0, b, r, :] = dq
            dpt[1, b, r, :] = dk
            dpt[2, b, r, :] = dv
        text.partial(phase, mm_nt(dpt[0, b], vt[0]) + mm_nt(dpt[1, b], vt[1]) + mm_nt(dpt[2, b], vt[2]))
    image.forward()
    text.forward()
    for i in range(3):
        wgt[:, i * m : (i + 1) * m] = mm_tn(vgt[...].reshape(4 * RT, DT), dpt[i].reshape(4 * RT, m)).astype(BF16)
    wgt[:, 3 * m :] = mm_tn(text.slots[...].reshape(4 * RT, DT), smt[...].reshape(4 * RT, m)).astype(BF16)
    wgi[:, 0 : 3 * n] = mm_tn(vgi[...].reshape(4 * RP, DV), dpi[...].reshape(4 * RP, 3 * n)).astype(BF16)
    wgi[:, 3 * n :] = mm_tn(image.slots[...].reshape(4 * RP, DV), smi[...].reshape(4 * RP, n)).astype(BF16)
    oi[...] = (keep_i[...] + image.total()).astype(oi.dtype)
    ot[...] = (keep_t[...] + text.total()).astype(ot.dtype)
    text.end()
    image.end()


def attn_scratch(weights, saved):
    return [pltpu.VMEM(w.shape, BF16) for w in weights] + [pltpu.VMEM(s, BF16) for s in saved]


def attn_fwd_call(kernel, cid, name, tl, rc, xt, xi, weights, norms, saved):
    outs = NORM_OUT(F32) + [sds((4, RT, DT), BF16), sds((4, RP, DV), BF16)] + [sds(s, BF16) for s in saved]
    scratch = attn_scratch(weights, saved) + [
        pltpu.SemaphoreType.DMA((len(weights),)), pltpu.SemaphoreType.DMA((6,))]
    return call(kernel, outs, 0, [SM] * 2 + [VM] * 2 + [ANY] * len(weights) + [VM] * 4,
                [VM] * 6 + [ANY] * 6, scratch, cid, name, 10**9, (tl, rc, xt, xi, *weights, *norms))


def attn_bwd_call(kernel, cid, name, tl, rc, dt, di, saved, weights, norms, out_type, wide):
    xht, xhi, rst, rsi, gt, gi, pt_, pi_, mt_, mi_ = saved
    outs = [
        sds((RT, DT), out_type), sds((RP, DV), out_type), sds((2, DT)), sds((2, DV)),
        sds((DT, wide[0]), BF16), sds((DV, wide[1]), BF16),
    ]
    keep = [x.shape for x in (gt, gi, pt_, pi_, mt_, mi_)]
    scratch = (
        [pltpu.VMEM(s, BF16) for s in keep]
        + [pltpu.VMEM(w.shape, BF16) for w in weights]
        + [pltpu.VMEM(pt_.shape, BF16), pltpu.VMEM(pi_.shape, BF16),
           pltpu.VMEM((RT, DT), F32), pltpu.VMEM((RP, DV), F32),
           pltpu.SemaphoreType.DMA((len(weights) + 6,))]
    )
    tg, tb, ig, ib = norms
    return call(kernel, outs, 0, [SM] * 2 + [VM] * 8 + [ANY] * (6 + len(weights)), [VM] * 6, scratch,
                cid, name, 10**9,
                (tl, rc, dt, di, xht, xhi, rst, rsi, tg, ig, gt, gi, pt_, pi_, mt_, mi_, *weights))


def pad_rows(x):
    return jnp.pad(x, ((0, RP - RI), (0, 0)))


def local(
    dp,
    text_in, image_in, text_len, region_count,
    co_query_text, co_kv_image, co_out_text, co_query_image, co_kv_text, co_out_image,
    co_ff_text_in, co_ff_text_out, co_ff_image_in, co_ff_image_out,
    self_qkv_text, self_out_text, self_ff_text_in, self_ff_text_out,
    self_qkv_image, self_out_image, self_ff_image_in, self_ff_image_out,
    text_gains, text_biases, image_gains, image_biases,
    text_cot, image_cot,
):
    norms = (text_gains, text_biases, image_gains, image_biases)
    co_w = (co_query_text, co_kv_image, co_out_text, co_query_image, co_kv_text, co_out_image)
    cf_w = (co_ff_text_in, co_ff_text_out, co_ff_image_in, co_ff_image_out)
    sa_w = (self_qkv_text, self_out_text, self_qkv_image, self_out_image)
    sf_w = (self_ff_text_in, self_ff_text_out, self_ff_image_in, self_ff_image_out)
    n, m = co_query_text.shape[1], self_qkv_text.shape[2]
    tl, rc = text_len, region_count
    co = attn_fwd_call(co_fwd_kernel, 1, "co_fwd", tl, rc, text_in, pad_rows(image_in), co_w, norms,
                       [(4, RT, 3 * n), (4, RP, 3 * n), (4, RT, n), (4, RP, n)])
    cf = ff_fwd(1, co[0], co[1], *cf_w, norms, F32)
    sa = attn_fwd_call(self_fwd_kernel, 3, "self_fwd", tl, rc, cf[0], cf[1], sa_w, norms,
                       [(3, 4, RT, m), (4, RP, 3 * n), (4, RT, m), (4, RP, n)])
    sf = ff_fwd(3, sa[0], sa[1], *sf_w, norms, BF16)
    bsf = ff_bwd(3, text_cot.astype(F32), pad_rows(image_cot).astype(F32), sf[2:], *sf_w, norms)
    bsa = attn_bwd_call(self_bwd_kernel, 13, "self_bwd", tl, rc, bsf[0], bsf[1], sa[2:], sa_w, norms,
                        F32, (4 * m, 4 * n))
    bcf = ff_bwd(1, bsa[0], bsa[1], cf[2:], *cf_w, norms)
    bco = attn_bwd_call(co_bwd_kernel, 11, "co_bwd", tl, rc, bcf[0], bcf[1], co[2:], co_w, norms,
                        BF16, (4 * n, 4 * n))
    layers = (bco, bcf, bsa, bsf)
    tgb = jnp.stack([x[2] for x in layers])
    igb = jnp.stack([x[3] for x in layers])
    tgb, igb = lax.psum((tgb, igb), ("dp", "tensor"))
    flat = jnp.concatenate(
        [x[4].reshape(dp, -1) for x in layers] + [x[5].reshape(dp, -1) for x in layers], axis=1)
    flat = lax.psum_scatter(flat.reshape(-1, 128), "dp", scatter_dimension=0, tiled=True)
    flat = flat.astype(F32).reshape(-1)
    parts, at = [], 0
    for x in [y[4] for y in layers] + [y[5] for y in layers]:
        size = x.size // dp
        parts.append(flat[at : at + size].reshape(x.shape[0] // dp, x.shape[1]))
        at += size
    ct, ft, st, gt_, ci, fi, si, gi_ = parts
    f = co_ff_text_in.shape[1]
    return (
        sf[0], sf[1][:RI], bco[0], bco[1][:RI],
        ct[:, :n],
        jnp.stack([ci[:, n : 2 * n], ci[:, 2 * n : 3 * n]]),
        ct[:, 3 * n :].T,
        ci[:, :n],
        jnp.stack([ct[:, n : 2 * n], ct[:, 2 * n : 3 * n]]),
        ci[:, 3 * n :].T,
        ft[:, :f], ft[:, f:].T, fi[:, :n], fi[:, n:].T,
        jnp.stack([st[:, i * m : (i + 1) * m] for i in range(3)]),
        st[:, 3 * m :].T,
        gt_[:, :f], gt_[:, f:].T,
        jnp.stack([si[:, i * n : (i + 1) * n] for i in range(3)]),
        si[:, 3 * n :].T,
        gi_[:, :n], gi_[:, n:].T,
        tgb[:, 0], tgb[:, 1], igb[:, 0], igb[:, 1],
    )


def solution(mesh):
    rows, pairs = P(("dp", "tensor"), None), P("dp")
    wide, tall, stack = P(None, "tensor"), P("tensor", None), P(None, None, "tensor")
    g_wide, g_tall, g_stack = P("dp", "tensor"), P("tensor", "dp"), P(None, "dp", "tensor")
    return jax.shard_map(
        functools.partial(local, mesh.shape["dp"]),
        mesh=mesh,
        in_specs=(
            rows, rows, pairs, pairs,
            wide, stack, tall, wide, stack, tall,
            wide, tall, wide, tall,
            stack, tall, wide, tall,
            stack, tall, wide, tall,
            P(), P(), P(), P(),
            rows, rows,
        ),
        out_specs=(
            rows, rows, rows, rows,
            g_wide, g_stack, g_tall, g_wide, g_stack, g_tall,
            g_wide, g_tall, g_wide, g_tall,
            g_stack, g_tall, g_wide, g_tall,
            g_stack, g_tall, g_wide, g_tall,
            P(), P(), P(), P(),
        ),
        check_vma=False,
    )
```

```python
import functools
import math

import jax
import jax.numpy as jnp
from jax import lax
from jax.experimental import pallas as pl
from jax.experimental.pallas import tpu as pltpu
from jax.sharding import PartitionSpec as P

KT = 64
KV = 128
KC = 128
LT = 128
RG = 36
RP = 48
DT = 768
DV = 1024

epsilon = 1e-05
masked_score = -1e30
F32 = jnp.float32
BF16 = jnp.bfloat16
MESH = pl.DeviceIdType.MESH
VM = pl.BlockSpec(memory_space=pltpu.VMEM)
SM = pl.BlockSpec(memory_space=pltpu.SMEM)
ANY = pl.BlockSpec(memory_space=pl.ANY)


def mm(a, b):
    return lax.dot_general(a, b, (((1,), (0,)), ((), ())), preferred_element_type=F32)


def mm_nt(a, b):
    return lax.dot_general(a, b, (((1,), (1,)), ((), ())), preferred_element_type=F32)


def mm_tn(a, b):
    return lax.dot_general(a, b, (((0,), (0,)), ((), ())), preferred_element_type=F32)


class Places:
    def __init__(self):
        me = lax.axis_index("tensor")
        chip, core = lax.div(me, 2), lax.rem(me, 2)
        self.me, self.chip, self.core = me, chip, core
        self.core_mate = 2 * chip + (1 - core)
        self.chip_mate = 2 * (1 - chip) + core

    def base(self, half):
        return 2 * (self.chip + half - 2 * self.chip * half)


class Stream:
    def __init__(self, at, stream, part, near, relay, out, got_near, got_far, got_chip, sends, recvs):
        self.at, self.stream, self.part = at, stream, part
        self.near, self.relay, self.out = near, relay, out
        self.got_near, self.got_far, self.got_chip = got_near, got_far, got_chip
        self.sends, self.recvs = sends, recvs

    def push(self, src, dst, m, slot, mate):
        return pltpu.make_async_remote_copy(
            src_ref=src,
            dst_ref=dst,
            send_sem=self.sends.at[self.stream, m, slot],
            recv_sem=self.recvs.at[self.stream, m, slot],
            device_id={"tensor": mate},
            device_id_type=MESH,
        )

    def copy(self, slots, m, which):
        at = self.at
        me, cm, xm = at.me, at.core_mate, at.chip_mate
        if which == 0:
            return self.push(slots.at[m, me], slots.at[m, me], m, 0, cm)
        if which == 1:
            return self.push(slots.at[m, me], slots.at[m, me], m, 1, xm)
        if which == 2:
            return self.push(slots.at[m, xm], slots.at[m, xm], m, 2, cm)
        if which == 3:
            return self.push(self.near.at[m], self.got_near.at[m], m, 3, cm)
        if which == 4:
            return self.push(self.relay.at[m], self.got_far.at[m], m, 4, cm)
        return self.push(self.out.at[m], self.got_chip.at[m], m, 5, xm)

    def begin(self, slots, m, rows):
        slots[m, self.at.me] = rows
        self.copy(slots, m, 1).start()
        self.copy(slots, m, 0).start()

    def relay_gather(self, slots, m):
        self.copy(slots, m, 1).wait_recv()
        self.copy(slots, m, 2).start()

    def partial(self, half, m, value):
        part, other = self.part, 1 - self.at.core
        part[m, half] = value.reshape(part.shape[2:])

        @pl.when(half == 0)
        def _():
            self.near[m] = part[m, 0, other].astype(BF16)
            self.copy(None, m, 3).start()

        @pl.when(half == 1)
        def _():
            self.relay[m] = part[m, 1, other].astype(BF16)
            self.copy(None, m, 4).start()

    def forward(self, m):
        self.copy(None, m, 4).wait_recv()
        self.out[m] = (self.part[m, 1, self.at.core] + self.got_far[m].astype(F32)).astype(BF16)
        self.copy(None, m, 5).start()

    def total(self, m):
        self.copy(None, m, 3).wait_recv()
        self.copy(None, m, 5).wait_recv()
        return self.part[m, 0, self.at.core] + self.got_near[m].astype(F32) + self.got_chip[m].astype(F32)

    def end(self, slots, m):
        for which in range(6):
            self.copy(slots, m, which).wait_send()


def stream_scratch(rows, width):
    return [pltpu.VMEM((2, 2, 2, rows, width), F32)] + [pltpu.VMEM((2, rows, width), BF16)] * 6


COMM = stream_scratch(LT, DT) + stream_scratch(RP, DV) + [pltpu.SemaphoreType.DMA((2, 2, 6))] * 2


def make_streams(at, refs):
    text = Stream(at, 0, *refs[0:7], refs[14], refs[15])
    image = Stream(at, 1, *refs[7:14], refs[14], refs[15])
    return text, image


def greet(at):
    barrier = pltpu.get_barrier_semaphore()
    for mate in (at.core_mate, at.chip_mate):
        pl.semaphore_signal(barrier, inc=1, device_id={"tensor": mate}, device_id_type=MESH)
    pl.semaphore_wait(barrier, 2)


def steps(text, image, tslots, islots, compute):
    @pl.loop(0, 4)
    def _(i):
        half, m = lax.div(i, 2), lax.rem(i, 2)

        @pl.when(half == 0)
        def _():
            image.copy(islots, m, 0).wait_recv()
            text.copy(tslots, m, 0).wait_recv()

        @pl.when(half == 1)
        def _():
            image.relay_gather(islots, m)
            text.relay_gather(tslots, m)
            image.copy(islots, m, 2).wait_recv()
            text.copy(tslots, m, 2).wait_recv()

        compute(half, m, pl.ds(text.at.base(half), 2))

        @pl.when(half == 1)
        def _():
            image.forward(m)
            text.forward(m)


def norm(pre, gain, bias, xh_ref, rs_ref, m):
    mean = jnp.mean(pre, axis=-1, keepdims=True)
    centered = pre - mean
    variance = jnp.mean(centered * centered, axis=-1, keepdims=True)
    rs = lax.rsqrt(variance + epsilon)
    xh = centered * rs
    xh_ref[m] = xh
    rs_ref[m] = jnp.broadcast_to(rs, rs_ref.shape[1:])
    return xh * gain + bias


def norm_back(grad, xh, rs, gain):
    dz = grad * gain
    dg = jnp.sum(grad * xh, axis=0, keepdims=True)
    db = jnp.sum(grad, axis=0, keepdims=True)
    m1 = jnp.mean(dz, axis=-1, keepdims=True)
    m2 = jnp.mean(dz * xh, axis=-1, keepdims=True)
    return (dz - m1 - xh * m2) * rs[:, 0:1], dg, db


def local_copies(pairs, sems, first=0):
    copies = [pltpu.make_async_copy(s, d, sems.at[first + i]) for i, (s, d) in enumerate(pairs)]
    for copy in copies:
        copy.start()
    return copies


def gelu_parts(u):
    phi = 0.5 * (1.0 + lax.erf(u * (1.0 / math.sqrt(2.0))))
    density = jnp.exp(u * u * -0.5) * (1.0 / math.sqrt(2.0 * math.pi))
    return u * phi, phi + u * density


def softmax(scores):
    top = jnp.max(scores, axis=-1, keepdims=True)
    e = jnp.exp(scores - top)
    return e / jnp.sum(e, axis=-1, keepdims=True)


def iota2(shape, dim):
    return lax.broadcasted_iota(jnp.int32, shape, dim)


def key_mask(queries, keys, count):
    return iota2((queries, keys), 1) < count


def head_masks(rows, width, size):
    lane = iota2((rows, width), 1)
    return [(lane >= h * size) & (lane < (h + 1) * size) for h in range(width // size)]


def pick(mask, x):
    return jnp.where(mask, x, jnp.zeros_like(x))


def attn_fwd(q, k, v, mask, heads, size):
    out = []
    for h in range(heads):
        s = slice(h * size, (h + 1) * size)
        scores = mm_nt(q[:, s], k[:, s]) * (1.0 / math.sqrt(size))
        p = softmax(jnp.where(mask, scores, masked_score))
        out.append(mm(p.astype(BF16), v[:, s]).astype(BF16))
    return jnp.concatenate(out, axis=1)


def attn_bwd(q, k, v, dm, mask, heads, size):
    dq, dk, dv = [], [], []
    for h in range(heads):
        s = slice(h * size, (h + 1) * size)
        scale = 1.0 / math.sqrt(size)
        scores = mm_nt(q[:, s], k[:, s]) * scale
        p = softmax(jnp.where(mask, scores, masked_score))
        dp = mm_nt(dm[:, s], v[:, s])
        dv.append(mm_tn(p.astype(BF16), dm[:, s]).astype(BF16))
        ds = p * (dp - jnp.sum(dp * p, axis=-1, keepdims=True))
        dr = (ds * scale).astype(BF16)
        dq.append(mm(dr, k[:, s]).astype(BF16))
        dk.append(mm_tn(dr, q[:, s]).astype(BF16))
    return tuple(jnp.concatenate(x, axis=1) for x in (dq, dk, dv))


def attn_fwd_small(q, k, v, mask, hm):
    total = None
    for m in hm:
        scores = mm_nt(pick(m, q), k) * (1.0 / math.sqrt(KT))
        p = softmax(jnp.where(mask, scores, masked_score))
        part = mm(p.astype(BF16), pick(m, v))
        total = part if total is None else total + part
    return total.astype(BF16)


def attn_bwd_small(q, k, v, dm, mask, hm):
    dq = dk = dv = None
    scale = 1.0 / math.sqrt(KT)
    for m in hm:
        scores = mm_nt(pick(m, q), k) * scale
        p = softmax(jnp.where(mask, scores, masked_score))
        dmh = pick(m, dm)
        dp = mm_nt(dmh, v)
        dvp = mm_tn(p.astype(BF16), dmh)
        ds = p * (dp - jnp.sum(dp * p, axis=-1, keepdims=True))
        dr = (ds * scale).astype(BF16)
        dqp = mm(dr, pick(m, k))
        dkp = mm_tn(dr, pick(m, q))
        dq, dk, dv = (dqp, dkp, dvp) if dq is None else (dq + dqp, dk + dkp, dv + dvp)
    return dq.astype(BF16), dk.astype(BF16), dv.astype(BF16)


def put(ref, m, rows, value, cols=None):
    value = value.reshape(2, value.shape[0] // 2, value.shape[1])
    if cols is None:
        ref[m, rows] = value
    else:
        ref[m, rows, :, cols] = value


def take(ref, m, rows):
    value = ref[m, rows]
    return value.reshape(2 * value.shape[1], value.shape[2])


def wide(m):
    return -(-m // 128) * 128

def weight_groups(ws):
    return ws[0:6], ws[6:10], ws[10:12] + ws[14:16], ws[12:14] + ws[16:18]


def saved_shapes(n, m, f, fi):
    text, image = (2, 4, LT, DT), (2, 4, RP, DV)
    att = [text, image, (2, 4, LT, 3 * n), (2, 4, RP, 3 * n), (2, 4, LT, n), (2, 4, RP, n)]
    own = [text, image, (2, 4, LT, 3 * wide(m)), (2, 4, RP, 3 * n), (2, 4, LT, wide(m)), (2, 4, RP, n)]
    ff = [text, image, (2, 4, LT, f), (2, 4, LT, f), (2, 4, RP, fi), (2, 4, RP, fi)]
    return [att, ff, own, ff]


NORM_SAVED = [(2, LT, DT), (2, RP, DV), (2, LT, 128), (2, RP, 128)]


def fwd_kernel(*refs):
    refs = list(refs)

    def grab(count):
        got = refs[:count]
        del refs[:count]
        return got

    tl, rc, xt, xi = grab(4)
    weights = grab(18)
    gains = grab(4)
    ot, oi = grab(2)
    saved_out = [grab(6) for _ in range(4)]
    norm_out = [grab(4) for _ in range(4)]
    vw = grab(18)
    saved = [grab(6) for _ in range(4)]
    norms = [grab(4) for _ in range(4)]
    rt, ri = grab(2)
    wsem, osem = grab(2)
    tg, tb, ig, ib = gains
    at = Places()
    loading = local_copies(list(zip(weights, vw)), wsem)
    greet(at)
    text, image = make_streams(at, refs)
    co_w, cf_w, sa_w, sf_w = weight_groups(vw)

    for m in range(2):
        ri[m] = xi[m].astype(F32)
        image.begin(saved[0][1], m, xi[m])
        rt[m] = xt[m].astype(F32)
        text.begin(saved[0][0], m, xt[m])

    storing = []

    def finish(s, last=False):
        slots_t, slots_i = saved[s][0], saved[s][1]
        xht, xhi, rst, rsi = norms[s]

        @pl.loop(0, 2)
        def _(m):
            yi = norm(ri[m] + image.total(m), ig[s : s + 1, :], ib[s : s + 1, :], xhi, rsi, m)
            image.end(slots_i, m)
            yt = norm(rt[m] + text.total(m), tg[s : s + 1, :], tb[s : s + 1, :], xht, rst, m)
            text.end(slots_t, m)
            if last:
                oi[m] = yi.astype(BF16)
                ot[m] = yt.astype(BF16)
            else:
                image.begin(saved[s + 1][1], m, yi.astype(BF16))
                text.begin(saved[s + 1][0], m, yt.astype(BF16))
                ri[m] = yi
                rt[m] = yt

        storing.extend(
            local_copies(
                list(zip(saved[s], saved_out[s])) + list(zip(norms[s], norm_out[s])), osem, 10 * s
            )
        )

    slots_t, slots_i, spt, spi, smt, smi = saved[0]
    wqt, wkvi, wot, wqi, wkvt, woi = co_w
    n = wqt.shape[1]
    heads = n // KC
    for c in loading[0:6]:
        c.wait()

    def co(half, m, rows):
        x = take(slots_i, m, rows)
        put(spi, m, rows, mm(x, wqi[...]).astype(BF16), slice(0, n))
        put(spi, m, rows, mm(x, wkvi[0]).astype(BF16), slice(n, 2 * n))
        put(spi, m, rows, mm(x, wkvi[1]).astype(BF16), slice(2 * n, 3 * n))
        x = take(slots_t, m, rows)
        put(spt, m, rows, mm(x, wqt[...]).astype(BF16), slice(0, n))
        put(spt, m, rows, mm(x, wkvt[0]).astype(BF16), slice(n, 2 * n))
        put(spt, m, rows, mm(x, wkvt[1]).astype(BF16), slice(2 * n, 3 * n))
        for j in range(2):
            b = at.base(half) + j
            t, v = spt[m, b], spi[m, b]
            smt[m, b] = attn_fwd(t[:, 0:n], v[:, n : 2 * n], v[:, 2 * n :],
                                 key_mask(LT, RP, rc[2 * b + m]), heads, KC)
            smi[m, b] = attn_fwd(v[:, 0:n], t[:, n : 2 * n], t[:, 2 * n :],
                                 key_mask(RP, LT, tl[2 * b + m]), heads, KC)
        image.partial(half, m, mm(take(smi, m, rows), woi[...]))
        text.partial(half, m, mm(take(smt, m, rows), wot[...]))

    steps(text, image, slots_t, slots_i, co)
    finish(0)

    def feed(s, w):
        slots_t, slots_i, sat, spt, sai, spi = saved[s]
        wti, wto, wii, wio = w

        def compute(half, m, rows):
            act, slope = gelu_parts(mm(take(slots_i, m, rows), wii[...]))
            act = act.astype(BF16)
            put(sai, m, rows, act)
            put(spi, m, rows, slope.astype(BF16))
            image.partial(half, m, mm(act, wio[...]))
            act, slope = gelu_parts(mm(take(slots_t, m, rows), wti[...]))
            act = act.astype(BF16)
            put(sat, m, rows, act)
            put(spt, m, rows, slope.astype(BF16))
            text.partial(half, m, mm(act, wto[...]))

        steps(text, image, slots_t, slots_i, compute)

    for c in loading[6:]:
        c.wait()
    feed(1, cf_w)
    finish(1)

    slots_t, slots_i, sqt, sqi, sst, ssi = saved[2]
    wt, wto, wi, wio = sa_w
    km = wt.shape[2]
    ks = wide(km)
    hm = head_masks(LT, km, KT)

    def own(half, m, rows):
        x = take(slots_i, m, rows)
        for i in range(3):
            put(sqi, m, rows, mm(x, wi[i]).astype(BF16), slice(i * n, (i + 1) * n))
        x = take(slots_t, m, rows)
        for i in range(3):
            put(sqt, m, rows, mm(x, wt[i]).astype(BF16), slice(i * ks, i * ks + km))
        for j in range(2):
            b = at.base(half) + j
            v = sqi[m, b]
            ssi[m, b] = attn_fwd(v[:, 0:n], v[:, n : 2 * n], v[:, 2 * n :],
                                 key_mask(RP, RP, rc[2 * b + m]), n // KV, KV)
            q, k, v = (sqt[m, b, :, i * ks : i * ks + km] for i in range(3))
            sst[m, b, :, 0:km] = attn_fwd_small(q, k, v, key_mask(LT, LT, tl[2 * b + m]), hm)
        image.partial(half, m, mm(take(ssi, m, rows), wio[...]))
        text.partial(half, m, mm(take(sst, m, rows)[:, 0:km], wto[...]))

    steps(text, image, slots_t, slots_i, own)
    finish(2)
    feed(3, sf_w)
    finish(3, True)
    for c in storing:
        c.wait()


def sds(shape, dtype=F32):
    return jax.ShapeDtypeStruct(shape, dtype)


def forward(tl, rc, xt, xi, weights, gains):
    n, m = weights[0].shape[1], weights[10].shape[2]
    f, fi = weights[6].shape[1], weights[8].shape[1]
    saved = saved_shapes(n, m, f, fi)
    flat = [s for group in saved for s in group]
    outs = (
        [sds((2, LT, DT), BF16), sds((2, RP, DV), BF16)]
        + [sds(s, BF16) for s in flat]
        + [sds(s) for _ in range(4) for s in NORM_SAVED]
    )
    scratch = (
        [pltpu.VMEM(w.shape, BF16) for w in weights]
        + [pltpu.VMEM(s, BF16) for s in flat]
        + [pltpu.VMEM(s, F32) for _ in range(4) for s in NORM_SAVED]
        + [pltpu.VMEM((2, LT, DT), F32), pltpu.VMEM((2, RP, DV), F32)]
        + [pltpu.SemaphoreType.DMA((18,)), pltpu.SemaphoreType.DMA((40,))]
        + COMM
    )
    got = pl.pallas_call(
        fwd_kernel,
        out_shape=outs,
        in_specs=[SM] * 2 + [VM] * 2 + [ANY] * 18 + [VM] * 4,
        out_specs=[VM] * 2 + [ANY] * 40,
        scratch_shapes=scratch,
        compiler_params=pltpu.CompilerParams(
            collective_id=1, has_side_effects=True, vmem_limit_bytes=63 << 20
        ),
        cost_estimate=pl.CostEstimate(flops=10**10, bytes_accessed=60 << 20, transcendentals=0),
        name="forward",
    )(tl, rc, xt, xi, *weights, *gains)
    return got[0], got[1], [got[2 + 6 * s : 8 + 6 * s] for s in range(4)], [got[26 + 4 * s : 30 + 4 * s] for s in range(4)]


def weight_grad(x, d, dw, dst, src=None):
    width = x.shape[3]
    blocks = width // 384 if width % 384 == 0 else width // 256
    cut = width // blocks
    per = 4 // blocks

    @pl.loop(0, blocks)
    def _(j):
        left = x[:, :, :, pl.ds(pl.multiple_of(j * cut, 128), cut)]
        left = left.reshape(-1, cut)
        right = d[...] if src is None else d[:, :, :, src]
        right = right.reshape(left.shape[0], right.shape[-1])
        got = mm_tn(left, right).astype(BF16)
        dw[pl.ds(j * per, per), :, :, dst] = got.reshape(per, 2, width // 8, got.shape[1])


def bwd_kernel(fast, *refs):
    refs = list(refs)

    def grab(count):
        got = refs[:count]
        del refs[:count]
        return got

    tl, rc, dt, di = grab(4)
    tg, ig = grab(2)
    weights = grab(18)
    saved_in = [grab(6) for _ in range(4)]
    norm_in = [grab(4) for _ in range(4)]
    ot, oi, gbt, gbi = grab(4)
    grads_out = [grab(2) for _ in range(4)]
    vff, vsa, vco = grab(4), grab(4), grab(6)
    feed_saved, att_saved = grab(4), grab(4)
    vxt, vxi = grab(2)
    xht, xhi, rst, rsi = grab(4)
    slots = [grab(2), grab(2)]
    dut, dui, dpt, dpi = grab(4)
    kt, ki = grab(2)
    dw = [grab(2) for _ in range(4)]
    lsem, osem = grab(2)
    at = Places()
    co_w, cf_w, sa_w, sf_w = weight_groups(weights)

    count = [0]

    def load(pairs):
        copies = local_copies(pairs, lsem, count[0])
        count[0] += len(pairs)
        return copies

    def done(copies):
        for c in copies:
            c.wait()

    vnorm = [xht, xhi, rst, rsi]
    norm_load = load(list(zip(norm_in[3], vnorm)))
    feed_load = load(list(zip(sf_w, vff)) + list(zip(saved_in[3][2:], feed_saved)))
    x_load = load(list(zip(saved_in[3][:2], (vxt, vxi))))
    sa_load = load(list(zip(sa_w, vsa)) + list(zip(saved_in[2][2:], att_saved)))
    co_load = load(list(zip(co_w, vco)))
    greet(at)
    text, image = make_streams(at, refs)
    gbt[...] = jnp.zeros_like(gbt)
    gbi[...] = jnp.zeros_like(gbi)

    def enter(s, m, gi, gt, slots_t, slots_i):
        dx, dg, db = norm_back(gi, xhi[m], rsi[m], ig[s : s + 1, :])
        ki[m] = dx
        image.begin(slots_i, m, dx.astype(BF16))
        gbi[s, 0:1, :] += dg
        gbi[s, 1:2, :] += db
        dx, dg, db = norm_back(gt, xht[m], rst[m], tg[s : s + 1, :])
        kt[m] = dx
        text.begin(slots_t, m, dx.astype(BF16))
        gbt[s, 0:1, :] += dg
        gbt[s, 1:2, :] += db

    done(norm_load)

    @pl.loop(0, 2)
    def _(m):
        enter(3, m, di[m].astype(F32), dt[m].astype(F32), *slots[0])

    norm_load = load(list(zip(norm_in[2], vnorm)))

    def finish(s, norm_load):
        if s > 0:
            done(norm_load)
        slots_t, slots_i = slots[(3 - s) % 2]

        @pl.loop(0, 2)
        def _(m):
            gi = ki[m] + image.total(m)
            image.end(slots_i, m)
            gt = kt[m] + text.total(m)
            text.end(slots_t, m)
            if s == 0:
                oi[m] = gi.astype(BF16)
                ot[m] = gt.astype(BF16)
            else:
                enter(s - 1, m, gi, gt, *slots[(4 - s) % 2])

        if s > 1:
            return load(list(zip(norm_in[s - 2], vnorm)))
        return None

    storing = []

    def feed(s, feed_load, x_load):
        wti, wto, wii, wio = vff
        sat, spt, sai, spi = feed_saved
        slots_t, slots_i = slots[(3 - s) % 2]
        done(feed_load)

        def compute(half, m, rows):
            du = (mm_nt(take(slots_i, m, rows), wio[...]) * take(spi, m, rows).astype(F32)).astype(BF16)
            put(dui, m, rows, du)
            image.partial(half, m, mm_nt(du, wii[...]))
            du = (mm_nt(take(slots_t, m, rows), wto[...]) * take(spt, m, rows).astype(F32)).astype(BF16)
            put(dut, m, rows, du)
            text.partial(half, m, mm_nt(du, wti[...]))

        steps(text, image, slots_t, slots_i, compute)
        done(x_load)
        dwt, dwi = dw[s]
        f, fi = wti.shape[1], wii.shape[1]
        weight_grad(vxt, dut, dwt, slice(0, f))
        weight_grad(slots_t, sat, dwt, slice(f, 2 * f))
        weight_grad(vxi, dui, dwi, slice(0, fi))
        weight_grad(slots_i, sai, dwi, slice(fi, 2 * fi))

    def send_grads(s):
        storing.extend(local_copies(list(zip(dw[s], grads_out[s])), osem, 2 * s))

    feed(3, feed_load, x_load)
    send_grads(3)
    x_load = load(list(zip(saved_in[2][:2], (vxt, vxi))))
    feed_load = load(list(zip(cf_w, vff)) + list(zip(saved_in[1][2:], feed_saved)))
    norm_load = finish(3, norm_load)

    wt, wto, wi, wio = vsa
    sqt, sqi, sst, ssi = att_saved
    n, km = wi.shape[2], wt.shape[2]
    ks = wide(km)
    hm = head_masks(LT, km, KT)
    own_t, own_i = slots[1]
    done(sa_load)

    def own(half, m, rows):
        dm = mm_nt(take(own_i, m, rows), wio[...]).astype(BF16)
        dmt = mm_nt(take(own_t, m, rows), wto[...]).astype(BF16)
        for j in range(2):
            b = at.base(half) + j
            v = sqi[m, b]
            grads = attn_bwd(v[:, 0:n], v[:, n : 2 * n], v[:, 2 * n :], dm[j * RP : (j + 1) * RP],
                             key_mask(RP, RP, rc[2 * b + m]), n // KV, KV)
            for i, g in enumerate(grads):
                dpi[m, b, :, i * n : (i + 1) * n] = g
            q, k, v = (sqt[m, b, :, i * ks : i * ks + km] for i in range(3))
            grads = attn_bwd_small(q, k, v, dmt[j * LT : (j + 1) * LT], key_mask(LT, LT, tl[2 * b + m]), hm)
            for i, g in enumerate(grads):
                dpt[m, b, :, i * ks : i * ks + km] = g
        dp = take(dpi, m, rows)
        image.partial(half, m, sum(mm_nt(dp[:, i * n : (i + 1) * n], wi[i]) for i in range(3)))
        dp = take(dpt, m, rows)
        text.partial(half, m, sum(mm_nt(dp[:, i * ks : i * ks + km], wt[i]) for i in range(3)))

    steps(text, image, own_t, own_i, own)
    done(x_load)
    dwt, dwi = dw[2]
    for i in range(3):
        weight_grad(vxt, dpt, dwt, slice(i * km, (i + 1) * km), slice(i * ks, i * ks + km))
    weight_grad(own_t, sst, dwt, slice(3 * km, 4 * km), slice(0, km))
    weight_grad(vxi, dpi, dwi, slice(0, 3 * n))
    weight_grad(own_i, ssi, dwi, slice(3 * n, 4 * n))
    send_grads(2)
    x_load = load(list(zip(saved_in[1][:2], (vxt, vxi))))
    co_load += load(list(zip(saved_in[0][2:], att_saved)))
    norm_load = finish(2, norm_load)

    feed(1, feed_load, x_load)
    send_grads(1)
    x_load = load(list(zip(saved_in[0][:2], (vxt, vxi))))
    finish(1, norm_load)

    wqt, wkvi, wot, wqi, wkvt, woi = vco
    heads = n // KC
    co_t, co_i = slots[1]
    done(co_load)

    def co(half, m, rows):
        dm = mm_nt(take(co_i, m, rows), woi[...]).astype(BF16)
        dmt = mm_nt(take(co_t, m, rows), wot[...]).astype(BF16)
        for j in range(2):
            b = at.base(half) + j
            t, v = sqt[m, b], sqi[m, b]
            dq, dk, dv = attn_bwd(v[:, 0:n], t[:, n : 2 * n], t[:, 2 * n :], dm[j * RP : (j + 1) * RP],
                                  key_mask(RP, LT, tl[2 * b + m]), heads, KC)
            dpi[m, b, :, 0:n] = dq
            dpt[m, b, :, n : 2 * n] = dk
            dpt[m, b, :, 2 * n :] = dv
            dq, dk, dv = attn_bwd(t[:, 0:n], v[:, n : 2 * n], v[:, 2 * n :], dmt[j * LT : (j + 1) * LT],
                                  key_mask(LT, RP, rc[2 * b + m]), heads, KC)
            dpt[m, b, :, 0:n] = dq
            dpi[m, b, :, n : 2 * n] = dk
            dpi[m, b, :, 2 * n :] = dv
        dp = take(dpi, m, rows)
        image.partial(half, m, mm_nt(dp[:, 0:n], wqi[...]) + mm_nt(dp[:, n : 2 * n], wkvi[0])
                      + mm_nt(dp[:, 2 * n :], wkvi[1]))
        dp = take(dpt, m, rows)
        text.partial(half, m, mm_nt(dp[:, 0:n], wqt[...]) + mm_nt(dp[:, n : 2 * n], wkvt[0])
                     + mm_nt(dp[:, 2 * n :], wkvt[1]))

    steps(text, image, co_t, co_i, co)
    done(x_load)
    dwt, dwi = dw[0]
    weight_grad(vxt, dpt, dwt, slice(0, 3 * n))
    weight_grad(co_t, sst, dwt, slice(3 * n, 4 * n))
    weight_grad(vxi, dpi, dwi, slice(0, 3 * n))
    weight_grad(co_i, ssi, dwi, slice(3 * n, 4 * n))
    send_grads(0)
    finish(0, None)
    done(storing)


def backward(fast, tl, rc, dt, di, weights, gains, saved, norms):
    n, m = weights[0].shape[1], weights[10].shape[2]
    f, fi = weights[6].shape[1], weights[8].shape[1]
    tg, _, ig, _ = gains
    co_w, cf_w, sa_w, sf_w = weight_groups(list(weights))
    text_cols = (4 * n, 2 * f, 4 * m, 2 * f)
    image_cols = (4 * n, 2 * fi, 4 * n, 2 * fi)
    dw_shapes = [
        s
        for i in range(4)
        for s in ((4, 2, DT // 8, text_cols[i]), (4, 2, DV // 8, image_cols[i]))
    ]
    text, image = (2, 4, LT, DT), (2, 4, RP, DV)
    outs = [
        sds((2, LT, DT), BF16), sds((2, RP, DV), BF16), sds((4, 2, DT)), sds((4, 2, DV)),
    ] + [sds(s, BF16) for s in dw_shapes]
    buffers = (
        [w.shape for w in cf_w] + [w.shape for w in sa_w] + [w.shape for w in co_w]
        + [x.shape for x in saved[1][2:]] + [x.shape for x in saved[0][2:]]
        + [text, image]
    )
    scratch = (
        [pltpu.VMEM(s, BF16) for s in buffers]
        + [pltpu.VMEM(s, F32) for s in NORM_SAVED]
        + [pltpu.VMEM(s, BF16) for s in (text, image, text, image)]
        + [pltpu.VMEM(s, BF16) for s in ((2, 4, LT, f), (2, 4, RP, fi), (2, 4, LT, 3 * n), (2, 4, RP, 3 * n))]
        + [pltpu.VMEM((2, LT, DT), F32), pltpu.VMEM((2, RP, DV), F32)]
        + [pltpu.VMEM(s, BF16) for s in dw_shapes]
        + [pltpu.SemaphoreType.DMA((64,)), pltpu.SemaphoreType.DMA((8,))]
        + COMM
    )
    got = pl.pallas_call(
        functools.partial(bwd_kernel, fast),
        out_shape=outs,
        in_specs=[SM] * 2 + [VM] * 4 + [ANY] * (18 + 24 + 16),
        out_specs=[VM] * 4 + [ANY] * 8,
        scratch_shapes=scratch,
        compiler_params=pltpu.CompilerParams(
            collective_id=2, has_side_effects=True, vmem_limit_bytes=63 << 20
        ),
        cost_estimate=pl.CostEstimate(flops=2 * 10**10, bytes_accessed=60 << 20, transcendentals=0),
        name="backward",
    )(tl, rc, dt, di, tg, ig, *weights, *[x for g in saved for x in g], *[x for g in norms for x in g])
    return got[0:4], [got[4 + 2 * s : 6 + 2 * s] for s in range(4)]


def to_pairs(x):
    return jnp.pad(x.reshape(2, RG, DV), ((0, 0), (0, RP - RG), (0, 0)))


def from_pairs(x):
    return x[:, :RG].reshape(2 * RG, DV)


def local(dp, text_in, image_in, tl, rc, *rest):
    weights, gains, (text_cot, image_cot) = rest[:18], rest[18:22], rest[22:]
    n, m, f = weights[0].shape[1], weights[10].shape[2], weights[6].shape[1]
    rows = (2, LT, DT)
    yt, yi, saved, norms = forward(tl, rc, text_in.reshape(rows), to_pairs(image_in), weights, gains)
    (gt, gi, tgb, igb), grads = backward(
        False, tl, rc, text_cot.reshape(rows), to_pairs(image_cot), weights, gains, saved, norms
    )
    tgb, igb = lax.psum((tgb, igb), ("dp", "tensor"))
    flat = [g for pair in grads for g in pair]
    whole = jnp.concatenate([g.reshape(dp, -1) for g in flat], axis=1)
    whole = lax.psum_scatter(whole.reshape(-1, 128), "dp", scatter_dimension=0, tiled=True)
    whole = whole.astype(F32).reshape(-1)
    parts, at = [], 0
    for g in flat:
        size = g.size // dp
        parts.append(whole[at : at + size].reshape(-1, g.shape[3]))
        at += size
    ct, ci, ft, fi, st, si, ht, hi = parts
    return (
        yt.reshape(2 * LT, DT), from_pairs(yi), gt.reshape(2 * LT, DT), from_pairs(gi),
        ct[:, :n],
        jnp.stack([ci[:, n : 2 * n], ci[:, 2 * n : 3 * n]]),
        ct[:, 3 * n :].T,
        ci[:, :n],
        jnp.stack([ct[:, n : 2 * n], ct[:, 2 * n : 3 * n]]),
        ci[:, 3 * n :].T,
        ft[:, :f], ft[:, f:].T, fi[:, :n], fi[:, n:].T,
        jnp.stack([st[:, i * m : (i + 1) * m] for i in range(3)]),
        st[:, 3 * m :].T,
        ht[:, :f], ht[:, f:].T,
        jnp.stack([si[:, i * n : (i + 1) * n] for i in range(3)]),
        si[:, 3 * n :].T,
        hi[:, :n], hi[:, n:].T,
        tgb[:, 0], tgb[:, 1], igb[:, 0], igb[:, 1],
    )


def solution(mesh):
    rows, pairs = P(("dp", "tensor"), None), P("dp")
    wide, tall, stack = P(None, "tensor"), P("tensor", None), P(None, None, "tensor")
    g_wide, g_tall, g_stack = P("dp", "tensor"), P("tensor", "dp"), P(None, "dp", "tensor")
    return jax.shard_map(
        functools.partial(local, mesh.shape["dp"]),
        mesh=mesh,
        in_specs=(
            rows, rows, pairs, pairs,
            wide, stack, tall, wide, stack, tall,
            wide, tall, wide, tall,
            stack, tall, wide, tall,
            stack, tall, wide, tall,
            P(), P(), P(), P(),
            rows, rows,
        ),
        out_specs=(
            rows, rows, rows, rows,
            g_wide, g_stack, g_tall, g_wide, g_stack, g_tall,
            g_wide, g_tall, g_wide, g_tall,
            g_stack, g_tall, g_wide, g_tall,
            g_stack, g_tall, g_wide, g_tall,
            P(), P(), P(), P(),
        ),
        check_vma=False,
    )
```

```python
import functools
import math

import jax
import jax.numpy as jnp
from jax import lax
from jax.experimental import pallas as pl
from jax.experimental.pallas import tpu as pltpu
from jax.sharding import PartitionSpec as P

KT = 64
KV = 128
KC = 128
LT = 128
RG = 36
RP = 48
DT = 768
DV = 1024

epsilon = 1e-05
masked_score = -1e30
F32 = jnp.float32
BF16 = jnp.bfloat16
MESH = pl.DeviceIdType.MESH
VM = pl.BlockSpec(memory_space=pltpu.VMEM)
SM = pl.BlockSpec(memory_space=pltpu.SMEM)
ANY = pl.BlockSpec(memory_space=pl.ANY)


def mm(a, b):
    return lax.dot_general(a, b, (((1,), (0,)), ((), ())), preferred_element_type=F32)


def mm_nt(a, b):
    return lax.dot_general(a, b, (((1,), (1,)), ((), ())), preferred_element_type=F32)


def mm_tn(a, b):
    return lax.dot_general(a, b, (((0,), (0,)), ((), ())), preferred_element_type=F32)


class Places:
    def __init__(self):
        me = lax.axis_index("tensor")
        chip, core = lax.div(me, 2), lax.rem(me, 2)
        self.me, self.chip, self.core = me, chip, core
        self.core_mate = 2 * chip + (1 - core)
        self.chip_mate = 2 * (1 - chip) + core

    def base(self, half):
        return 2 * (self.chip + half - 2 * self.chip * half)


class Stream:
    def __init__(self, at, stream, part, near, relay, out, got_near, got_far, got_chip, sends, recvs):
        self.at, self.stream, self.part = at, stream, part
        self.near, self.relay, self.out = near, relay, out
        self.got_near, self.got_far, self.got_chip = got_near, got_far, got_chip
        self.sends, self.recvs = sends, recvs

    def push(self, src, dst, m, slot, mate):
        return pltpu.make_async_remote_copy(
            src_ref=src,
            dst_ref=dst,
            send_sem=self.sends.at[self.stream, m, slot],
            recv_sem=self.recvs.at[self.stream, m, slot],
            device_id={"tensor": mate},
            device_id_type=MESH,
        )

    def copy(self, slots, m, which):
        at = self.at
        me, cm, xm = at.me, at.core_mate, at.chip_mate
        if which == 0:
            return self.push(slots.at[m, me], slots.at[m, me], m, 0, cm)
        if which == 1:
            return self.push(slots.at[m, me], slots.at[m, me], m, 1, xm)
        if which == 2:
            return self.push(slots.at[m, xm], slots.at[m, xm], m, 2, cm)
        if which == 3:
            return self.push(self.near.at[m], self.got_near.at[m], m, 3, cm)
        if which == 4:
            return self.push(self.relay.at[m], self.got_far.at[m], m, 4, cm)
        return self.push(self.out.at[m], self.got_chip.at[m], m, 5, xm)

    def begin(self, slots, m, rows):
        slots[m, self.at.me] = rows
        self.copy(slots, m, 1).start()
        self.copy(slots, m, 0).start()

    def relay_gather(self, slots, m):
        self.copy(slots, m, 1).wait_recv()
        self.copy(slots, m, 2).start()

    def partial(self, half, m, value):
        part, other = self.part, 1 - self.at.core
        part[m, half] = value.reshape(part.shape[2:])

        @pl.when(half == 0)
        def _():
            self.near[m] = part[m, 0, other].astype(BF16)
            self.copy(None, m, 3).start()

        @pl.when(half == 1)
        def _():
            self.relay[m] = part[m, 1, other].astype(BF16)
            self.copy(None, m, 4).start()

    def forward(self, m):
        self.copy(None, m, 4).wait_recv()
        self.out[m] = (self.part[m, 1, self.at.core] + self.got_far[m].astype(F32)).astype(BF16)
        self.copy(None, m, 5).start()

    def total(self, m):
        self.copy(None, m, 3).wait_recv()
        self.copy(None, m, 5).wait_recv()
        return self.part[m, 0, self.at.core] + self.got_near[m].astype(F32) + self.got_chip[m].astype(F32)

    def end(self, slots, m):
        for which in range(6):
            self.copy(slots, m, which).wait_send()


def stream_scratch(rows, width):
    return [pltpu.VMEM((2, 2, 2, rows, width), F32)] + [pltpu.VMEM((2, rows, width), BF16)] * 6


COMM = stream_scratch(LT, DT) + stream_scratch(RP, DV) + [pltpu.SemaphoreType.DMA((2, 2, 6))] * 2


def make_streams(at, refs):
    text = Stream(at, 0, *refs[0:7], refs[14], refs[15])
    image = Stream(at, 1, *refs[7:14], refs[14], refs[15])
    return text, image


def greet(at):
    barrier = pltpu.get_barrier_semaphore()
    for mate in (at.core_mate, at.chip_mate):
        pl.semaphore_signal(barrier, inc=1, device_id={"tensor": mate}, device_id_type=MESH)
    pl.semaphore_wait(barrier, 2)


def steps(text, image, tslots, islots, compute, between=()):
    @pl.loop(0, 4)
    def _(i):
        half, m = lax.div(i, 2), lax.rem(i, 2)
        for place, task in enumerate(between):
            pl.when(i == 2 + place)(task)

        @pl.when(half == 0)
        def _():
            image.copy(islots, m, 0).wait_recv()
            text.copy(tslots, m, 0).wait_recv()

        @pl.when(half == 1)
        def _():
            image.relay_gather(islots, m)
            text.relay_gather(tslots, m)
            image.copy(islots, m, 2).wait_recv()
            text.copy(tslots, m, 2).wait_recv()

        compute(half, m, pl.ds(text.at.base(half), 2))

        @pl.when(half == 1)
        def _():
            image.forward(m)
            text.forward(m)


def norm(pre, gain, bias, xh_ref, rs_ref, m):
    mean = jnp.mean(pre, axis=-1, keepdims=True)
    centered = pre - mean
    variance = jnp.mean(centered * centered, axis=-1, keepdims=True)
    rs = lax.rsqrt(variance + epsilon)
    xh = centered * rs
    xh_ref[m] = xh
    rs_ref[m] = jnp.broadcast_to(rs, rs_ref.shape[1:])
    return xh * gain + bias


def norm_back(grad, xh, rs, gain):
    dz = grad * gain
    dg = jnp.sum(grad * xh, axis=0, keepdims=True)
    db = jnp.sum(grad, axis=0, keepdims=True)
    m1 = jnp.mean(dz, axis=-1, keepdims=True)
    m2 = jnp.mean(dz * xh, axis=-1, keepdims=True)
    return (dz - m1 - xh * m2) * rs[:, 0:1], dg, db


def local_copies(pairs, sems, first=0):
    copies = [pltpu.make_async_copy(s, d, sems.at[first + i]) for i, (s, d) in enumerate(pairs)]
    for copy in copies:
        copy.start()
    return copies


def gelu_parts(u):
    phi = 0.5 * (1.0 + lax.erf(u * (1.0 / math.sqrt(2.0))))
    density = jnp.exp(u * u * -0.5) * (1.0 / math.sqrt(2.0 * math.pi))
    return u * phi, phi + u * density


def softmax(scores):
    top = jnp.max(scores, axis=-1, keepdims=True)
    e = jnp.exp(scores - top)
    return e / jnp.sum(e, axis=-1, keepdims=True)


def iota2(shape, dim):
    return lax.broadcasted_iota(jnp.int32, shape, dim)


def key_mask(queries, keys, count):
    return iota2((queries, keys), 1) < count


def head_masks(rows, width, size):
    lane = iota2((rows, width), 1)
    return [(lane >= h * size) & (lane < (h + 1) * size) for h in range(width // size)]


def pick(mask, x):
    return jnp.where(mask, x, jnp.zeros_like(x))


def attn_fwd(q, k, v, mask, heads, size):
    out = []
    for h in range(heads):
        s = slice(h * size, (h + 1) * size)
        scores = mm_nt(q[:, s], k[:, s]) * (1.0 / math.sqrt(size))
        p = softmax(jnp.where(mask, scores, masked_score))
        out.append(mm(p.astype(BF16), v[:, s]).astype(BF16))
    return jnp.concatenate(out, axis=1)


def attn_bwd(q, k, v, dm, mask, heads, size):
    dq, dk, dv = [], [], []
    for h in range(heads):
        s = slice(h * size, (h + 1) * size)
        scale = 1.0 / math.sqrt(size)
        scores = mm_nt(q[:, s], k[:, s]) * scale
        p = softmax(jnp.where(mask, scores, masked_score))
        dp = mm_nt(dm[:, s], v[:, s])
        dv.append(mm_tn(p.astype(BF16), dm[:, s]).astype(BF16))
        ds = p * (dp - jnp.sum(dp * p, axis=-1, keepdims=True))
        dr = (ds * scale).astype(BF16)
        dq.append(mm(dr, k[:, s]).astype(BF16))
        dk.append(mm_tn(dr, q[:, s]).astype(BF16))
    return tuple(jnp.concatenate(x, axis=1) for x in (dq, dk, dv))


def attn_fwd_small(q, k, v, mask, hm):
    total = None
    for m in hm:
        scores = mm_nt(pick(m, q), k) * (1.0 / math.sqrt(KT))
        p = softmax(jnp.where(mask, scores, masked_score))
        part = mm(p.astype(BF16), pick(m, v))
        total = part if total is None else total + part
    return total.astype(BF16)


def attn_bwd_small(q, k, v, dm, mask, hm):
    dq = dk = dv = None
    scale = 1.0 / math.sqrt(KT)
    for m in hm:
        scores = mm_nt(pick(m, q), k) * scale
        p = softmax(jnp.where(mask, scores, masked_score))
        dmh = pick(m, dm)
        dp = mm_nt(dmh, v)
        dvp = mm_tn(p.astype(BF16), dmh)
        ds = p * (dp - jnp.sum(dp * p, axis=-1, keepdims=True))
        dr = (ds * scale).astype(BF16)
        dqp = mm(dr, pick(m, k))
        dkp = mm_tn(dr, pick(m, q))
        dq, dk, dv = (dqp, dkp, dvp) if dq is None else (dq + dqp, dk + dkp, dv + dvp)
    return dq.astype(BF16), dk.astype(BF16), dv.astype(BF16)


def put(ref, m, rows, value, cols=None):
    value = value.reshape(2, value.shape[0] // 2, value.shape[1])
    if cols is None:
        ref[m, rows] = value
    else:
        ref[m, rows, :, cols] = value


def take(ref, m, rows):
    value = ref[m, rows]
    return value.reshape(2 * value.shape[1], value.shape[2])


def wide(m):
    return -(-m // 128) * 128

def weight_groups(ws):
    return ws[0:6], ws[6:10], ws[10:12] + ws[14:16], ws[12:14] + ws[16:18]


def saved_shapes(n, m, f, fi):
    text, image = (2, 4, LT, DT), (2, 4, RP, DV)
    att = [text, image, (2, 4, LT, 3 * n), (2, 4, RP, 3 * n), (2, 4, LT, n), (2, 4, RP, n)]
    own = [text, image, (2, 4, LT, 3 * wide(m)), (2, 4, RP, 3 * n), (2, 4, LT, wide(m)), (2, 4, RP, n)]
    ff = [text, image, (2, 4, LT, f), (2, 4, LT, f), (2, 4, RP, fi), (2, 4, RP, fi)]
    return [att, ff, own, ff]


NORM_SAVED = [(2, LT, DT), (2, RP, DV), (2, LT, 128), (2, RP, 128)]


def fwd_kernel(*refs):
    refs = list(refs)

    def grab(count):
        got = refs[:count]
        del refs[:count]
        return got

    tl, rc, xt, xi = grab(4)
    weights = grab(18)
    gains = grab(4)
    ot, oi = grab(2)
    saved_out = [grab(6) for _ in range(4)]
    norm_out = [grab(4) for _ in range(4)]
    vw = grab(18)
    saved = [grab(6) for _ in range(4)]
    norms = [grab(4) for _ in range(4)]
    rt, ri = grab(2)
    wsem, osem = grab(2)
    tg, tb, ig, ib = gains
    at = Places()
    loading = local_copies(list(zip(weights, vw)), wsem)
    greet(at)
    text, image = make_streams(at, refs)
    co_w, cf_w, sa_w, sf_w = weight_groups(vw)

    for m in range(2):
        ri[m] = xi[m].astype(F32)
        image.begin(saved[0][1], m, xi[m])
        rt[m] = xt[m].astype(F32)
        text.begin(saved[0][0], m, xt[m])

    storing = []

    def finish(s, last=False):
        slots_t, slots_i = saved[s][0], saved[s][1]
        xht, xhi, rst, rsi = norms[s]

        @pl.loop(0, 2)
        def _(m):
            yi = norm(ri[m] + image.total(m), ig[s : s + 1, :], ib[s : s + 1, :], xhi, rsi, m)
            image.end(slots_i, m)
            yt = norm(rt[m] + text.total(m), tg[s : s + 1, :], tb[s : s + 1, :], xht, rst, m)
            text.end(slots_t, m)
            if last:
                oi[m] = yi.astype(BF16)
                ot[m] = yt.astype(BF16)
            else:
                image.begin(saved[s + 1][1], m, yi.astype(BF16))
                text.begin(saved[s + 1][0], m, yt.astype(BF16))
                ri[m] = yi
                rt[m] = yt

        storing.extend(
            local_copies(
                list(zip(saved[s], saved_out[s])) + list(zip(norms[s], norm_out[s])), osem, 10 * s
            )
        )

    slots_t, slots_i, spt, spi, smt, smi = saved[0]
    wqt, wkvi, wot, wqi, wkvt, woi = co_w
    n = wqt.shape[1]
    heads = n // KC
    for c in loading[0:6]:
        c.wait()

    def co(half, m, rows):
        x = take(slots_i, m, rows)
        put(spi, m, rows, mm(x, wqi[...]).astype(BF16), slice(0, n))
        put(spi, m, rows, mm(x, wkvi[0]).astype(BF16), slice(n, 2 * n))
        put(spi, m, rows, mm(x, wkvi[1]).astype(BF16), slice(2 * n, 3 * n))
        x = take(slots_t, m, rows)
        put(spt, m, rows, mm(x, wqt[...]).astype(BF16), slice(0, n))
        put(spt, m, rows, mm(x, wkvt[0]).astype(BF16), slice(n, 2 * n))
        put(spt, m, rows, mm(x, wkvt[1]).astype(BF16), slice(2 * n, 3 * n))
        for j in range(2):
            b = at.base(half) + j
            t, v = spt[m, b], spi[m, b]
            smt[m, b] = attn_fwd(t[:, 0:n], v[:, n : 2 * n], v[:, 2 * n :],
                                 key_mask(LT, RP, rc[2 * b + m]), heads, KC)
            smi[m, b] = attn_fwd(v[:, 0:n], t[:, n : 2 * n], t[:, 2 * n :],
                                 key_mask(RP, LT, tl[2 * b + m]), heads, KC)
        image.partial(half, m, mm(take(smi, m, rows), woi[...]))
        text.partial(half, m, mm(take(smt, m, rows), wot[...]))

    steps(text, image, slots_t, slots_i, co)
    finish(0)

    def feed(s, w):
        slots_t, slots_i, sat, spt, sai, spi = saved[s]
        wti, wto, wii, wio = w

        def compute(half, m, rows):
            act, slope = gelu_parts(mm(take(slots_i, m, rows), wii[...]))
            act = act.astype(BF16)
            put(sai, m, rows, act)
            put(spi, m, rows, slope.astype(BF16))
            image.partial(half, m, mm(act, wio[...]))
            act, slope = gelu_parts(mm(take(slots_t, m, rows), wti[...]))
            act = act.astype(BF16)
            put(sat, m, rows, act)
            put(spt, m, rows, slope.astype(BF16))
            text.partial(half, m, mm(act, wto[...]))

        steps(text, image, slots_t, slots_i, compute)

    for c in loading[6:]:
        c.wait()
    feed(1, cf_w)
    finish(1)

    slots_t, slots_i, sqt, sqi, sst, ssi = saved[2]
    wt, wto, wi, wio = sa_w
    km = wt.shape[2]
    ks = wide(km)
    hm = head_masks(LT, km, KT)

    def own(half, m, rows):
        x = take(slots_i, m, rows)
        for i in range(3):
            put(sqi, m, rows, mm(x, wi[i]).astype(BF16), slice(i * n, (i + 1) * n))
        x = take(slots_t, m, rows)
        for i in range(3):
            put(sqt, m, rows, mm(x, wt[i]).astype(BF16), slice(i * ks, i * ks + km))
        for j in range(2):
            b = at.base(half) + j
            v = sqi[m, b]
            ssi[m, b] = attn_fwd(v[:, 0:n], v[:, n : 2 * n], v[:, 2 * n :],
                                 key_mask(RP, RP, rc[2 * b + m]), n // KV, KV)
            q, k, v = (sqt[m, b, :, i * ks : i * ks + km] for i in range(3))
            sst[m, b, :, 0:km] = attn_fwd_small(q, k, v, key_mask(LT, LT, tl[2 * b + m]), hm)
        image.partial(half, m, mm(take(ssi, m, rows), wio[...]))
        text.partial(half, m, mm(take(sst, m, rows)[:, 0:km], wto[...]))

    steps(text, image, slots_t, slots_i, own)
    finish(2)
    feed(3, sf_w)
    finish(3, True)
    for c in storing:
        c.wait()


def sds(shape, dtype=F32):
    return jax.ShapeDtypeStruct(shape, dtype)


def forward(tl, rc, xt, xi, weights, gains):
    n, m = weights[0].shape[1], weights[10].shape[2]
    f, fi = weights[6].shape[1], weights[8].shape[1]
    saved = saved_shapes(n, m, f, fi)
    flat = [s for group in saved for s in group]
    outs = (
        [sds((2, LT, DT), BF16), sds((2, RP, DV), BF16)]
        + [sds(s, BF16) for s in flat]
        + [sds(s) for _ in range(4) for s in NORM_SAVED]
    )
    scratch = (
        [pltpu.VMEM(w.shape, BF16) for w in weights]
        + [pltpu.VMEM(s, BF16) for s in flat]
        + [pltpu.VMEM(s, F32) for _ in range(4) for s in NORM_SAVED]
        + [pltpu.VMEM((2, LT, DT), F32), pltpu.VMEM((2, RP, DV), F32)]
        + [pltpu.SemaphoreType.DMA((18,)), pltpu.SemaphoreType.DMA((40,))]
        + COMM
    )
    got = pl.pallas_call(
        fwd_kernel,
        out_shape=outs,
        in_specs=[SM] * 2 + [VM] * 2 + [ANY] * 18 + [VM] * 4,
        out_specs=[VM] * 2 + [ANY] * 40,
        scratch_shapes=scratch,
        compiler_params=pltpu.CompilerParams(
            collective_id=1, has_side_effects=True, vmem_limit_bytes=63 << 20
        ),
        cost_estimate=pl.CostEstimate(flops=10**10, bytes_accessed=60 << 20, transcendentals=0),
        name="forward",
    )(tl, rc, xt, xi, *weights, *gains)
    return got[0], got[1], [got[2 + 6 * s : 8 + 6 * s] for s in range(4)], [got[26 + 4 * s : 30 + 4 * s] for s in range(4)]


def weight_grad(x, d, dw, dst, src=None):
    width = x.shape[3]
    blocks = width // 384 if width % 384 == 0 else width // 256
    cut = width // blocks
    per = 4 // blocks

    @pl.loop(0, blocks)
    def _(j):
        left = x[:, :, :, pl.ds(pl.multiple_of(j * cut, 128), cut)]
        left = left.reshape(-1, cut)
        right = d[...] if src is None else d[:, :, :, src]
        right = right.reshape(left.shape[0], right.shape[-1])
        got = mm_tn(left, right).astype(BF16)
        dw[pl.ds(j * per, per), :, :, dst] = got.reshape(per, 2, width // 8, got.shape[1])


class Depth:
    def __init__(self):
        self.p = lax.axis_index("dp")
        self.z, self.y = lax.div(self.p, 2), lax.rem(self.p, 2)
        self.y_mate = 2 * self.z + 1 - self.y

    def greet(self, at):
        barrier = pltpu.get_barrier_semaphore()

        def hello(who):
            pl.semaphore_signal(barrier, inc=1, device_id=who, device_id_type=MESH)

        hello({"tensor": at.core_mate})
        hello({"tensor": at.chip_mate})
        hello({"dp": self.y_mate})
        hello({"dp": lax.rem(self.p + 4, 8)})
        pl.when(self.z < 3)(lambda: hello({"dp": self.p + 2}))
        pl.when(self.z > 0)(lambda: hello({"dp": self.p - 2}))
        pl.semaphore_wait(barrier, 4 + (self.z + 2) // 3 + (5 - self.z) // 3)


def add_rows(dst, src):
    @pl.loop(0, dst.shape[0] // 16)
    def _(i):
        r = pl.ds(pl.multiple_of(i * 16, 16), 16)
        dst[r, :] = (dst[r, :].astype(F32) + src[r, :].astype(F32)).astype(BF16)


class Unit:
    def __init__(self, depth, index, dw, from_y, from_z, out, ysem, zsem, credit, osem, credit_used):
        cols = dw.shape[3]
        self.d, self.k, self.dw, self.out = depth, index, dw, out
        self.from_y, self.from_z = from_y.at[:, :, 0:cols], from_z.at[:, :, :, 0:cols]
        self.ysem, self.zsem, self.credit, self.osem = ysem, zsem, credit, osem
        self.credit_used = credit_used

    def y_copy(self):
        d = self.d
        return pltpu.make_async_remote_copy(
            src_ref=self.dw.at[:, 1 - d.y],
            dst_ref=self.from_y,
            send_sem=self.ysem.at[0, self.k],
            recv_sem=self.ysem.at[1, self.k],
            device_id={"dp": d.y_mate},
            device_id_type=MESH,
        )

    def z_copy(self, flow, step, t, to):
        return pltpu.make_async_remote_copy(
            src_ref=self.dw.at[t, self.d.y],
            dst_ref=self.from_z.at[flow, step],
            send_sem=self.zsem.at[0, self.k, flow, step],
            recv_sem=self.zsem.at[1, self.k, flow, step],
            device_id={"dp": to},
            device_id_type=MESH,
        )

    def start_y(self):
        if self.credit_used:
            pl.semaphore_wait(self.credit.at[self.k % 2], 1)
        self.y_copy().start()

    def send(self, step):
        d = self.d
        w = 3 - d.z
        pl.when(d.z <= step)(lambda: self.z_copy(0, step, 3 - step + d.z, d.p + 2).start())
        pl.when(w <= step)(lambda: self.z_copy(1, step, step - w, d.p - 2).start())

    def receive(self, step):
        d = self.d
        w = 3 - d.z

        def right():
            t = 2 - step + d.z
            self.z_copy(0, step, t, d.p).wait_recv()
            add_rows(self.dw.at[t, d.y], self.from_z.at[0, step])

        def left():
            t = 1 + step - w
            self.z_copy(1, step, t, d.p).wait_recv()
            add_rows(self.dw.at[t, d.y], self.from_z.at[1, step])

        pl.when((d.z >= 1) & (d.z - 1 <= step))(right)
        pl.when((w >= 1) & (w - 1 <= step))(left)

    def task(self, number):
        d = self.d
        if number == 0:
            self.y_copy().wait_recv()

            @pl.loop(0, 4)
            def _(t):
                add_rows(self.dw.at[t, d.y], self.from_y.at[t])

            if self.k < 4:
                pl.semaphore_signal(
                    self.credit.at[self.k % 2], inc=1, device_id={"dp": d.y_mate}, device_id_type=MESH
                )
        else:
            self.receive(number - 1)
        if number < 3:
            self.send(number)
        else:
            self.copy_out().start()

    def copy_out(self):
        return pltpu.make_async_copy(self.dw.at[self.d.z, self.d.y], self.out, self.osem.at[self.k])

    def end(self):
        d = self.d
        w = 3 - d.z
        self.y_copy().wait_send()
        for step in range(3):
            pl.when(d.z <= step)(self.z_copy(0, step, 0, d.p).wait_send)
            pl.when(w <= step)(self.z_copy(1, step, 0, d.p).wait_send)
        self.copy_out().wait()


class NormSum:
    def __init__(self, at, depth, text, image, got_t, got_i, sems):
        p, z, y = depth.p, depth.z, depth.y
        self.text, self.image, self.got_t, self.got_i, self.sems = text, image, got_t, got_i, sems
        self.to = [
            {"tensor": at.core_mate},
            {"tensor": at.chip_mate},
            {"dp": depth.y_mate},
            {"dp": 2 * (z + 1 - 2 * lax.rem(z, 2)) + y},
            {"dp": lax.rem(p + 4, 8)},
        ]

    def copies(self, k):
        return [
            pltpu.make_async_remote_copy(
                src_ref=src.at[k],
                dst_ref=dst.at[k],
                send_sem=self.sems.at[0, i, k],
                recv_sem=self.sems.at[1, i, k],
                device_id=self.to[k],
                device_id_type=MESH,
            )
            for i, (src, dst) in enumerate(((self.text, self.got_t), (self.image, self.got_i)))
        ]

    def task(self, k):
        if k > 0:
            for c in self.copies(k - 1):
                c.wait_recv()
            self.text[k] = self.text[k - 1] + self.got_t[k - 1]
            self.image[k] = self.image[k - 1] + self.got_i[k - 1]
        if k < 5:
            for c in self.copies(k):
                c.start()

    def end(self):
        for k in range(5):
            for c in self.copies(k):
                c.wait_send()


def bwd_kernel(fast, *refs):
    refs = list(refs)

    def grab(count):
        got = refs[:count]
        del refs[:count]
        return got

    tl, rc, dt, di = grab(4)
    tg, ig = grab(2)
    weights = grab(18)
    saved_in = [grab(6) for _ in range(4)]
    norm_in = [grab(4) for _ in range(4)]
    ot, oi, gbt, gbi = grab(4)
    grads_out = [grab(2) for _ in range(4)]
    vff, vsa, vco = grab(4), grab(4), grab(6)
    feed_saved, att_saved = grab(4), grab(4)
    vxt, vxi = grab(2)
    xht, xhi, rst, rsi = grab(4)
    slots = [grab(2), grab(2)]
    dut, dui, dpt, dpi = grab(4)
    kt, ki = grab(2)
    dw = [grab(2) for _ in range(4)]
    lsem, osem = grab(2)
    at = Places()
    co_w, cf_w, sa_w, sf_w = weight_groups(weights)
    units, nsum = {}, None
    if fast:
        depth = Depth()
        from_y, from_z = [grab(2), grab(2)], [grab(2), grab(2)]
        ysem, zsem, credit = grab(3)
        nt, ni, got_nt, got_ni, nsem = grab(5)
        nsum = NormSum(at, depth, nt, ni, got_nt, got_ni, nsem)
        for s in range(4):
            order = 3 - s
            for i in range(2):
                units[s, i] = Unit(depth, 2 * order + i, dw[s][i], from_y[order % 2][i], from_z[order % 2][i],
                                   grads_out[s][i], ysem, zsem, credit.at[order % 2], osem, order >= 2)

    count = [0]

    def load(pairs):
        copies = local_copies(pairs, lsem, count[0])
        count[0] += len(pairs)
        return copies

    def done(copies):
        for c in copies:
            c.wait()

    vnorm = [xht, xhi, rst, rsi]
    norm_load = load(list(zip(norm_in[3], vnorm)))
    feed_load = load(list(zip(sf_w, vff)) + list(zip(saved_in[3][2:], feed_saved)))
    x_load = load(list(zip(saved_in[3][:2], (vxt, vxi))))
    sa_load = load(list(zip(sa_w, vsa)) + list(zip(saved_in[2][2:], att_saved)))
    co_load = load(list(zip(co_w, vco)))
    if fast:
        depth.greet(at)
        acc_t, acc_i = nt.at[0], ni.at[0]
    else:
        greet(at)
        acc_t, acc_i = gbt, gbi
    text, image = make_streams(at, refs)
    acc_t[...] = jnp.zeros_like(acc_t)
    acc_i[...] = jnp.zeros_like(acc_i)

    def run(*tasks):
        def go():
            for unit, number in tasks:
                if unit == "norm":
                    nsum.task(number)
                elif number == "y":
                    units[unit].start_y()
                else:
                    units[unit].task(number)

        return go if fast else (lambda: None)

    def enter(s, m, gi, gt, slots_t, slots_i):
        dx, dg, db = norm_back(gi, xhi[m], rsi[m], ig[s : s + 1, :])
        ki[m] = dx
        image.begin(slots_i, m, dx.astype(BF16))
        acc_i[s, 0:1, :] += dg
        acc_i[s, 1:2, :] += db
        dx, dg, db = norm_back(gt, xht[m], rst[m], tg[s : s + 1, :])
        kt[m] = dx
        text.begin(slots_t, m, dx.astype(BF16))
        acc_t[s, 0:1, :] += dg
        acc_t[s, 1:2, :] += db

    done(norm_load)

    @pl.loop(0, 2)
    def _(m):
        enter(3, m, di[m].astype(F32), dt[m].astype(F32), *slots[0])

    norm_load = load(list(zip(norm_in[2], vnorm)))

    def finish(s, norm_load):
        if s > 0:
            done(norm_load)
        slots_t, slots_i = slots[(3 - s) % 2]

        @pl.loop(0, 2)
        def _(m):
            gi = ki[m] + image.total(m)
            image.end(slots_i, m)
            gt = kt[m] + text.total(m)
            text.end(slots_t, m)
            if s == 0:
                oi[m] = gi.astype(BF16)
                ot[m] = gt.astype(BF16)
            else:
                enter(s - 1, m, gi, gt, *slots[(4 - s) % 2])

        if s > 1:
            return load(list(zip(norm_in[s - 2], vnorm)))
        return None

    storing = []

    def feed(s, feed_load, x_load, between=()):
        wti, wto, wii, wio = vff
        sat, spt, sai, spi = feed_saved
        slots_t, slots_i = slots[(3 - s) % 2]
        done(feed_load)

        def compute(half, m, rows):
            du = (mm_nt(take(slots_i, m, rows), wio[...]) * take(spi, m, rows).astype(F32)).astype(BF16)
            put(dui, m, rows, du)
            image.partial(half, m, mm_nt(du, wii[...]))
            du = (mm_nt(take(slots_t, m, rows), wto[...]) * take(spt, m, rows).astype(F32)).astype(BF16)
            put(dut, m, rows, du)
            text.partial(half, m, mm_nt(du, wti[...]))

        steps(text, image, slots_t, slots_i, compute, between)
        done(x_load)
        dwt, dwi = dw[s]
        f, fi = wti.shape[1], wii.shape[1]
        weight_grad(vxt, dut, dwt, slice(0, f))
        weight_grad(slots_t, sat, dwt, slice(f, 2 * f))
        weight_grad(vxi, dui, dwi, slice(0, fi))
        weight_grad(slots_i, sai, dwi, slice(fi, 2 * fi))

    def send_grads(s):
        if not fast:
            storing.extend(local_copies(list(zip(dw[s], grads_out[s])), osem, 2 * s))

    feed(3, feed_load, x_load)
    send_grads(3)
    run(((3, 0), "y"), ((3, 1), "y"))()
    x_load = load(list(zip(saved_in[2][:2], (vxt, vxi))))
    feed_load = load(list(zip(cf_w, vff)) + list(zip(saved_in[1][2:], feed_saved)))
    norm_load = finish(3, norm_load)

    wt, wto, wi, wio = vsa
    sqt, sqi, sst, ssi = att_saved
    n, km = wi.shape[2], wt.shape[2]
    ks = wide(km)
    hm = head_masks(LT, km, KT)
    own_t, own_i = slots[1]
    done(sa_load)

    def own(half, m, rows):
        dm = mm_nt(take(own_i, m, rows), wio[...]).astype(BF16)
        dmt = mm_nt(take(own_t, m, rows), wto[...]).astype(BF16)
        for j in range(2):
            b = at.base(half) + j
            v = sqi[m, b]
            grads = attn_bwd(v[:, 0:n], v[:, n : 2 * n], v[:, 2 * n :], dm[j * RP : (j + 1) * RP],
                             key_mask(RP, RP, rc[2 * b + m]), n // KV, KV)
            for i, g in enumerate(grads):
                dpi[m, b, :, i * n : (i + 1) * n] = g
            q, k, v = (sqt[m, b, :, i * ks : i * ks + km] for i in range(3))
            grads = attn_bwd_small(q, k, v, dmt[j * LT : (j + 1) * LT], key_mask(LT, LT, tl[2 * b + m]), hm)
            for i, g in enumerate(grads):
                dpt[m, b, :, i * ks : i * ks + km] = g
        dp = take(dpi, m, rows)
        image.partial(half, m, sum(mm_nt(dp[:, i * n : (i + 1) * n], wi[i]) for i in range(3)))
        dp = take(dpt, m, rows)
        text.partial(half, m, sum(mm_nt(dp[:, i * ks : i * ks + km], wt[i]) for i in range(3)))

    steps(text, image, own_t, own_i, own)
    done(x_load)
    dwt, dwi = dw[2]
    for i in range(3):
        weight_grad(vxt, dpt, dwt, slice(i * km, (i + 1) * km), slice(i * ks, i * ks + km))
    weight_grad(own_t, sst, dwt, slice(3 * km, 4 * km), slice(0, km))
    weight_grad(vxi, dpi, dwi, slice(0, 3 * n))
    weight_grad(own_i, ssi, dwi, slice(3 * n, 4 * n))
    send_grads(2)
    run(((2, 0), "y"), ((2, 1), "y"))()
    x_load = load(list(zip(saved_in[1][:2], (vxt, vxi))))
    co_load += load(list(zip(saved_in[0][2:], att_saved)))
    norm_load = finish(2, norm_load)

    feed(1, feed_load, x_load, (run(((3, 0), 0)), run(((3, 0), 1))))
    send_grads(1)
    run(((3, 0), 2))()
    x_load = load(list(zip(saved_in[0][:2], (vxt, vxi))))
    finish(1, norm_load)
    run(("norm", 0), ((3, 0), 3), ((3, 1), 0), ((1, 0), "y"), ((1, 1), "y"))()

    wqt, wkvi, wot, wqi, wkvt, woi = vco
    heads = n // KC
    co_t, co_i = slots[1]
    done(co_load)

    def co(half, m, rows):
        dm = mm_nt(take(co_i, m, rows), woi[...]).astype(BF16)
        dmt = mm_nt(take(co_t, m, rows), wot[...]).astype(BF16)
        for j in range(2):
            b = at.base(half) + j
            t, v = sqt[m, b], sqi[m, b]
            dq, dk, dv = attn_bwd(v[:, 0:n], t[:, n : 2 * n], t[:, 2 * n :], dm[j * RP : (j + 1) * RP],
                                  key_mask(RP, LT, tl[2 * b + m]), heads, KC)
            dpi[m, b, :, 0:n] = dq
            dpt[m, b, :, n : 2 * n] = dk
            dpt[m, b, :, 2 * n :] = dv
            dq, dk, dv = attn_bwd(t[:, 0:n], v[:, n : 2 * n], v[:, 2 * n :], dmt[j * LT : (j + 1) * LT],
                                  key_mask(LT, RP, rc[2 * b + m]), heads, KC)
            dpt[m, b, :, 0:n] = dq
            dpi[m, b, :, n : 2 * n] = dk
            dpi[m, b, :, 2 * n :] = dv
        dp = take(dpi, m, rows)
        image.partial(half, m, mm_nt(dp[:, 0:n], wqi[...]) + mm_nt(dp[:, n : 2 * n], wkvi[0])
                      + mm_nt(dp[:, 2 * n :], wkvi[1]))
        dp = take(dpt, m, rows)
        text.partial(half, m, mm_nt(dp[:, 0:n], wqt[...]) + mm_nt(dp[:, n : 2 * n], wkvt[0])
                     + mm_nt(dp[:, 2 * n :], wkvt[1]))

    steps(text, image, co_t, co_i, co,
          (run(((3, 1), 1), ("norm", 1)), run(((3, 1), 2), ("norm", 2))))
    done(x_load)
    dwt, dwi = dw[0]
    weight_grad(vxt, dpt, dwt, slice(0, 3 * n))
    weight_grad(co_t, sst, dwt, slice(3 * n, 4 * n))
    weight_grad(vxi, dpi, dwi, slice(0, 3 * n))
    weight_grad(co_i, ssi, dwi, slice(3 * n, 4 * n))
    send_grads(0)
    run(("norm", 3), ((3, 1), 3), ((2, 0), 0), ((0, 0), "y"))()
    finish(0, None)
    run(("norm", 4), ((2, 0), 1), ("norm", 5))()
    if fast:
        gbt[...] = nt[5]
        gbi[...] = ni[5]
    run(((2, 0), 2), ((2, 0), 3), ((2, 1), 0), ((0, 1), "y"), ((2, 1), 1), ((2, 1), 2), ((2, 1), 3))()
    run(*(((s, i), k) for s in (1, 0) for i in range(2) for k in range(4)))()
    if fast:
        nsum.end()
        for unit in units.values():
            unit.end()
    done(storing)


def backward(fast, tl, rc, dt, di, weights, gains, saved, norms):
    n, m = weights[0].shape[1], weights[10].shape[2]
    f, fi = weights[6].shape[1], weights[8].shape[1]
    tg, _, ig, _ = gains
    co_w, cf_w, sa_w, sf_w = weight_groups(list(weights))
    text_cols = (4 * n, 2 * f, 4 * m, 2 * f)
    image_cols = (4 * n, 2 * fi, 4 * n, 2 * fi)
    dw_shapes = [
        s
        for i in range(4)
        for s in ((4, 2, DT // 8, text_cols[i]), (4, 2, DV // 8, image_cols[i]))
    ]
    text, image = (2, 4, LT, DT), (2, 4, RP, DV)
    outs = [
        sds((2, LT, DT), BF16), sds((2, RP, DV), BF16), sds((4, 2, DT)), sds((4, 2, DV)),
    ] + [sds(s[2:] if fast else s, BF16) for s in dw_shapes]
    both = [((DT // 8, c), (DV // 8, d)) for c, d in
            ((2 * f, 2 * fi), (max(4 * n, 4 * m), 4 * n))]
    sums = [] if not fast else (
        [pltpu.VMEM((4, *s), BF16) for pair in both for s in pair]
        + [pltpu.VMEM((2, 3, *s), BF16) for pair in both for s in pair]
        + [pltpu.SemaphoreType.DMA((2, 8)), pltpu.SemaphoreType.DMA((2, 8, 2, 3)),
           pltpu.SemaphoreType.REGULAR((2, 2))]
        + [pltpu.VMEM((6, 4, 2, w), F32) for w in (DT, DV)]
        + [pltpu.VMEM((5, 4, 2, w), F32) for w in (DT, DV)]
        + [pltpu.SemaphoreType.DMA((2, 2, 5))]
    )
    buffers = (
        [w.shape for w in cf_w] + [w.shape for w in sa_w] + [w.shape for w in co_w]
        + [x.shape for x in saved[1][2:]] + [x.shape for x in saved[0][2:]]
        + [text, image]
    )
    scratch = (
        [pltpu.VMEM(s, BF16) for s in buffers]
        + [pltpu.VMEM(s, F32) for s in NORM_SAVED]
        + [pltpu.VMEM(s, BF16) for s in (text, image, text, image)]
        + [pltpu.VMEM(s, BF16) for s in ((2, 4, LT, f), (2, 4, RP, fi), (2, 4, LT, 3 * n), (2, 4, RP, 3 * n))]
        + [pltpu.VMEM((2, LT, DT), F32), pltpu.VMEM((2, RP, DV), F32)]
        + [pltpu.VMEM(s, BF16) for s in dw_shapes]
        + [pltpu.SemaphoreType.DMA((64,)), pltpu.SemaphoreType.DMA((8,))]
        + sums
        + COMM
    )
    got = pl.pallas_call(
        functools.partial(bwd_kernel, fast),
        out_shape=outs,
        in_specs=[SM] * 2 + [VM] * 4 + [ANY] * (18 + 24 + 16),
        out_specs=[VM] * 4 + [ANY] * 8,
        scratch_shapes=scratch,
        compiler_params=pltpu.CompilerParams(
            collective_id=2, has_side_effects=True, vmem_limit_bytes=63 << 20
        ),
        cost_estimate=pl.CostEstimate(flops=2 * 10**10, bytes_accessed=60 << 20, transcendentals=0),
        name="backward",
    )(tl, rc, dt, di, tg, ig, *weights, *[x for g in saved for x in g], *[x for g in norms for x in g])
    return got[0:4], [got[4 + 2 * s : 6 + 2 * s] for s in range(4)]


def to_pairs(x):
    return jnp.pad(x.reshape(2, RG, DV), ((0, 0), (0, RP - RG), (0, 0)))


def from_pairs(x):
    return x[:, :RG].reshape(2 * RG, DV)


def local(dp, text_in, image_in, tl, rc, *rest):
    weights, gains, (text_cot, image_cot) = rest[:18], rest[18:22], rest[22:]
    n, m, f = weights[0].shape[1], weights[10].shape[2], weights[6].shape[1]
    rows, fast = (2, LT, DT), dp == 8
    yt, yi, saved, norms = forward(tl, rc, text_in.reshape(rows), to_pairs(image_in), weights, gains)
    (gt, gi, tgb, igb), grads = backward(
        fast, tl, rc, text_cot.reshape(rows), to_pairs(image_cot), weights, gains, saved, norms
    )
    flat = [g for pair in grads for g in pair]
    if fast:
        parts = [g.astype(F32) for g in flat]
    else:
        tgb, igb = lax.psum((tgb, igb), ("dp", "tensor"))
        parts = []
        for g in flat:
            g = g.reshape(-1, g.shape[3])
            parts.append(lax.psum_scatter(g, "dp", scatter_dimension=0, tiled=True).astype(F32))
    ct, ci, ft, fi, st, si, ht, hi = parts
    return (
        yt.reshape(2 * LT, DT), from_pairs(yi), gt.reshape(2 * LT, DT), from_pairs(gi),
        ct[:, :n],
        jnp.stack([ci[:, n : 2 * n], ci[:, 2 * n : 3 * n]]),
        ct[:, 3 * n :].T,
        ci[:, :n],
        jnp.stack([ct[:, n : 2 * n], ct[:, 2 * n : 3 * n]]),
        ci[:, 3 * n :].T,
        ft[:, :f], ft[:, f:].T, fi[:, :n], fi[:, n:].T,
        jnp.stack([st[:, i * m : (i + 1) * m] for i in range(3)]),
        st[:, 3 * m :].T,
        ht[:, :f], ht[:, f:].T,
        jnp.stack([si[:, i * n : (i + 1) * n] for i in range(3)]),
        si[:, 3 * n :].T,
        hi[:, :n], hi[:, n:].T,
        tgb[:, 0], tgb[:, 1], igb[:, 0], igb[:, 1],
    )


def solution(mesh):
    rows, pairs = P(("dp", "tensor"), None), P("dp")
    wide, tall, stack = P(None, "tensor"), P("tensor", None), P(None, None, "tensor")
    g_wide, g_tall, g_stack = P("dp", "tensor"), P("tensor", "dp"), P(None, "dp", "tensor")
    return jax.shard_map(
        functools.partial(local, mesh.shape["dp"]),
        mesh=mesh,
        in_specs=(
            rows, rows, pairs, pairs,
            wide, stack, tall, wide, stack, tall,
            wide, tall, wide, tall,
            stack, tall, wide, tall,
            stack, tall, wide, tall,
            P(), P(), P(), P(),
            rows, rows,
        ),
        out_specs=(
            rows, rows, rows, rows,
            g_wide, g_stack, g_tall, g_wide, g_stack, g_tall,
            g_wide, g_tall, g_wide, g_tall,
            g_stack, g_tall, g_wide, g_tall,
            g_stack, g_tall, g_wide, g_tall,
            P(), P(), P(), P(),
        ),
        check_vma=False,
    )
```

```python
import functools
import math

import jax
import jax.numpy as jnp
from jax import lax
from jax.experimental import pallas as pl
from jax.experimental.pallas import tpu as pltpu
from jax.sharding import PartitionSpec as P

KT = 64
KV = 128
KC = 128
LT = 128
RG = 36
RP = 48
RS = 40
VMEM_LIMIT = 63 << 20
DT = 768
DV = 1024

epsilon = 1e-05
masked_score = -1e30
F32 = jnp.float32
BF16 = jnp.bfloat16
MESH = pl.DeviceIdType.MESH
VM = pl.BlockSpec(memory_space=pltpu.VMEM)
SM = pl.BlockSpec(memory_space=pltpu.SMEM)
ANY = pl.BlockSpec(memory_space=pl.ANY)


def mm(a, b):
    return lax.dot_general(a, b, (((1,), (0,)), ((), ())), preferred_element_type=F32)


def mm_nt(a, b):
    return lax.dot_general(a, b, (((1,), (1,)), ((), ())), preferred_element_type=F32)


def mm_tn(a, b):
    return lax.dot_general(a, b, (((0,), (0,)), ((), ())), preferred_element_type=F32)


class Places:
    def __init__(self):
        me = lax.axis_index("tensor")
        chip, core = lax.div(me, 2), lax.rem(me, 2)
        self.me, self.chip, self.core = me, chip, core
        self.core_mate = 2 * chip + (1 - core)
        self.chip_mate = 2 * (1 - chip) + core

    def base(self, half):
        return 2 * (self.chip + half - 2 * self.chip * half)


class Stream:
    def __init__(self, at, stream, part, near, relay, out, got_near, got_far, got_chip, sends, recvs):
        self.at, self.stream, self.part = at, stream, part
        self.sent = pl.ds(0, RS if stream else LT)
        self.near, self.relay, self.out = near, relay, out
        self.got_near, self.got_far, self.got_chip = got_near, got_far, got_chip
        self.sends, self.recvs = sends, recvs

    def push(self, src, dst, m, slot, mate):
        return pltpu.make_async_remote_copy(
            src_ref=src,
            dst_ref=dst,
            send_sem=self.sends.at[self.stream, m, slot],
            recv_sem=self.recvs.at[self.stream, m, slot],
            device_id={"tensor": mate},
            device_id_type=MESH,
        )

    def copy(self, slots, m, which):
        at = self.at
        me, cm, xm, r = at.me, at.core_mate, at.chip_mate, self.sent
        if which == 0:
            return self.push(slots.at[m, me, r], slots.at[m, me, r], m, 0, cm)
        if which == 1:
            return self.push(slots.at[m, me, r], slots.at[m, me, r], m, 1, xm)
        if which == 2:
            return self.push(slots.at[m, xm, r], slots.at[m, xm, r], m, 2, cm)
        if which == 3:
            return self.push(self.near.at[m, r], self.got_near.at[m, r], m, 3, cm)
        if which == 4:
            return self.push(self.relay.at[m, r], self.got_far.at[m, r], m, 4, cm)
        return self.push(self.out.at[m, r], self.got_chip.at[m, r], m, 5, xm)

    def clear(self, slot_sets):
        for got in (self.got_near, self.got_far, self.got_chip):
            got[:, RS:, :] = jnp.zeros((2, RP - RS, got.shape[2]), BF16)
        for slots in slot_sets:
            slots[:, :, RS:, :] = jnp.zeros((2, 4, RP - RS, slots.shape[3]), BF16)

    def begin(self, slots, m, rows):
        slots[m, self.at.me] = rows
        self.copy(slots, m, 1).start()
        self.copy(slots, m, 0).start()

    def relay_gather(self, slots, m):
        self.copy(slots, m, 1).wait_recv()
        self.copy(slots, m, 2).start()

    def partial(self, half, m, value):
        part, other = self.part, 1 - self.at.core
        value = value.reshape(part.shape[1:])

        @pl.when(half == 0)
        def _():
            part[m] = value
            self.near[m] = part[m, other].astype(BF16)
            self.copy(None, m, 3).start()

        @pl.when(half == 1)
        def _():
            part[2] = value
            self.relay[m] = part[2, other].astype(BF16)
            self.copy(None, m, 4).start()

    def forward(self, m):
        self.copy(None, m, 4).wait_recv()
        self.out[m] = (self.part[2, self.at.core] + self.got_far[m].astype(F32)).astype(BF16)
        self.copy(None, m, 5).start()

    def total(self, m):
        self.copy(None, m, 3).wait_recv()
        self.copy(None, m, 5).wait_recv()
        return self.part[m, self.at.core] + self.got_near[m].astype(F32) + self.got_chip[m].astype(F32)

    def end(self, slots, m):
        for which in range(6):
            self.copy(slots, m, which).wait_send()


def stream_scratch(rows, width):
    return [pltpu.VMEM((3, 2, rows, width), F32)] + [pltpu.VMEM((2, rows, width), BF16)] * 6


COMM = stream_scratch(LT, DT) + stream_scratch(RP, DV) + [pltpu.SemaphoreType.DMA((2, 2, 6))] * 2


def make_streams(at, refs):
    text = Stream(at, 0, *refs[0:7], refs[14], refs[15])
    image = Stream(at, 1, *refs[7:14], refs[14], refs[15])
    return text, image


def greet(at):
    barrier = pltpu.get_barrier_semaphore()
    for mate in (at.core_mate, at.chip_mate):
        pl.semaphore_signal(barrier, inc=1, device_id={"tensor": mate}, device_id_type=MESH)
    pl.semaphore_wait(barrier, 2)


def steps(text, image, tslots, islots, compute, between=()):
    @pl.loop(0, 4)
    def _(i):
        half, m = lax.div(i, 2), lax.rem(i, 2)
        for place, task in enumerate(between):
            if task is not None:
                pl.when(i == place)(task)

        @pl.when(half == 0)
        def _():
            image.copy(islots, m, 0).wait_recv()
            text.copy(tslots, m, 0).wait_recv()

        @pl.when(half == 1)
        def _():
            image.relay_gather(islots, m)
            text.relay_gather(tslots, m)
            image.copy(islots, m, 2).wait_recv()
            text.copy(tslots, m, 2).wait_recv()

        compute(half, m, pl.ds(text.at.base(half), 2))

        @pl.when(half == 1)
        def _():
            image.forward(m)
            text.forward(m)


def norm(pre, gain, bias, xh_ref, rs_ref, m):
    mean = jnp.mean(pre, axis=-1, keepdims=True)
    centered = pre - mean
    variance = jnp.mean(centered * centered, axis=-1, keepdims=True)
    rs = lax.rsqrt(variance + epsilon)
    xh = centered * rs
    xh_ref[m] = xh
    rs_ref[m] = jnp.broadcast_to(rs, rs_ref.shape[1:])
    return xh * gain + bias


def norm_back(grad, xh, rs, gain):
    dz = grad * gain
    dg = jnp.sum(grad * xh, axis=0, keepdims=True)
    db = jnp.sum(grad, axis=0, keepdims=True)
    m1 = jnp.mean(dz, axis=-1, keepdims=True)
    m2 = jnp.mean(dz * xh, axis=-1, keepdims=True)
    return (dz - m1 - xh * m2) * rs[:, 0:1], dg, db


def local_copies(pairs, sems, first=0):
    copies = [pltpu.make_async_copy(s, d, sems.at[first + i]) for i, (s, d) in enumerate(pairs)]
    for copy in copies:
        copy.start()
    return copies


def gelu_parts(u):
    phi = 0.5 * (1.0 + lax.erf(u * (1.0 / math.sqrt(2.0))))
    density = jnp.exp(u * u * -0.5) * (1.0 / math.sqrt(2.0 * math.pi))
    return u * phi, phi + u * density


def softmax(scores):
    top = jnp.max(scores, axis=-1, keepdims=True)
    e = jnp.exp(scores - top)
    return e / jnp.sum(e, axis=-1, keepdims=True)


def iota2(shape, dim):
    return lax.broadcasted_iota(jnp.int32, shape, dim)


def key_mask(queries, keys, count):
    return iota2((queries, keys), 1) < count


def head_masks(rows, width, size):
    lane = iota2((rows, width), 1)
    return [(lane >= h * size) & (lane < (h + 1) * size) for h in range(width // size)]


def pick(mask, x):
    return jnp.where(mask, x, jnp.zeros_like(x))


def attn_fwd(q, k, v, mask, heads, size):
    out = []
    for h in range(heads):
        s = slice(h * size, (h + 1) * size)
        scores = mm_nt(q[:, s], k[:, s]) * (1.0 / math.sqrt(size))
        p = softmax(jnp.where(mask, scores, masked_score))
        out.append(mm(p.astype(BF16), v[:, s]).astype(BF16))
    return jnp.concatenate(out, axis=1)


def attn_bwd(q, k, v, dm, mask, heads, size):
    dq, dk, dv = [], [], []
    for h in range(heads):
        s = slice(h * size, (h + 1) * size)
        scale = 1.0 / math.sqrt(size)
        scores = mm_nt(q[:, s], k[:, s]) * scale
        p = softmax(jnp.where(mask, scores, masked_score))
        dp = mm_nt(dm[:, s], v[:, s])
        dv.append(mm_tn(p.astype(BF16), dm[:, s]).astype(BF16))
        ds = p * (dp - jnp.sum(dp * p, axis=-1, keepdims=True))
        dr = (ds * scale).astype(BF16)
        dq.append(mm(dr, k[:, s]).astype(BF16))
        dk.append(mm_tn(dr, q[:, s]).astype(BF16))
    return tuple(jnp.concatenate(x, axis=1) for x in (dq, dk, dv))


def attn_fwd_small(q, k, v, mask, hm):
    total = None
    for m in hm:
        scores = mm_nt(pick(m, q), k) * (1.0 / math.sqrt(KT))
        p = softmax(jnp.where(mask, scores, masked_score))
        part = mm(p.astype(BF16), pick(m, v))
        total = part if total is None else total + part
    return total.astype(BF16)


def attn_bwd_small(q, k, v, dm, mask, hm):
    dq = dk = dv = None
    scale = 1.0 / math.sqrt(KT)
    for m in hm:
        scores = mm_nt(pick(m, q), k) * scale
        p = softmax(jnp.where(mask, scores, masked_score))
        dmh = pick(m, dm)
        dp = mm_nt(dmh, v)
        dvp = mm_tn(p.astype(BF16), dmh)
        ds = p * (dp - jnp.sum(dp * p, axis=-1, keepdims=True))
        dr = (ds * scale).astype(BF16)
        dqp = mm(dr, pick(m, k))
        dkp = mm_tn(dr, pick(m, q))
        dq, dk, dv = (dqp, dkp, dvp) if dq is None else (dq + dqp, dk + dkp, dv + dvp)
    return dq.astype(BF16), dk.astype(BF16), dv.astype(BF16)


def split_rows(x, pairs):
    value = x[...].astype(F32)
    pairs[...] = jnp.zeros(pairs.shape, F32)
    pairs[0, 0:RG] = value[0:RG]
    pairs[1, 0:RG] = value[RG:]


def join_rows(pairs, out):
    out[...] = jnp.concatenate([pairs[0, 0:RG], pairs[1, 0:RG]], axis=0).astype(out.dtype)


def put(ref, m, rows, value, cols=None):
    value = value.reshape(2, value.shape[0] // 2, value.shape[1])
    if cols is None:
        ref[m, rows] = value
    else:
        ref[m, rows, :, cols] = value


def take(ref, m, rows):
    value = ref[m, rows]
    return value.reshape(2 * value.shape[1], value.shape[2])


def wide(m):
    return -(-m // 128) * 128

def weight_groups(ws):
    return ws[0:6], ws[6:10], ws[10:12] + ws[14:16], ws[12:14] + ws[16:18]


def saved_shapes(n, m, f, fi):
    text, image = (2, 4, LT, DT), (2, 4, RP, DV)
    att = [text, image, (2, 4, LT, 3 * n), (2, 4, RP, 3 * n), (2, 4, LT, n), (2, 4, RP, n)]
    ff = [text, image, (2, 4, LT, f), (2, 4, LT, f), (2, 4, RP, fi), (2, 4, RP, fi)]
    assert wide(m) == n
    return [att, ff, att, ff]


SAVED = [6, 6, 6, 6]
NORM_SAVED = [(2, LT, DT), (2, RP, DV), (2, LT, 128), (2, RP, 128)]


def fwd_kernel(*refs):
    refs = list(refs)

    def grab(count):
        got = refs[:count]
        del refs[:count]
        return got

    tl, rc, xt, xi = grab(4)
    weights = grab(18)
    gains = grab(4)
    ot, oi = grab(2)
    saved_out = [grab(k) for k in SAVED]
    norm_out = [grab(4) for _ in range(4)]
    vw = grab(18)
    saved = [grab(k) for k in SAVED]
    norms = [grab(4) for _ in range(4)]
    rt, ri = grab(2)
    wsem, osem = grab(2)
    tg, tb, ig, ib = gains
    at = Places()
    loading = local_copies(list(zip(weights, vw)), wsem)
    text, image = make_streams(at, refs)
    image.clear([group[1] for group in saved])
    greet(at)
    co_w, cf_w, sa_w, sf_w = weight_groups(vw)

    split_rows(xi, ri)
    for m in range(2):
        image.begin(saved[0][1], m, ri[m].astype(BF16))
        rt[m] = xt[m].astype(F32)
        text.begin(saved[0][0], m, xt[m])

    storing = []

    def finish(s, last=False):
        slots_t, slots_i = saved[s][0], saved[s][1]
        xht, xhi, rst, rsi = norms[s]

        @pl.loop(0, 2)
        def _(m):
            yi = norm(ri[m] + image.total(m), ig[s : s + 1, :], ib[s : s + 1, :], xhi, rsi, m)
            image.end(slots_i, m)
            yt = norm(rt[m] + text.total(m), tg[s : s + 1, :], tb[s : s + 1, :], xht, rst, m)
            text.end(slots_t, m)
            if last:
                ri[m] = yi
                ot[m] = yt.astype(BF16)
            else:
                image.begin(saved[s + 1][1], m, yi.astype(BF16))
                text.begin(saved[s + 1][0], m, yt.astype(BF16))
                ri[m] = yi
                rt[m] = yt

        storing.extend(
            local_copies(
                list(zip(saved[s], saved_out[s])) + list(zip(norms[s], norm_out[s])), osem, 12 * s
            )
        )
        if last:
            join_rows(ri, oi)

    slots_t, slots_i, spt, spi, smt, smi = saved[0]
    wqt, wkvi, wot, wqi, wkvt, woi = co_w
    n = wqt.shape[1]
    heads = n // KC
    for c in loading[0:6]:
        c.wait()

    def co(half, m, rows):
        x = take(slots_i, m, rows)
        put(spi, m, rows, mm(x, wqi[...]).astype(BF16), slice(0, n))
        put(spi, m, rows, mm(x, wkvi[0]).astype(BF16), slice(n, 2 * n))
        put(spi, m, rows, mm(x, wkvi[1]).astype(BF16), slice(2 * n, 3 * n))
        x = take(slots_t, m, rows)
        put(spt, m, rows, mm(x, wqt[...]).astype(BF16), slice(0, n))
        put(spt, m, rows, mm(x, wkvt[0]).astype(BF16), slice(n, 2 * n))
        put(spt, m, rows, mm(x, wkvt[1]).astype(BF16), slice(2 * n, 3 * n))
        for j in range(2):
            b = at.base(half) + j
            t, v = spt[m, b], spi[m, b]
            smt[m, b] = attn_fwd(t[:, 0:n], v[:, n : 2 * n], v[:, 2 * n :],
                                 key_mask(LT, RP, rc[2 * b + m]), heads, KC)
            smi[m, b] = attn_fwd(v[:, 0:n], t[:, n : 2 * n], t[:, 2 * n :],
                                 key_mask(RP, LT, tl[2 * b + m]), heads, KC)
        image.partial(half, m, mm(take(smi, m, rows), woi[...]))
        text.partial(half, m, mm(take(smt, m, rows), wot[...]))

    steps(text, image, slots_t, slots_i, co)
    finish(0)

    def feed(s, w):
        slots_t, slots_i, sat, spt, sai, spi = saved[s]
        wti, wto, wii, wio = w

        def compute(half, m, rows):
            act, slope = gelu_parts(mm(take(slots_i, m, rows), wii[...]))
            act = act.astype(BF16)
            put(sai, m, rows, act)
            put(spi, m, rows, slope.astype(BF16))
            image.partial(half, m, mm(act, wio[...]))
            act, slope = gelu_parts(mm(take(slots_t, m, rows), wti[...]))
            act = act.astype(BF16)
            put(sat, m, rows, act)
            put(spt, m, rows, slope.astype(BF16))
            text.partial(half, m, mm(act, wto[...]))

        steps(text, image, slots_t, slots_i, compute)

    for c in loading[6:]:
        c.wait()
    feed(1, cf_w)
    finish(1)

    slots_t, slots_i, sqt, sqi, sst, ssi = saved[2]
    wt, wto, wi, wio = sa_w
    km = wt.shape[1]
    ks = wide(km)
    hm = head_masks(LT, km, KT)

    def own(half, m, rows):
        x = take(slots_i, m, rows)
        for i in range(3):
            put(sqi, m, rows, mm(x, wi[i]).astype(BF16), slice(i * n, (i + 1) * n))
        x = take(slots_t, m, rows)
        for i in range(3):
            put(sqt, m, rows, mm_nt(x, wt[i]).astype(BF16), slice(i * ks, i * ks + km))
        for j in range(2):
            b = at.base(half) + j
            v = sqi[m, b]
            ssi[m, b] = attn_fwd(v[:, 0:n], v[:, n : 2 * n], v[:, 2 * n :],
                                 key_mask(RP, RP, rc[2 * b + m]), n // KV, KV)
            q, k, v = (sqt[m, b, :, i * ks : i * ks + km] for i in range(3))
            sst[m, b, :, 0:km] = attn_fwd_small(
                q, k, v, key_mask(LT, LT, tl[2 * b + m]), hm)
        image.partial(half, m, mm(take(ssi, m, rows), wio[...]))
        text.partial(half, m, mm(take(sst, m, rows)[:, 0:km], wto[...]))

    steps(text, image, slots_t, slots_i, own)
    finish(2)
    feed(3, sf_w)
    finish(3, True)
    for c in storing:
        c.wait()


def sds(shape, dtype=F32):
    return jax.ShapeDtypeStruct(shape, dtype)


def forward(tl, rc, xt, xi, weights, gains):
    n, m = weights[0].shape[1], weights[10].shape[1]
    f, fi = weights[6].shape[1], weights[8].shape[1]
    saved = saved_shapes(n, m, f, fi)
    flat = [s for group in saved for s in group]
    outs = (
        [sds((2, LT, DT), BF16), sds((2 * RG, DV), BF16)]
        + [sds(s, BF16) for s in flat]
        + [sds(s) for _ in range(4) for s in NORM_SAVED]
    )
    scratch = (
        [pltpu.VMEM(w.shape, BF16) for w in weights]
        + [pltpu.VMEM(s, BF16) for s in flat]
        + [pltpu.VMEM(s, F32) for _ in range(4) for s in NORM_SAVED]
        + [pltpu.VMEM((2, LT, DT), F32), pltpu.VMEM((2, RP, DV), F32)]
        + [pltpu.SemaphoreType.DMA((18,)), pltpu.SemaphoreType.DMA((48,))]
        + COMM
    )
    got = pl.pallas_call(
        fwd_kernel,
        out_shape=outs,
        in_specs=[SM] * 2 + [VM] * 2 + [ANY] * 18 + [VM] * 4,
        out_specs=[VM] * 2 + [ANY] * (sum(SAVED) + 16),
        scratch_shapes=scratch,
        compiler_params=pltpu.CompilerParams(
            collective_id=1, has_side_effects=True, vmem_limit_bytes=VMEM_LIMIT
        ),
        cost_estimate=pl.CostEstimate(flops=10**10, bytes_accessed=60 << 20, transcendentals=0),
        name="forward",
    )(tl, rc, xt, xi, *weights, *gains)
    got = list(got)
    kept = [[got.pop(2) for _ in range(k)] for k in SAVED]
    return got[0], got[1], kept, [got[2 + 4 * s : 6 + 4 * s] for s in range(4)]


def weight_grad(x, d, dw, dst, src=None):
    width = x.shape[3]
    blocks = width // 384 if width % 384 == 0 else width // 256
    cut = width // blocks
    per = 4 // blocks

    @pl.loop(0, blocks)
    def _(j):
        left = x[:, :, :, pl.ds(pl.multiple_of(j * cut, 128), cut)]
        left = left.reshape(-1, cut)
        right = d[...] if src is None else d[:, :, :, src]
        right = right.reshape(left.shape[0], right.shape[-1])
        got = mm_tn(left, right).astype(BF16)
        dw[pl.ds(j * per, per), :, :, dst] = got.reshape(per, 2, width // 8, got.shape[1])


class Depth:
    def __init__(self):
        self.p = lax.axis_index("dp")
        self.z, self.y = lax.div(self.p, 2), lax.rem(self.p, 2)
        self.y_mate = 2 * self.z + 1 - self.y

    def greet(self, at):
        barrier = pltpu.get_barrier_semaphore()

        def hello(who):
            pl.semaphore_signal(barrier, inc=1, device_id=who, device_id_type=MESH)

        hello({"tensor": at.core_mate})
        hello({"tensor": at.chip_mate})
        hello({"dp": self.y_mate})
        hello({"dp": lax.rem(self.p + 4, 8)})
        pl.when(self.z < 3)(lambda: hello({"dp": self.p + 2}))
        pl.when(self.z > 0)(lambda: hello({"dp": self.p - 2}))
        pl.semaphore_wait(barrier, 4 + (self.z + 2) // 3 + (5 - self.z) // 3)


def add_rows(dst, src):
    @pl.loop(0, dst.shape[0] // 16)
    def _(i):
        r = pl.ds(pl.multiple_of(i * 16, 16), 16)
        dst[r, :] = (dst[r, :].astype(F32) + src[r, :].astype(F32)).astype(BF16)


class Unit:
    def __init__(self, depth, index, dw, cols, from_y, from_z, z_first, waits, frees, sems, out, osem):
        self.d, self.k, self.dw, self.cols = depth, index, dw, cols
        self.from_y, self.from_z, self.z_first = from_y, from_z, z_first
        self.waits, self.frees = waits, frees
        self.ysem, self.zsem, self.ycredit, self.zcredit = sems
        self.out, self.osem = out, osem

    def mine(self, t, y):
        return self.dw.at[t, y, :, self.cols]

    def y_copy(self):
        d = self.d
        src = self.mine(d.z, 1 - d.y) if self.z_first else self.dw.at[:, 1 - d.y, :, self.cols]
        return pltpu.make_async_remote_copy(
            src_ref=src,
            dst_ref=self.from_y,
            send_sem=self.ysem.at[0, self.k],
            recv_sem=self.ysem.at[1, self.k],
            device_id={"dp": d.y_mate},
            device_id_type=MESH,
        )

    def z_copy(self, flow, step, t, to):
        src = self.dw.at[t, :, :, self.cols] if self.z_first else self.mine(t, self.d.y)
        return pltpu.make_async_remote_copy(
            src_ref=src,
            dst_ref=self.from_z.at[flow, step],
            send_sem=self.zsem.at[0, self.k, flow, step],
            recv_sem=self.zsem.at[1, self.k, flow, step],
            device_id={"dp": to},
            device_id_type=MESH,
        )

    def send(self, step):
        d = self.d
        w = 3 - d.z
        if step == 0 and self.waits:
            pl.semaphore_wait(self.zcredit.at[self.k], (d.z + 2) // 3 + (5 - d.z) // 3)
        pl.when(d.z <= step)(lambda: self.z_copy(0, step, 3 - step + d.z, d.p + 2).start())
        pl.when(w <= step)(lambda: self.z_copy(1, step, step - w, d.p - 2).start())

    def receive(self, step):
        d = self.d
        w = 3 - d.z

        def add(t, got):
            if self.z_first:
                for y in range(2):
                    add_rows(self.mine(t, y), got.at[y])
            else:
                add_rows(self.mine(t, d.y), got)

        def right():
            t = 2 - step + d.z
            self.z_copy(0, step, t, d.p).wait_recv()
            add(t, self.from_z.at[0, step])

        def left():
            t = 1 + step - w
            self.z_copy(1, step, t, d.p).wait_recv()
            add(t, self.from_z.at[1, step])

        pl.when((d.z >= 1) & (d.z - 1 <= step))(right)
        pl.when((w >= 1) & (w - 1 <= step))(left)
        if step == 2 and self.frees is not None:

            def free(to):
                pl.semaphore_signal(
                    self.zcredit.at[self.frees], inc=1, device_id={"dp": to}, device_id_type=MESH
                )

            pl.when(d.z < 3)(lambda: free(d.p + 2))
            pl.when(d.z > 0)(lambda: free(d.p - 2))

    def take_y(self):
        d = self.d
        self.y_copy().wait_recv()
        if self.z_first:
            add_rows(self.mine(d.z, d.y), self.from_y)
            return

        @pl.loop(0, 4)
        def _(t):
            add_rows(self.mine(t, d.y), self.from_y.at[t])

        if self.frees is not None and not self.z_first:
            pl.semaphore_signal(
                self.ycredit.at[self.frees], inc=1, device_id={"dp": d.y_mate}, device_id_type=MESH
            )

    def give_y(self):
        if self.waits == "both":
            pl.semaphore_wait(self.ycredit.at[self.k], 1)
        self.y_copy().start()

    def task(self, name):
        if name == "start":
            if self.z_first:
                self.send(0)
            else:
                self.give_y()
        elif name == "S":
            self.take_y()
            self.send(0)
        elif name in ("r0", "r1"):
            self.receive(int(name[1]))
            self.send(int(name[1]) + 1)
        elif name == "r2":
            self.receive(2)
            self.give_y()
        else:
            if self.z_first:
                self.take_y()
            else:
                self.receive(2)
            self.copy_out().start()

    def copy_out(self):
        return pltpu.make_async_copy(self.mine(self.d.z, self.d.y), self.out, self.osem.at[self.k])

    def end(self):
        d = self.d
        w = 3 - d.z
        self.copy_out().wait()
        self.y_copy().wait_send()
        for step in range(3):
            pl.when(d.z <= step)(self.z_copy(0, step, 0, d.p).wait_send)
            pl.when(w <= step)(self.z_copy(1, step, 0, d.p).wait_send)


UNITS = ["sf1", "sf2", "sfi", "sa1", "sai", "cf1", "cf2", "cfi", "coi", "co1"]

PLAN = [
    ("0e", "sf1 start", "sf2 start", "sfi start"),
    ("1d", "sf1 S"),
    ("1e", "sa1 start", "sai start"),
    ("2a", "sf1 r0", "sf2 S"),
    ("2c", "sfi S", "sai r0", "sf1 r1"),
    ("2e", "cf2 start", "sf2 r0", "sfi r0", "cf1 start", "cfi start", "sa1 S"),
    ("3a", "n 0"), ("3b", "n 1"),
    ("3c", "n 2", "sf1 F", "sf2 r1", "sai r1"),
    ("3d", "n 3", "sfi r1"),
    ("3e", "n 4", "coi start", "sa1 r0", "co1 start", "sf2 F", "cf2 S"),
    ("t", "n 5", "cf1 S", "cf2 r0", "sa1 r1", "sfi F", "cf1 r0", "cf2 r1", "sa1 F", "cfi S", "cf1 r1", "sai r2",
     "coi S", "cfi r0", "cf2 F", "cf1 F", "coi r0", "co1 S", "coi r1", "co1 r0", "sai F", "cfi r1", "coi F",
     "co1 r1", "cfi F", "co1 F"),
]


class NormSum:
    def __init__(self, at, depth, text, image, got_t, got_i, sems):
        p, z, y = depth.p, depth.z, depth.y
        self.text, self.image, self.got_t, self.got_i, self.sems = text, image, got_t, got_i, sems
        self.to = [
            {"tensor": at.core_mate},
            {"tensor": at.chip_mate},
            {"dp": depth.y_mate},
            {"dp": 2 * (z + 1 - 2 * lax.rem(z, 2)) + y},
            {"dp": lax.rem(p + 4, 8)},
        ]

    def copies(self, k):
        return [
            pltpu.make_async_remote_copy(
                src_ref=src.at[k],
                dst_ref=dst.at[k],
                send_sem=self.sems.at[0, i, k],
                recv_sem=self.sems.at[1, i, k],
                device_id=self.to[k],
                device_id_type=MESH,
            )
            for i, (src, dst) in enumerate(((self.text, self.got_t), (self.image, self.got_i)))
        ]

    def task(self, k):
        if k > 0:
            for c in self.copies(k - 1):
                c.wait_recv()
            self.text[k] = self.text[k - 1] + self.got_t[k - 1]
            self.image[k] = self.image[k - 1] + self.got_i[k - 1]
        if k < 5:
            for c in self.copies(k):
                c.start()

    def end(self):
        for k in range(5):
            for c in self.copies(k):
                c.wait_send()


def bwd_kernel(fast, *refs):
    refs = list(refs)

    def grab(count):
        got = refs[:count]
        del refs[:count]
        return got

    tl, rc, dt, di = grab(4)
    tg, ig = grab(2)
    weights = grab(18)
    saved_in = [grab(k) for k in SAVED]
    norm_in = [grab(4) for _ in range(4)]
    ot, oi, gbt, gbi = grab(4)
    grads_out = grab(len(UNITS)) if fast else [grab(2) for _ in range(4)]
    vff, vsa, vco = grab(4), grab(4), grab(6)
    feed_saved, att_saved = grab(4), grab(4)
    vxt, vxi = grab(2)
    xht, xhi, rst, rsi = grab(4)
    slots = [grab(2), grab(2)]
    dpt, dpi, dui = grab(3)
    dut = dpt
    kt, ki = grab(2)
    dw = [grab(2) for _ in range(4)]
    lsem, osem = grab(2)
    at = Places()
    co_w, cf_w, sa_w, sf_w = weight_groups(weights)
    if fast:
        depth = Depth()
        buffers = grab(11)
        y0, z0, y1, z1 = buffers[0:3], buffers[3:6], buffers[6:8], buffers[8:10]
        sums = grab(4)
        nt, ni, got_nt, got_ni, nsem = grab(5)
        nsum = NormSum(at, depth, nt, ni, got_nt, got_ni, nsem)

        def made(name, s, i, cols, from_y, from_z, z_first=False, waits=None, frees=None):
            k = UNITS.index(name)
            units[name] = Unit(depth, k, dw[s][i], cols, from_y, from_z, z_first, waits,
                               None if frees is None else UNITS.index(frees), sums, grads_out[k], osem)

        units = {}
        ff = dw[3][0].shape[3] // 2
        wide_t = {s: dw[s][0].shape[3] for s in (0, 2)}
        for pre, s, waits in (("sf", 3, None), ("cf", 1, "both")):
            frees = [None] * 3 if waits else ["cf1", "cf2", "cfi"]
            made(pre + "1", s, 0, pl.ds(0, ff), y0[0], z0[0], False, waits, frees[0])
            made(pre + "2", s, 0, pl.ds(ff, ff), y0[1], z0[1], False, waits, frees[1])
            made(pre + "i", s, 1, pl.ds(0, dw[s][1].shape[3]), y0[2], z0[2], False, waits, frees[2])
        cols = pl.ds(0, wide_t[2])
        made("sa1", 2, 0, cols, y1[0].at[:, :, cols], z1[0].at[:, :, :, cols], frees="co1")
        cols = pl.ds(0, dw[2][1].shape[3])
        made("sai", 2, 1, cols, buffers[10], z1[1], True, frees="coi")
        made("coi", 0, 1, cols, y1[1], z1[1].at[:, :, 0], waits="z")
        made("co1", 0, 0, pl.ds(0, wide_t[0]), y1[0], z1[0], waits="both")

    def place(where):
        def go():
            for entry in PLAN:
                if entry[0] == where:
                    for name, task in (x.split() for x in entry[1:]):
                        if name == "n":
                            nsum.task(int(task))
                        else:
                            units[name].task(task)

        return go if fast else (lambda: None)

    def places(cycle):
        named = {entry[0] for entry in PLAN} if fast else ()
        return [place(cycle + x) if cycle + x in named else None for x in ("a", "b", "f", "c")]

    count = [0]

    def load(pairs):
        copies = local_copies(pairs, lsem, count[0])
        count[0] += len(pairs)
        return copies

    def done(copies):
        for c in copies:
            c.wait()

    vnorm = [xht, xhi, rst, rsi]
    norm_load = load(list(zip(norm_in[3], vnorm)))
    feed_load = load(list(zip(sf_w, vff)) + list(zip(saved_in[3][2:], feed_saved)))
    x_load = load(list(zip(saved_in[3][:2], (vxt, vxi))))
    sa_load = load(list(zip(sa_w, vsa)) + list(zip(saved_in[2][2:], att_saved)))
    co_load = load(list(zip(co_w, vco)))
    text, image = make_streams(at, refs)
    image.clear([pair[1] for pair in slots])
    if fast:
        depth.greet(at)
        acc_t, acc_i = nt.at[0], ni.at[0]
    else:
        greet(at)
        acc_t, acc_i = gbt, gbi
    acc_t[...] = jnp.zeros_like(acc_t)
    acc_i[...] = jnp.zeros_like(acc_i)

    def enter(s, m, gi, gt, slots_t, slots_i):
        dx, dg, db = norm_back(gi, xhi[m], rsi[m], ig[s : s + 1, :])
        ki[m] = dx
        image.begin(slots_i, m, dx.astype(BF16))
        acc_i[s : s + 1, :] += dg
        acc_i[4 + s : 5 + s, :] += db
        dx, dg, db = norm_back(gt, xht[m], rst[m], tg[s : s + 1, :])
        kt[m] = dx
        text.begin(slots_t, m, dx.astype(BF16))
        acc_t[s : s + 1, :] += dg
        acc_t[4 + s : 5 + s, :] += db

    done(norm_load)
    split_rows(di, ki)

    @pl.loop(0, 2)
    def _(m):
        enter(3, m, ki[m], dt[m].astype(F32), *slots[0])

    norm_load = load(list(zip(norm_in[2], vnorm)))

    def finish(s, norm_load):
        if s > 0:
            done(norm_load)
        slots_t, slots_i = slots[(3 - s) % 2]

        @pl.loop(0, 2)
        def _(m):
            gi = ki[m] + image.total(m)
            image.end(slots_i, m)
            gt = kt[m] + text.total(m)
            text.end(slots_t, m)
            if s == 0:
                ki[m] = gi
                ot[m] = gt.astype(BF16)
            else:
                enter(s - 1, m, gi, gt, *slots[(4 - s) % 2])

        if s == 0:
            join_rows(ki, oi)
        if s > 1:
            return load(list(zip(norm_in[s - 2], vnorm)))
        return None

    storing = []

    def feed(s, feed_load, x_load, cycle):
        wti, wto, wii, wio = vff
        sat, spt, sai, spi = feed_saved
        slots_t, slots_i = slots[(3 - s) % 2]
        done(feed_load)

        def compute(half, m, rows):
            du = (mm_nt(take(slots_i, m, rows), wio[...]) * take(spi, m, rows).astype(F32)).astype(BF16)
            put(dui, m, rows, du)
            image.partial(half, m, mm_nt(du, wii[...]))
            du = (mm_nt(take(slots_t, m, rows), wto[...]) * take(spt, m, rows).astype(F32)).astype(BF16)
            put(dut, m, rows, du)
            text.partial(half, m, mm_nt(du, wti[...]))

        steps(text, image, slots_t, slots_i, compute, places(cycle))
        done(x_load)
        place(cycle + "d")()
        dwt, dwi = dw[s]
        f, fi = wti.shape[1], wii.shape[1]
        weight_grad(vxt, dut, dwt, slice(0, f))
        weight_grad(slots_t, sat, dwt, slice(f, 2 * f))
        weight_grad(vxi, dui, dwi, slice(0, fi))
        weight_grad(slots_i, sai, dwi, slice(fi, 2 * fi))

    def send_grads(s):
        if not fast:
            storing.extend(local_copies(list(zip(dw[s], grads_out[s])), osem, 2 * s))

    feed(3, feed_load, x_load, "0")
    send_grads(3)
    place("0e")()
    x_load = load(list(zip(saved_in[2][:2], (vxt, vxi))))
    feed_load = load(list(zip(cf_w, vff)) + list(zip(saved_in[1][2:], feed_saved)))
    norm_load = finish(3, norm_load)

    wt, wto, wi, wio = vsa
    sqt, sqi, sst, ssi = att_saved
    n, km = wi.shape[2], wt.shape[1]
    ks = wide(km)
    hm = head_masks(LT, km, KT)
    own_t, own_i = slots[1]
    done(sa_load)

    def own(half, m, rows):
        dm = mm_nt(take(own_i, m, rows), wio[...]).astype(BF16)
        dmt = mm_nt(take(own_t, m, rows), wto[...]).astype(BF16)
        for j in range(2):
            b = at.base(half) + j
            v = sqi[m, b]
            grads = attn_bwd(v[:, 0:n], v[:, n : 2 * n], v[:, 2 * n :], dm[j * RP : (j + 1) * RP],
                             key_mask(RP, RP, rc[2 * b + m]), n // KV, KV)
            for i, g in enumerate(grads):
                dpi[m, b, :, i * n : (i + 1) * n] = g
            q, k, v = (sqt[m, b, :, i * ks : i * ks + km] for i in range(3))
            grads = attn_bwd_small(q, k, v, dmt[j * LT : (j + 1) * LT],
                                   key_mask(LT, LT, tl[2 * b + m]), hm)
            for i, g in enumerate(grads):
                dpt[m, b, :, i * ks : i * ks + km] = g
        dp = take(dpi, m, rows)
        image.partial(half, m, sum(mm_nt(dp[:, i * n : (i + 1) * n], wi[i]) for i in range(3)))
        dp = take(dpt, m, rows)
        text.partial(half, m, sum(mm(dp[:, i * ks : i * ks + km], wt[i]) for i in range(3)))

    steps(text, image, own_t, own_i, own, places("1"))
    done(x_load)
    place("1d")()
    dwt, dwi = dw[2]
    for i in range(3):
        weight_grad(vxt, dpt, dwt, slice(i * km, (i + 1) * km), slice(i * ks, i * ks + km))
    weight_grad(own_t, sst, dwt, slice(3 * km, 4 * km), slice(0, km))
    weight_grad(vxi, dpi, dwi, slice(0, 3 * n))
    weight_grad(own_i, ssi, dwi, slice(3 * n, 4 * n))
    send_grads(2)
    place("1e")()
    x_load = load(list(zip(saved_in[1][:2], (vxt, vxi))))
    co_load += load(list(zip(saved_in[0][2:], att_saved)))
    norm_load = finish(2, norm_load)

    feed(1, feed_load, x_load, "2")
    send_grads(1)
    place("2e")()
    x_load = load(list(zip(saved_in[0][:2], (vxt, vxi))))
    finish(1, norm_load)

    wqt, wkvi, wot, wqi, wkvt, woi = vco
    heads = n // KC
    co_t, co_i = slots[1]
    done(co_load)

    def co(half, m, rows):
        dm = mm_nt(take(co_i, m, rows), woi[...]).astype(BF16)
        dmt = mm_nt(take(co_t, m, rows), wot[...]).astype(BF16)
        for j in range(2):
            b = at.base(half) + j
            t, v = sqt[m, b], sqi[m, b]
            dq, dk, dv = attn_bwd(v[:, 0:n], t[:, n : 2 * n], t[:, 2 * n :], dm[j * RP : (j + 1) * RP],
                                  key_mask(RP, LT, tl[2 * b + m]), heads, KC)
            dpi[m, b, :, 0:n] = dq
            dpt[m, b, :, n : 2 * n] = dk
            dpt[m, b, :, 2 * n :] = dv
            dq, dk, dv = attn_bwd(t[:, 0:n], v[:, n : 2 * n], v[:, 2 * n :], dmt[j * LT : (j + 1) * LT],
                                  key_mask(LT, RP, rc[2 * b + m]), heads, KC)
            dpt[m, b, :, 0:n] = dq
            dpi[m, b, :, n : 2 * n] = dk
            dpi[m, b, :, 2 * n :] = dv
        dp = take(dpi, m, rows)
        image.partial(half, m, mm_nt(dp[:, 0:n], wqi[...]) + mm_nt(dp[:, n : 2 * n], wkvi[0])
                      + mm_nt(dp[:, 2 * n :], wkvi[1]))
        dp = take(dpt, m, rows)
        text.partial(half, m, mm_nt(dp[:, 0:n], wqt[...]) + mm_nt(dp[:, n : 2 * n], wkvt[0])
                     + mm_nt(dp[:, 2 * n :], wkvt[1]))

    steps(text, image, co_t, co_i, co, places("3"))
    done(x_load)
    place("3d")()
    dwt, dwi = dw[0]
    weight_grad(vxt, dpt, dwt, slice(0, 3 * n))
    weight_grad(co_t, sst, dwt, slice(3 * n, 4 * n))
    weight_grad(vxi, dpi, dwi, slice(0, 3 * n))
    weight_grad(co_i, ssi, dwi, slice(3 * n, 4 * n))
    send_grads(0)
    place("3e")()
    finish(0, None)
    place("t")()
    if fast:
        gbt[...] = nt[5]
        gbi[...] = ni[5]
        nsum.end()
        for unit in units.values():
            unit.end()
    done(storing)


def backward(fast, tl, rc, dt, di, weights, gains, saved, norms):
    n, m = weights[0].shape[1], weights[10].shape[1]
    f, fi = weights[6].shape[1], weights[8].shape[1]
    tg, _, ig, _ = gains
    co_w, cf_w, sa_w, sf_w = weight_groups(list(weights))
    text_cols = (4 * n, 2 * f, 4 * m, 2 * f)
    image_cols = (4 * n, 2 * fi, 4 * n, 2 * fi)
    rt, ri = DT // 8, DV // 8
    dw_shapes = [s for i in range(4) for s in ((4, 2, rt, text_cols[i]), (4, 2, ri, image_cols[i]))]
    text, image = (2, 4, LT, DT), (2, 4, RP, DV)
    outs = [sds((2, LT, DT), BF16), sds((2 * RG, DV), BF16), sds((8, DT)), sds((8, DV))]
    blocks = {
        "sf1": (rt, f), "sf2": (rt, f), "sfi": (ri, 2 * fi), "sa1": (rt, 4 * m), "sai": (ri, 4 * n),
        "cf1": (rt, f), "cf2": (rt, f), "cfi": (ri, 2 * fi), "coi": (ri, 4 * n), "co1": (rt, 4 * n),
    }
    outs += [sds(blocks[u], BF16) for u in UNITS] if fast else [sds(s, BF16) for s in dw_shapes]
    sums = []
    if fast:
        tc = max(4 * n, 4 * m)
        shapes = [
            (4, rt, f), (4, rt, f), (4, ri, 2 * fi), (2, 3, rt, f), (2, 3, rt, f), (2, 3, ri, 2 * fi),
            (4, rt, tc), (4, ri, 4 * n), (2, 3, rt, tc), (2, 3, 2, ri, 4 * n), (ri, 4 * n),
        ]
        k = len(UNITS)
        sums = (
            [pltpu.VMEM(s, BF16) for s in shapes]
            + [pltpu.SemaphoreType.DMA((2, k)), pltpu.SemaphoreType.DMA((2, k, 2, 3)),
               pltpu.SemaphoreType.REGULAR((k,)), pltpu.SemaphoreType.REGULAR((k,))]
            + [pltpu.VMEM((6, 8, w), F32) for w in (DT, DV)]
            + [pltpu.VMEM((5, 8, w), F32) for w in (DT, DV)]
            + [pltpu.SemaphoreType.DMA((2, 2, 5))]
        )
    buffers = (
        [w.shape for w in cf_w] + [w.shape for w in sa_w] + [w.shape for w in co_w]
        + [x.shape for x in saved[1][2:]] + [x.shape for x in saved[0][2:]]
        + [text, image]
    )
    scratch = (
        [pltpu.VMEM(s, BF16) for s in buffers]
        + [pltpu.VMEM(s, F32) for s in NORM_SAVED]
        + [pltpu.VMEM(s, BF16) for s in (text, image, text, image)]
        + [pltpu.VMEM(s, BF16) for s in ((2, 4, LT, 3 * n), (2, 4, RP, 3 * n), (2, 4, RP, fi))]
        + [pltpu.VMEM((2, LT, DT), F32), pltpu.VMEM((2, RP, DV), F32)]
        + [pltpu.VMEM(s, BF16) for s in dw_shapes]
        + [pltpu.SemaphoreType.DMA((72,)), pltpu.SemaphoreType.DMA((40,))]
        + sums
        + COMM
    )
    got = pl.pallas_call(
        functools.partial(bwd_kernel, fast),
        out_shape=outs,
        in_specs=[SM] * 2 + [VM] * 4 + [ANY] * (18 + sum(SAVED) + 16),
        out_specs=[VM] * 4 + [ANY] * (len(outs) - 4),
        scratch_shapes=scratch,
        compiler_params=pltpu.CompilerParams(
            collective_id=2, has_side_effects=True, vmem_limit_bytes=VMEM_LIMIT
        ),
        cost_estimate=pl.CostEstimate(flops=2 * 10**10, bytes_accessed=60 << 20, transcendentals=0),
        name="backward",
    )(tl, rc, dt, di, tg, ig, *weights, *[x for g in saved for x in g], *[x for g in norms for x in g])
    return got[0:4], got[4:]


def last_kernel(yt, yi, gt, gi, nt, ni, *refs):
    block = dict(zip(UNITS, refs))
    outs = list(refs[len(UNITS) :])

    def out():
        return outs.pop(0)

    for x in (yt, yi, gt, gi):
        out()[...] = x[...]
    rt, ri = block["co1"].shape[0], block["coi"].shape[0]
    n, m = block["coi"].shape[1] // 4, block["sa1"].shape[1] // 4

    def part(name, i, size):
        return block[name][:, i * size : (i + 1) * size].astype(F32)

    def one(name, i, size, turn=False):
        value = part(name, i, size)
        out()[...] = value.T if turn else value

    def stack(name, first, count, size):
        ref = out()
        for i in range(count):
            ref[i] = part(name, first + i, size)

    one("co1", 0, n)
    stack("coi", 1, 2, n)
    one("co1", 3, n)
    one("coi", 0, n)
    stack("co1", 1, 2, n)
    one("coi", 3, n, True)
    one("cf1", 0, block["cf1"].shape[1])
    one("cf2", 0, block["cf2"].shape[1])
    one("cfi", 0, n)
    one("cfi", 1, n, True)
    stack("sa1", 0, 3, m)
    one("sa1", 3, m, True)
    one("sf1", 0, block["sf1"].shape[1])
    one("sf2", 0, block["sf2"].shape[1])
    stack("sai", 0, 3, n)
    one("sai", 3, n, True)
    one("sfi", 0, n)
    one("sfi", 1, n, True)
    for x in (nt, ni):
        out()[...] = x[0:4]
        out()[...] = x[4:8]


def last(yt, yi, gt, gi, nt, ni, blocks):
    shape = {u: b.shape for u, b in zip(UNITS, blocks)}
    rt, ri = shape["co1"][0], shape["coi"][0]
    n, m, f = shape["coi"][1] // 4, shape["sa1"][1] // 4, shape["sf1"][1]
    final = [
        (rt, n), (2, ri, n), (rt, n), (ri, n), (2, rt, n), (n, ri),
        (rt, f), (rt, f), (ri, n), (n, ri),
        (3, rt, m), (m, rt), (rt, f), (rt, f), (3, ri, n), (n, ri), (ri, n), (n, ri),
        (4, DT), (4, DT), (4, DV), (4, DV),
    ]
    outs = [sds(x.shape, BF16) for x in (yt, yi, gt, gi)] + [sds(s) for s in final]
    return pl.pallas_call(
        last_kernel,
        out_shape=outs,
        in_specs=[VM] * (6 + len(blocks)),
        out_specs=[VM] * len(outs),
        compiler_params=pltpu.CompilerParams(vmem_limit_bytes=VMEM_LIMIT),
        name="last",
    )(yt, yi, gt, gi, nt, ni, *blocks)


def local(dp, text_in, image_in, tl, rc, *rest):
    weights, gains, (text_cot, image_cot) = list(rest[:18]), rest[18:22], rest[22:]
    n, m, f = weights[0].shape[1], weights[10].shape[2], weights[6].shape[1]
    weights[10] = jnp.swapaxes(weights[10], 1, 2)
    rows, fast = (2, LT, DT), dp == 8
    yt, yi, saved, norms = forward(tl, rc, text_in.reshape(rows), image_in, weights, gains)
    (gt, gi, tgb, igb), grads = backward(
        fast, tl, rc, text_cot.reshape(rows), image_cot, weights, gains, saved, norms
    )
    if fast:
        yt, yi, gt, gi, *rest = last(yt, yi, gt, gi, tgb, igb, grads)
        grads, norm_grads = rest[:18], rest[18:]
        grads = [g.T if i in (2, 7, 13) else g for i, g in enumerate(grads)]
    else:
        tgb, igb = lax.psum((tgb, igb), ("dp", "tensor"))
        parts = []
        for g in grads:
            g = g.reshape(-1, g.shape[3])
            parts.append(lax.psum_scatter(g, "dp", scatter_dimension=0, tiled=True).astype(F32))
        ct, ci, ft, fi, st, si, ht, hi = parts
        grads = [
            ct[:, :n],
            jnp.stack([ci[:, n : 2 * n], ci[:, 2 * n : 3 * n]]),
            ct[:, 3 * n :].T,
            ci[:, :n],
            jnp.stack([ct[:, n : 2 * n], ct[:, 2 * n : 3 * n]]),
            ci[:, 3 * n :].T,
            ft[:, :f], ft[:, f:].T, fi[:, :n], fi[:, n:].T,
            jnp.stack([st[:, i * m : (i + 1) * m] for i in range(3)]),
            st[:, 3 * m :].T,
            ht[:, :f], ht[:, f:].T,
            jnp.stack([si[:, i * n : (i + 1) * n] for i in range(3)]),
            si[:, 3 * n :].T,
            hi[:, :n], hi[:, n:].T,
        ]
        norm_grads = tgb[0:4], tgb[4:8], igb[0:4], igb[4:8]
    return (
        yt.reshape(2 * LT, DT), yi, gt.reshape(2 * LT, DT), gi, *grads,
        *norm_grads,
    )


def solution(mesh):
    rows, pairs = P(("dp", "tensor"), None), P("dp")
    wide, tall, stack = P(None, "tensor"), P("tensor", None), P(None, None, "tensor")
    g_wide, g_tall, g_stack = P("dp", "tensor"), P("tensor", "dp"), P(None, "dp", "tensor")
    return jax.shard_map(
        functools.partial(local, mesh.shape["dp"]),
        mesh=mesh,
        in_specs=(
            rows, rows, pairs, pairs,
            wide, stack, tall, wide, stack, tall,
            wide, tall, wide, tall,
            stack, tall, wide, tall,
            stack, tall, wide, tall,
            P(), P(), P(), P(),
            rows, rows,
        ),
        out_specs=(
            rows, rows, rows, rows,
            g_wide, g_stack, g_tall, g_wide, g_stack, g_tall,
            g_wide, g_tall, g_wide, g_tall,
            g_stack, g_tall, g_wide, g_tall,
            g_stack, g_tall, g_wide, g_tall,
            P(), P(), P(), P(),
        ),
        check_vma=False,
    )
```

```python
import functools
import math

import jax
import jax.numpy as jnp
from jax import lax
from jax.experimental import pallas as pl
from jax.experimental.pallas import tpu as pltpu
from jax.sharding import PartitionSpec as P

KT = 64
KV = 128
KC = 128
LT = 128
RG = 36
RP = 48
RS = 40
VMEM_LIMIT = 63 << 20
DT = 768
DV = 1024

epsilon = 1e-05
masked_score = -1e30
F32 = jnp.float32
BF16 = jnp.bfloat16
MESH = pl.DeviceIdType.MESH
VM = pl.BlockSpec(memory_space=pltpu.VMEM)
SM = pl.BlockSpec(memory_space=pltpu.SMEM)
ANY = pl.BlockSpec(memory_space=pl.ANY)


def mm(a, b):
    return lax.dot_general(a, b, (((1,), (0,)), ((), ())), preferred_element_type=F32)


def mm_nt(a, b):
    return lax.dot_general(a, b, (((1,), (1,)), ((), ())), preferred_element_type=F32)


def mm_tn(a, b):
    return lax.dot_general(a, b, (((0,), (0,)), ((), ())), preferred_element_type=F32)


class Places:
    def __init__(self):
        me = lax.axis_index("tensor")
        chip, core = lax.div(me, 2), lax.rem(me, 2)
        self.me, self.chip, self.core = me, chip, core
        self.core_mate = 2 * chip + (1 - core)
        self.chip_mate = 2 * (1 - chip) + core

    def base(self, half):
        return 2 * (self.chip + half - 2 * self.chip * half)


class Stream:
    def __init__(self, at, stream, part, near, relay, out, got_near, got_far, got_chip, sends, recvs):
        self.at, self.stream, self.part = at, stream, part
        self.sent = pl.ds(0, RS if stream else LT)
        self.near, self.relay, self.out = near, relay, out
        self.got_near, self.got_far, self.got_chip = got_near, got_far, got_chip
        self.sends, self.recvs = sends, recvs

    def push(self, src, dst, m, slot, mate):
        return pltpu.make_async_remote_copy(
            src_ref=src,
            dst_ref=dst,
            send_sem=self.sends.at[self.stream, m, slot],
            recv_sem=self.recvs.at[self.stream, m, slot],
            device_id={"tensor": mate},
            device_id_type=MESH,
        )

    def copy(self, slots, m, which):
        at = self.at
        me, cm, xm, r = at.me, at.core_mate, at.chip_mate, self.sent
        if which == 0:
            return self.push(slots.at[m, me, r], slots.at[m, me, r], m, 0, cm)
        if which == 1:
            return self.push(slots.at[m, me, r], slots.at[m, me, r], m, 1, xm)
        if which == 2:
            return self.push(slots.at[m, xm, r], slots.at[m, xm, r], m, 2, cm)
        if which == 3:
            return self.push(self.near.at[m, r], self.got_near.at[m, r], m, 3, cm)
        if which == 4:
            return self.push(self.relay.at[m, r], self.got_far.at[m, r], m, 4, cm)
        return self.push(self.out.at[m, r], self.got_chip.at[m, r], m, 5, xm)

    def clear(self, slot_sets):
        for got in (self.got_near, self.got_far, self.got_chip):
            got[:, RS:, :] = jnp.zeros((2, RP - RS, got.shape[2]), BF16)
        for slots in slot_sets:
            slots[:, :, RS:, :] = jnp.zeros((2, 4, RP - RS, slots.shape[3]), BF16)

    def begin(self, slots, m, rows):
        slots[m, self.at.me] = rows
        self.copy(slots, m, 1).start()
        self.copy(slots, m, 0).start()

    def relay_gather(self, slots, m):
        self.copy(slots, m, 1).wait_recv()
        self.copy(slots, m, 2).start()

    def partial(self, half, m, value):
        part, other = self.part, 1 - self.at.core
        value = value.reshape(part.shape[1:])

        @pl.when(half == 0)
        def _():
            part[m] = value
            self.near[m] = part[m, other].astype(BF16)
            self.copy(None, m, 3).start()

        @pl.when(half == 1)
        def _():
            part[2] = value
            self.relay[m] = part[2, other].astype(BF16)
            self.copy(None, m, 4).start()

    def forward(self, m):
        self.copy(None, m, 4).wait_recv()
        self.out[m] = (self.part[2, self.at.core] + self.got_far[m].astype(F32)).astype(BF16)
        self.copy(None, m, 5).start()

    def total(self, m):
        self.copy(None, m, 3).wait_recv()
        self.copy(None, m, 5).wait_recv()
        return self.part[m, self.at.core] + self.got_near[m].astype(F32) + self.got_chip[m].astype(F32)

    def end(self, slots, m):
        for which in range(6):
            self.copy(slots, m, which).wait_send()


def stream_scratch(rows, width):
    return [pltpu.VMEM((3, 2, rows, width), F32)] + [pltpu.VMEM((2, rows, width), BF16)] * 6


COMM = stream_scratch(LT, DT) + stream_scratch(RP, DV) + [pltpu.SemaphoreType.DMA((2, 2, 6))] * 2


def make_streams(at, refs):
    text = Stream(at, 0, *refs[0:7], refs[14], refs[15])
    image = Stream(at, 1, *refs[7:14], refs[14], refs[15])
    return text, image


def greet(at):
    barrier = pltpu.get_barrier_semaphore()
    for mate in (at.core_mate, at.chip_mate):
        pl.semaphore_signal(barrier, inc=1, device_id={"tensor": mate}, device_id_type=MESH)
    pl.semaphore_wait(barrier, 2)


def steps(text, image, tslots, islots, compute, between=()):
    @pl.loop(0, 4)
    def _(i):
        half, m = lax.div(i, 2), lax.rem(i, 2)
        for place, task in enumerate(between):
            if task is not None:
                pl.when(i == place)(task)

        @pl.when(half == 0)
        def _():
            image.copy(islots, m, 0).wait_recv()
            text.copy(tslots, m, 0).wait_recv()

        @pl.when(half == 1)
        def _():
            image.relay_gather(islots, m)
            text.relay_gather(tslots, m)
            image.copy(islots, m, 2).wait_recv()
            text.copy(tslots, m, 2).wait_recv()

        compute(half, m, pl.ds(text.at.base(half), 2))

        @pl.when(half == 1)
        def _():
            image.forward(m)
            text.forward(m)


def norm(pre, gain, bias, xh_ref, rs_ref, m):
    mean = jnp.mean(pre, axis=-1, keepdims=True)
    centered = pre - mean
    variance = jnp.mean(centered * centered, axis=-1, keepdims=True)
    rs = lax.rsqrt(variance + epsilon)
    xh = centered * rs
    xh_ref[m] = xh
    rs_ref[m] = jnp.broadcast_to(rs, rs_ref.shape[1:])
    return xh * gain + bias


def norm_back(grad, xh, rs, gain):
    dz = grad * gain
    dg = jnp.sum(grad * xh, axis=0, keepdims=True)
    db = jnp.sum(grad, axis=0, keepdims=True)
    m1 = jnp.mean(dz, axis=-1, keepdims=True)
    m2 = jnp.mean(dz * xh, axis=-1, keepdims=True)
    return (dz - m1 - xh * m2) * rs[:, 0:1], dg, db


def local_copies(pairs, sems, first=0):
    copies = [pltpu.make_async_copy(s, d, sems.at[first + i]) for i, (s, d) in enumerate(pairs)]
    for copy in copies:
        copy.start()
    return copies


def gelu_parts(u):
    phi = 0.5 * (1.0 + lax.erf(u * (1.0 / math.sqrt(2.0))))
    density = jnp.exp(u * u * -0.5) * (1.0 / math.sqrt(2.0 * math.pi))
    return u * phi, phi + u * density


def softmax(scores):
    top = jnp.max(scores, axis=-1, keepdims=True)
    e = jnp.exp(scores - top)
    return e / jnp.sum(e, axis=-1, keepdims=True)


def iota2(shape, dim):
    return lax.broadcasted_iota(jnp.int32, shape, dim)


def key_mask(queries, keys, count):
    return iota2((queries, keys), 1) < count


def head_masks(rows, width, size):
    lane = iota2((rows, width), 1)
    return [(lane >= h * size) & (lane < (h + 1) * size) for h in range(width // size)]


def pick(mask, x):
    return jnp.where(mask, x, jnp.zeros_like(x))


def attn_fwd(q, k, v, mask, heads, size):
    out = []
    for h in range(heads):
        s = slice(h * size, (h + 1) * size)
        scores = mm_nt(q[:, s], k[:, s]) * (1.0 / math.sqrt(size))
        p = softmax(jnp.where(mask, scores, masked_score))
        out.append(mm(p.astype(BF16), v[:, s]).astype(BF16))
    return jnp.concatenate(out, axis=1)


def attn_bwd(q, k, v, dm, mask, heads, size):
    dq, dk, dv = [], [], []
    for h in range(heads):
        s = slice(h * size, (h + 1) * size)
        scale = 1.0 / math.sqrt(size)
        scores = mm_nt(q[:, s], k[:, s]) * scale
        p = softmax(jnp.where(mask, scores, masked_score))
        dp = mm_nt(dm[:, s], v[:, s])
        dv.append(mm_tn(p.astype(BF16), dm[:, s]).astype(BF16))
        ds = p * (dp - jnp.sum(dp * p, axis=-1, keepdims=True))
        dr = (ds * scale).astype(BF16)
        dq.append(mm(dr, k[:, s]).astype(BF16))
        dk.append(mm_tn(dr, q[:, s]).astype(BF16))
    return tuple(jnp.concatenate(x, axis=1) for x in (dq, dk, dv))


def attn_fwd_small(q, k, v, mask, hm):
    total = None
    for m in hm:
        scores = mm_nt(pick(m, q), k) * (1.0 / math.sqrt(KT))
        p = softmax(jnp.where(mask, scores, masked_score))
        part = mm(p.astype(BF16), pick(m, v))
        total = part if total is None else total + part
    return total.astype(BF16)


def attn_bwd_small(q, k, v, dm, mask, hm):
    dq = dk = dv = None
    scale = 1.0 / math.sqrt(KT)
    for m in hm:
        scores = mm_nt(pick(m, q), k) * scale
        p = softmax(jnp.where(mask, scores, masked_score))
        dmh = pick(m, dm)
        dp = mm_nt(dmh, v)
        dvp = mm_tn(p.astype(BF16), dmh)
        ds = p * (dp - jnp.sum(dp * p, axis=-1, keepdims=True))
        dr = (ds * scale).astype(BF16)
        dqp = mm(dr, pick(m, k))
        dkp = mm_tn(dr, pick(m, q))
        dq, dk, dv = (dqp, dkp, dvp) if dq is None else (dq + dqp, dk + dkp, dv + dvp)
    return dq.astype(BF16), dk.astype(BF16), dv.astype(BF16)


def split_rows(x, pairs):
    value = x[...].astype(F32)
    pairs[...] = jnp.zeros(pairs.shape, F32)
    pairs[0, 0:RG] = value[0:RG]
    pairs[1, 0:RG] = value[RG:]


def join_rows(pairs, out):
    out[...] = jnp.concatenate([pairs[0, 0:RG], pairs[1, 0:RG]], axis=0).astype(out.dtype)


def put(ref, m, rows, value, cols=None):
    value = value.reshape(2, value.shape[0] // 2, value.shape[1])
    if cols is None:
        ref[m, rows] = value
    else:
        ref[m, rows, :, cols] = value


def take(ref, m, rows):
    value = ref[m, rows]
    return value.reshape(2 * value.shape[1], value.shape[2])


def wide(m):
    return -(-m // 128) * 128

def weight_groups(ws):
    return ws[0:6], ws[6:10], ws[10:12] + ws[14:16], ws[12:14] + ws[16:18]


def saved_shapes(n, m, f, fi):
    text, image = (2, 4, LT, DT), (2, 4, RP, DV)
    att = [text, image, (2, 4, LT, 3 * n), (2, 4, RP, 3 * n), (2, 4, LT, n), (2, 4, RP, n)]
    ff = [text, image, (2, 4, LT, f), (2, 4, LT, f), (2, 4, RP, fi), (2, 4, RP, fi)]
    assert wide(m) == n
    return [att, ff, att, ff]


SAVED = [6, 6, 6, 6]
NORM_SAVED = [(2, LT, DT), (2, RP, DV), (2, LT, 128), (2, RP, 128)]


def fwd_kernel(*refs):
    refs = list(refs)

    def grab(count):
        got = refs[:count]
        del refs[:count]
        return got

    tl, rc, xt, xi = grab(4)
    weights = grab(18)
    gains = grab(4)
    ot, oi = grab(2)
    saved_out = [grab(k) for k in SAVED]
    norm_out = [grab(4) for _ in range(4)]
    vw = grab(18)
    saved = [grab(k) for k in SAVED]
    norms = [grab(4) for _ in range(4)]
    rt, ri = grab(2)
    wsem, osem = grab(2)
    tg, tb, ig, ib = gains
    at = Places()
    loading = local_copies(list(zip(weights, vw)), wsem)
    text, image = make_streams(at, refs)
    image.clear([group[1] for group in saved])
    greet(at)
    co_w, cf_w, sa_w, sf_w = weight_groups(vw)

    split_rows(xi, ri)
    for m in range(2):
        image.begin(saved[0][1], m, ri[m].astype(BF16))
        rt[m] = xt[m].astype(F32)
        text.begin(saved[0][0], m, xt[m])

    storing = []

    def finish(s, last=False):
        slots_t, slots_i = saved[s][0], saved[s][1]
        xht, xhi, rst, rsi = norms[s]

        @pl.loop(0, 2)
        def _(m):
            yi = norm(ri[m] + image.total(m), ig[s : s + 1, :], ib[s : s + 1, :], xhi, rsi, m)
            image.end(slots_i, m)
            yt = norm(rt[m] + text.total(m), tg[s : s + 1, :], tb[s : s + 1, :], xht, rst, m)
            text.end(slots_t, m)
            if last:
                ri[m] = yi
                ot[m] = yt.astype(BF16)
            else:
                image.begin(saved[s + 1][1], m, yi.astype(BF16))
                text.begin(saved[s + 1][0], m, yt.astype(BF16))
                ri[m] = yi
                rt[m] = yt

        storing.extend(
            local_copies(
                list(zip(saved[s], saved_out[s])) + list(zip(norms[s], norm_out[s])), osem, 12 * s
            )
        )
        if last:
            join_rows(ri, oi)

    slots_t, slots_i, spt, spi, smt, smi = saved[0]
    wqt, wkvi, wot, wqi, wkvt, woi = co_w
    n = wqt.shape[1]
    heads = n // KC
    for c in loading[0:6]:
        c.wait()

    def co(half, m, rows):
        x = take(slots_i, m, rows)
        put(spi, m, rows, mm(x, wqi[...]).astype(BF16), slice(0, n))
        put(spi, m, rows, mm(x, wkvi[0]).astype(BF16), slice(n, 2 * n))
        put(spi, m, rows, mm(x, wkvi[1]).astype(BF16), slice(2 * n, 3 * n))
        x = take(slots_t, m, rows)
        put(spt, m, rows, mm(x, wqt[...]).astype(BF16), slice(0, n))
        put(spt, m, rows, mm(x, wkvt[0]).astype(BF16), slice(n, 2 * n))
        put(spt, m, rows, mm(x, wkvt[1]).astype(BF16), slice(2 * n, 3 * n))
        for j in range(2):
            b = at.base(half) + j
            t, v = spt[m, b], spi[m, b]
            smt[m, b] = attn_fwd(t[:, 0:n], v[:, n : 2 * n], v[:, 2 * n :],
                                 key_mask(LT, RP, rc[2 * b + m]), heads, KC)
            smi[m, b] = attn_fwd(v[:, 0:n], t[:, n : 2 * n], t[:, 2 * n :],
                                 key_mask(RP, LT, tl[2 * b + m]), heads, KC)
        image.partial(half, m, mm(take(smi, m, rows), woi[...]))
        text.partial(half, m, mm(take(smt, m, rows), wot[...]))

    steps(text, image, slots_t, slots_i, co)
    finish(0)

    def feed(s, w):
        slots_t, slots_i, sat, spt, sai, spi = saved[s]
        wti, wto, wii, wio = w

        def compute(half, m, rows):
            act, slope = gelu_parts(mm(take(slots_i, m, rows), wii[...]))
            act = act.astype(BF16)
            put(sai, m, rows, act)
            put(spi, m, rows, slope.astype(BF16))
            image.partial(half, m, mm(act, wio[...]))
            act, slope = gelu_parts(mm(take(slots_t, m, rows), wti[...]))
            act = act.astype(BF16)
            put(sat, m, rows, act)
            put(spt, m, rows, slope.astype(BF16))
            text.partial(half, m, mm(act, wto[...]))

        steps(text, image, slots_t, slots_i, compute)

    for c in loading[6:]:
        c.wait()
    feed(1, cf_w)
    finish(1)

    slots_t, slots_i, sqt, sqi, sst, ssi = saved[2]
    wt, wto, wi, wio = sa_w
    km = wt.shape[1]
    ks = wide(km)
    hm = head_masks(LT, km, KT)

    def own(half, m, rows):
        x = take(slots_i, m, rows)
        for i in range(3):
            put(sqi, m, rows, mm(x, wi[i]).astype(BF16), slice(i * n, (i + 1) * n))
        x = take(slots_t, m, rows)
        for i in range(3):
            put(sqt, m, rows, mm_nt(x, wt[i]).astype(BF16), slice(i * ks, i * ks + km))
        for j in range(2):
            b = at.base(half) + j
            v = sqi[m, b]
            ssi[m, b] = attn_fwd(v[:, 0:n], v[:, n : 2 * n], v[:, 2 * n :],
                                 key_mask(RP, RP, rc[2 * b + m]), n // KV, KV)
            q, k, v = (sqt[m, b, :, i * ks : i * ks + km] for i in range(3))
            sst[m, b, :, 0:km] = attn_fwd_small(
                q, k, v, key_mask(LT, LT, tl[2 * b + m]), hm)
        image.partial(half, m, mm(take(ssi, m, rows), wio[...]))
        text.partial(half, m, mm(take(sst, m, rows)[:, 0:km], wto[...]))

    steps(text, image, slots_t, slots_i, own)
    finish(2)
    feed(3, sf_w)
    finish(3, True)
    for c in storing:
        c.wait()


def sds(shape, dtype=F32):
    return jax.ShapeDtypeStruct(shape, dtype)


def forward(tl, rc, xt, xi, weights, gains):
    n, m = weights[0].shape[1], weights[10].shape[1]
    f, fi = weights[6].shape[1], weights[8].shape[1]
    saved = saved_shapes(n, m, f, fi)
    flat = [s for group in saved for s in group]
    outs = (
        [sds((2, LT, DT), BF16), sds((2 * RG, DV), BF16)]
        + [sds(s, BF16) for s in flat]
        + [sds(s) for _ in range(4) for s in NORM_SAVED]
    )
    scratch = (
        [pltpu.VMEM(w.shape, BF16) for w in weights]
        + [pltpu.VMEM(s, BF16) for s in flat]
        + [pltpu.VMEM(s, F32) for _ in range(4) for s in NORM_SAVED]
        + [pltpu.VMEM((2, LT, DT), F32), pltpu.VMEM((2, RP, DV), F32)]
        + [pltpu.SemaphoreType.DMA((18,)), pltpu.SemaphoreType.DMA((48,))]
        + COMM
    )
    got = pl.pallas_call(
        fwd_kernel,
        out_shape=outs,
        in_specs=[SM] * 2 + [VM] * 2 + [ANY] * 18 + [VM] * 4,
        out_specs=[VM] * 2 + [ANY] * (sum(SAVED) + 16),
        scratch_shapes=scratch,
        compiler_params=pltpu.CompilerParams(
            collective_id=1, has_side_effects=True, vmem_limit_bytes=VMEM_LIMIT
        ),
        cost_estimate=pl.CostEstimate(flops=10**10, bytes_accessed=60 << 20, transcendentals=0),
        name="forward",
    )(tl, rc, xt, xi, *weights, *gains)
    got = list(got)
    kept = [[got.pop(2) for _ in range(k)] for k in SAVED]
    return got[0], got[1], kept, [got[2 + 4 * s : 6 + 4 * s] for s in range(4)]


def weight_grad(x, d, dw, dst, src=None):
    width = x.shape[3]
    blocks = width // 384 if width % 384 == 0 else width // 256
    cut = width // blocks
    per = 4 // blocks

    @pl.loop(0, blocks)
    def _(j):
        left = x[:, :, :, pl.ds(pl.multiple_of(j * cut, 128), cut)]
        left = left.reshape(-1, cut)
        right = d[...] if src is None else d[:, :, :, src]
        right = right.reshape(left.shape[0], right.shape[-1])
        got = mm_tn(left, right).astype(BF16)
        dw[pl.ds(j * per, per), :, :, dst] = got.reshape(per, 2, width // 8, got.shape[1])


class Depth:
    def __init__(self):
        self.p = lax.axis_index("dp")
        self.z, self.y = lax.div(self.p, 2), lax.rem(self.p, 2)
        self.y_mate = 2 * self.z + 1 - self.y

    def greet(self, at):
        barrier = pltpu.get_barrier_semaphore()

        def hello(who):
            pl.semaphore_signal(barrier, inc=1, device_id=who, device_id_type=MESH)

        hello({"tensor": at.core_mate})
        hello({"tensor": at.chip_mate})
        hello({"dp": self.y_mate})
        hello({"dp": lax.rem(self.p + 4, 8)})
        pl.when(self.z < 3)(lambda: hello({"dp": self.p + 2}))
        pl.when(self.z > 0)(lambda: hello({"dp": self.p - 2}))
        pl.semaphore_wait(barrier, 4 + (self.z + 2) // 3 + (5 - self.z) // 3)


def add_rows(dst, src):
    @pl.loop(0, dst.shape[0] // 16)
    def _(i):
        r = pl.ds(pl.multiple_of(i * 16, 16), 16)
        dst[r, :] = (dst[r, :].astype(F32) + src[r, :].astype(F32)).astype(BF16)


class Unit:
    def __init__(self, depth, index, dw, cols, from_y, from_z, z_first, waits, frees, sems, out, osem):
        self.d, self.k, self.dw, self.cols = depth, index, dw, cols
        self.from_y, self.from_z, self.z_first = from_y, from_z, z_first
        self.waits, self.frees = waits, frees
        self.ysem, self.zsem, self.ycredit, self.zcredit = sems
        self.out, self.osem = out, osem

    def mine(self, t, y):
        return self.dw.at[t, y, :, self.cols]

    def y_copy(self):
        d = self.d
        src = self.mine(d.z, 1 - d.y) if self.z_first else self.dw.at[:, 1 - d.y, :, self.cols]
        return pltpu.make_async_remote_copy(
            src_ref=src,
            dst_ref=self.from_y,
            send_sem=self.ysem.at[0, self.k],
            recv_sem=self.ysem.at[1, self.k],
            device_id={"dp": d.y_mate},
            device_id_type=MESH,
        )

    def z_copy(self, flow, step, t, to):
        src = self.dw.at[t, :, :, self.cols] if self.z_first else self.mine(t, self.d.y)
        return pltpu.make_async_remote_copy(
            src_ref=src,
            dst_ref=self.from_z.at[flow, step],
            send_sem=self.zsem.at[0, self.k, flow, step],
            recv_sem=self.zsem.at[1, self.k, flow, step],
            device_id={"dp": to},
            device_id_type=MESH,
        )

    def send(self, step):
        d = self.d
        w = 3 - d.z
        if step == 0 and self.waits:
            pl.semaphore_wait(self.zcredit.at[self.k], (d.z + 2) // 3 + (5 - d.z) // 3)
        pl.when(d.z <= step)(lambda: self.z_copy(0, step, 3 - step + d.z, d.p + 2).start())
        pl.when(w <= step)(lambda: self.z_copy(1, step, step - w, d.p - 2).start())

    def receive(self, step):
        d = self.d
        w = 3 - d.z

        def add(t, got):
            if self.z_first:
                for y in range(2):
                    add_rows(self.mine(t, y), got.at[y])
            else:
                add_rows(self.mine(t, d.y), got)

        def right():
            t = 2 - step + d.z
            self.z_copy(0, step, t, d.p).wait_recv()
            add(t, self.from_z.at[0, step])

        def left():
            t = 1 + step - w
            self.z_copy(1, step, t, d.p).wait_recv()
            add(t, self.from_z.at[1, step])

        pl.when((d.z >= 1) & (d.z - 1 <= step))(right)
        pl.when((w >= 1) & (w - 1 <= step))(left)
        if step == 2 and self.frees is not None:

            def free(to):
                pl.semaphore_signal(
                    self.zcredit.at[self.frees], inc=1, device_id={"dp": to}, device_id_type=MESH
                )

            pl.when(d.z < 3)(lambda: free(d.p + 2))
            pl.when(d.z > 0)(lambda: free(d.p - 2))

    def take_y(self):
        d = self.d
        self.y_copy().wait_recv()
        if self.z_first:
            add_rows(self.mine(d.z, d.y), self.from_y)
            return

        @pl.loop(0, 4)
        def _(t):
            add_rows(self.mine(t, d.y), self.from_y.at[t])

        if self.frees is not None and not self.z_first:
            pl.semaphore_signal(
                self.ycredit.at[self.frees], inc=1, device_id={"dp": d.y_mate}, device_id_type=MESH
            )

    def give_y(self):
        if self.waits == "both":
            pl.semaphore_wait(self.ycredit.at[self.k], 1)
        self.y_copy().start()

    def task(self, name):
        if name == "start":
            if self.z_first:
                self.send(0)
            else:
                self.give_y()
        elif name == "S":
            self.take_y()
            self.send(0)
        elif name in ("r0", "r1"):
            self.receive(int(name[1]))
            self.send(int(name[1]) + 1)
        elif name == "r2":
            self.receive(2)
            self.give_y()
        else:
            if self.z_first:
                self.take_y()
            else:
                self.receive(2)
            self.copy_out().start()

    def copy_out(self):
        return pltpu.make_async_copy(self.mine(self.d.z, self.d.y), self.out, self.osem.at[self.k])

    def end(self):
        d = self.d
        w = 3 - d.z
        self.copy_out().wait()
        self.y_copy().wait_send()
        for step in range(3):
            pl.when(d.z <= step)(self.z_copy(0, step, 0, d.p).wait_send)
            pl.when(w <= step)(self.z_copy(1, step, 0, d.p).wait_send)


UNITS = ["sf1", "sf2", "sfi", "sa1", "sai", "cf1", "cf2", "cfi", "coi", "co1"]

PLAN = [
    ("0g", "sf1 start"), ("0h", "sf2 start"), ("0e", "sfi start"),
    ("1c", "sf1 S"),
    ("1d", "sf1 r0"),
    ("1e", "sa1 start", "sai start"),
    ("2a", "sf1 r1", "sf2 S"),
    ("2c", "sfi S", "sai r0", "sf1 F"),
    ("2d", "sf2 r0", "sa1 S"),
    ("2e", "cf2 start", "cf1 start", "cfi start", "sfi r0", "sf2 r1"),
    ("3a", "n 0", "sai r1"), ("3b", "n 1", "sf2 F"), ("3f", "sfi r1"),
    ("3c", "n 2", "sa1 r0", "cf2 S"),
    ("3d", "n 3", "sfi F"),
    ("3e", "co1 start", "coi start", "n 4", "cf1 S", "sa1 r1"),
    ("t", "n 5", "sai r2", "cf2 r0", "cf1 r0", "cfi S", "sa1 F", "cf2 r1", "cf1 r1", "cfi r0", "cf2 F", "co1 S",
     "cf1 F", "cfi r1", "co1 r0", "cfi F", "co1 r1", "coi S", "sai F", "co1 F", "coi r0", "coi r1", "coi F"),
]


class NormSum:
    def __init__(self, at, depth, text, image, got_t, got_i, sems):
        p, z, y = depth.p, depth.z, depth.y
        self.text, self.image, self.got_t, self.got_i, self.sems = text, image, got_t, got_i, sems
        self.to = [
            {"tensor": at.core_mate},
            {"tensor": at.chip_mate},
            {"dp": depth.y_mate},
            {"dp": 2 * (z + 1 - 2 * lax.rem(z, 2)) + y},
            {"dp": lax.rem(p + 4, 8)},
        ]

    def copies(self, k):
        return [
            pltpu.make_async_remote_copy(
                src_ref=src.at[k],
                dst_ref=dst.at[k],
                send_sem=self.sems.at[0, i, k],
                recv_sem=self.sems.at[1, i, k],
                device_id=self.to[k],
                device_id_type=MESH,
            )
            for i, (src, dst) in enumerate(((self.text, self.got_t), (self.image, self.got_i)))
        ]

    def task(self, k):
        if k > 0:
            for c in self.copies(k - 1):
                c.wait_recv()
            self.text[k] = self.text[k - 1] + self.got_t[k - 1]
            self.image[k] = self.image[k - 1] + self.got_i[k - 1]
        if k < 5:
            for c in self.copies(k):
                c.start()

    def end(self):
        for k in range(5):
            for c in self.copies(k):
                c.wait_send()


def bwd_kernel(fast, *refs):
    refs = list(refs)

    def grab(count):
        got = refs[:count]
        del refs[:count]
        return got

    tl, rc, dt, di = grab(4)
    tg, ig = grab(2)
    weights = grab(18)
    saved_in = [grab(k) for k in SAVED]
    norm_in = [grab(4) for _ in range(4)]
    ot, oi, gbt, gbi = grab(4)
    grads_out = grab(len(UNITS)) if fast else [grab(2) for _ in range(4)]
    vff, vsa, vco = grab(4), grab(4), grab(6)
    feed_saved, att_saved = grab(4), grab(4)
    vxt, vxi = grab(2)
    xht, xhi, rst, rsi = grab(4)
    slots = [grab(2), grab(2)]
    dpt, dpi, dui = grab(3)
    dut = dpt
    kt, ki = grab(2)
    dw = [grab(2) for _ in range(4)]
    lsem, osem = grab(2)
    at = Places()
    co_w, cf_w, sa_w, sf_w = weight_groups(weights)
    if fast:
        depth = Depth()
        buffers = grab(11)
        y0, z0, y1, z1 = buffers[0:3], buffers[3:6], buffers[6:8], buffers[8:10]
        sums = grab(4)
        nt, ni, got_nt, got_ni, nsem = grab(5)
        nsum = NormSum(at, depth, nt, ni, got_nt, got_ni, nsem)

        def made(name, s, i, cols, from_y, from_z, z_first=False, waits=None, frees=None):
            k = UNITS.index(name)
            units[name] = Unit(depth, k, dw[s][i], cols, from_y, from_z, z_first, waits,
                               None if frees is None else UNITS.index(frees), sums, grads_out[k], osem)

        units = {}
        ff = dw[3][0].shape[3] // 2
        wide_t = {s: dw[s][0].shape[3] for s in (0, 2)}
        for pre, s, waits in (("sf", 3, None), ("cf", 1, "both")):
            frees = [None] * 3 if waits else ["cf1", "cf2", "cfi"]
            made(pre + "1", s, 0, pl.ds(0, ff), y0[0], z0[0], False, waits, frees[0])
            made(pre + "2", s, 0, pl.ds(ff, ff), y0[1], z0[1], False, waits, frees[1])
            made(pre + "i", s, 1, pl.ds(0, dw[s][1].shape[3]), y0[2], z0[2], False, waits, frees[2])
        cols = pl.ds(0, wide_t[2])
        made("sa1", 2, 0, cols, y1[0].at[:, :, cols], z1[0].at[:, :, :, cols], frees="co1")
        cols = pl.ds(0, dw[2][1].shape[3])
        made("sai", 2, 1, cols, buffers[10], z1[1], True, frees="coi")
        made("coi", 0, 1, cols, y1[1], z1[1].at[:, :, 0], waits="z")
        made("co1", 0, 0, pl.ds(0, wide_t[0]), y1[0], z1[0], waits="both")

    def place(where):
        def go():
            for entry in PLAN:
                if entry[0] == where:
                    for name, task in (x.split() for x in entry[1:]):
                        if name == "n":
                            nsum.task(int(task))
                        else:
                            units[name].task(task)

        return go if fast else (lambda: None)

    def places(cycle):
        named = {entry[0] for entry in PLAN} if fast else ()
        return [place(cycle + x) if cycle + x in named else None for x in ("a", "b", "f", "c")]

    count = [0]

    def load(pairs):
        copies = local_copies(pairs, lsem, count[0])
        count[0] += len(pairs)
        return copies

    def done(copies):
        for c in copies:
            c.wait()

    vnorm = [xht, xhi, rst, rsi]
    norm_load = load(list(zip(norm_in[3], vnorm)))
    feed_load = load(list(zip(sf_w, vff)) + list(zip(saved_in[3][2:], feed_saved)))
    x_load = load(list(zip(saved_in[3][:2], (vxt, vxi))))
    sa_load = load(list(zip(sa_w, vsa)) + list(zip(saved_in[2][2:], att_saved)))
    co_load = load(list(zip(co_w, vco)))
    text, image = make_streams(at, refs)
    image.clear([pair[1] for pair in slots])
    if fast:
        depth.greet(at)
        acc_t, acc_i = nt.at[0], ni.at[0]
    else:
        greet(at)
        acc_t, acc_i = gbt, gbi
    acc_t[...] = jnp.zeros_like(acc_t)
    acc_i[...] = jnp.zeros_like(acc_i)

    def enter(s, m, gi, gt, slots_t, slots_i):
        dx, dg, db = norm_back(gi, xhi[m], rsi[m], ig[s : s + 1, :])
        ki[m] = dx
        image.begin(slots_i, m, dx.astype(BF16))
        acc_i[s : s + 1, :] += dg
        acc_i[4 + s : 5 + s, :] += db
        dx, dg, db = norm_back(gt, xht[m], rst[m], tg[s : s + 1, :])
        kt[m] = dx
        text.begin(slots_t, m, dx.astype(BF16))
        acc_t[s : s + 1, :] += dg
        acc_t[4 + s : 5 + s, :] += db

    done(norm_load)
    split_rows(di, ki)

    @pl.loop(0, 2)
    def _(m):
        enter(3, m, ki[m], dt[m].astype(F32), *slots[0])

    norm_load = load(list(zip(norm_in[2], vnorm)))

    def finish(s, norm_load):
        if s > 0:
            done(norm_load)
        slots_t, slots_i = slots[(3 - s) % 2]

        @pl.loop(0, 2)
        def _(m):
            gi = ki[m] + image.total(m)
            image.end(slots_i, m)
            gt = kt[m] + text.total(m)
            text.end(slots_t, m)
            if s == 0:
                ki[m] = gi
                ot[m] = gt.astype(BF16)
            else:
                enter(s - 1, m, gi, gt, *slots[(4 - s) % 2])

        if s == 0:
            join_rows(ki, oi)
        if s > 1:
            return load(list(zip(norm_in[s - 2], vnorm)))
        return None

    storing = []

    def feed(s, feed_load, x_load, cycle):
        wti, wto, wii, wio = vff
        sat, spt, sai, spi = feed_saved
        slots_t, slots_i = slots[(3 - s) % 2]
        done(feed_load)

        def compute(half, m, rows):
            du = (mm_nt(take(slots_i, m, rows), wio[...]) * take(spi, m, rows).astype(F32)).astype(BF16)
            put(dui, m, rows, du)
            image.partial(half, m, mm_nt(du, wii[...]))
            du = (mm_nt(take(slots_t, m, rows), wto[...]) * take(spt, m, rows).astype(F32)).astype(BF16)
            put(dut, m, rows, du)
            text.partial(half, m, mm_nt(du, wti[...]))

        steps(text, image, slots_t, slots_i, compute, places(cycle))
        done(x_load)
        place(cycle + "d")()
        dwt, dwi = dw[s]
        f, fi = wti.shape[1], wii.shape[1]
        weight_grad(vxt, dut, dwt, slice(0, f))
        place(cycle + "g")()
        weight_grad(slots_t, sat, dwt, slice(f, 2 * f))
        place(cycle + "h")()
        weight_grad(vxi, dui, dwi, slice(0, fi))
        weight_grad(slots_i, sai, dwi, slice(fi, 2 * fi))

    def send_grads(s):
        if not fast:
            storing.extend(local_copies(list(zip(dw[s], grads_out[s])), osem, 2 * s))

    feed(3, feed_load, x_load, "0")
    send_grads(3)
    place("0e")()
    x_load = load(list(zip(saved_in[2][:2], (vxt, vxi))))
    feed_load = load(list(zip(cf_w, vff)) + list(zip(saved_in[1][2:], feed_saved)))
    norm_load = finish(3, norm_load)

    wt, wto, wi, wio = vsa
    sqt, sqi, sst, ssi = att_saved
    n, km = wi.shape[2], wt.shape[1]
    ks = wide(km)
    hm = head_masks(LT, km, KT)
    own_t, own_i = slots[1]
    done(sa_load)

    def own(half, m, rows):
        dm = mm_nt(take(own_i, m, rows), wio[...]).astype(BF16)
        dmt = mm_nt(take(own_t, m, rows), wto[...]).astype(BF16)
        for j in range(2):
            b = at.base(half) + j
            v = sqi[m, b]
            grads = attn_bwd(v[:, 0:n], v[:, n : 2 * n], v[:, 2 * n :], dm[j * RP : (j + 1) * RP],
                             key_mask(RP, RP, rc[2 * b + m]), n // KV, KV)
            for i, g in enumerate(grads):
                dpi[m, b, :, i * n : (i + 1) * n] = g
            q, k, v = (sqt[m, b, :, i * ks : i * ks + km] for i in range(3))
            grads = attn_bwd_small(q, k, v, dmt[j * LT : (j + 1) * LT],
                                   key_mask(LT, LT, tl[2 * b + m]), hm)
            for i, g in enumerate(grads):
                dpt[m, b, :, i * ks : i * ks + km] = g
        dp = take(dpi, m, rows)
        image.partial(half, m, sum(mm_nt(dp[:, i * n : (i + 1) * n], wi[i]) for i in range(3)))
        dp = take(dpt, m, rows)
        text.partial(half, m, sum(mm(dp[:, i * ks : i * ks + km], wt[i]) for i in range(3)))

    steps(text, image, own_t, own_i, own, places("1"))
    done(x_load)
    place("1d")()
    dwt, dwi = dw[2]
    for i in range(3):
        weight_grad(vxt, dpt, dwt, slice(i * km, (i + 1) * km), slice(i * ks, i * ks + km))
    weight_grad(own_t, sst, dwt, slice(3 * km, 4 * km), slice(0, km))
    weight_grad(vxi, dpi, dwi, slice(0, 3 * n))
    weight_grad(own_i, ssi, dwi, slice(3 * n, 4 * n))
    send_grads(2)
    place("1e")()
    x_load = load(list(zip(saved_in[1][:2], (vxt, vxi))))
    co_load += load(list(zip(saved_in[0][2:], att_saved)))
    norm_load = finish(2, norm_load)

    feed(1, feed_load, x_load, "2")
    send_grads(1)
    place("2e")()
    x_load = load(list(zip(saved_in[0][:2], (vxt, vxi))))
    finish(1, norm_load)

    wqt, wkvi, wot, wqi, wkvt, woi = vco
    heads = n // KC
    co_t, co_i = slots[1]
    done(co_load)

    def co(half, m, rows):
        dm = mm_nt(take(co_i, m, rows), woi[...]).astype(BF16)
        dmt = mm_nt(take(co_t, m, rows), wot[...]).astype(BF16)
        for j in range(2):
            b = at.base(half) + j
            t, v = sqt[m, b], sqi[m, b]
            dq, dk, dv = attn_bwd(v[:, 0:n], t[:, n : 2 * n], t[:, 2 * n :], dm[j * RP : (j + 1) * RP],
                                  key_mask(RP, LT, tl[2 * b + m]), heads, KC)
            dpi[m, b, :, 0:n] = dq
            dpt[m, b, :, n : 2 * n] = dk
            dpt[m, b, :, 2 * n :] = dv
            dq, dk, dv = attn_bwd(t[:, 0:n], v[:, n : 2 * n], v[:, 2 * n :], dmt[j * LT : (j + 1) * LT],
                                  key_mask(LT, RP, rc[2 * b + m]), heads, KC)
            dpt[m, b, :, 0:n] = dq
            dpi[m, b, :, n : 2 * n] = dk
            dpi[m, b, :, 2 * n :] = dv
        dp = take(dpi, m, rows)
        image.partial(half, m, mm_nt(dp[:, 0:n], wqi[...]) + mm_nt(dp[:, n : 2 * n], wkvi[0])
                      + mm_nt(dp[:, 2 * n :], wkvi[1]))
        dp = take(dpt, m, rows)
        text.partial(half, m, mm_nt(dp[:, 0:n], wqt[...]) + mm_nt(dp[:, n : 2 * n], wkvt[0])
                     + mm_nt(dp[:, 2 * n :], wkvt[1]))

    steps(text, image, co_t, co_i, co, places("3"))
    done(x_load)
    place("3d")()
    dwt, dwi = dw[0]
    weight_grad(vxt, dpt, dwt, slice(0, 3 * n))
    weight_grad(co_t, sst, dwt, slice(3 * n, 4 * n))
    weight_grad(vxi, dpi, dwi, slice(0, 3 * n))
    weight_grad(co_i, ssi, dwi, slice(3 * n, 4 * n))
    send_grads(0)
    place("3e")()
    finish(0, None)
    place("t")()
    if fast:
        gbt[...] = nt[5]
        gbi[...] = ni[5]
        nsum.end()
        for unit in units.values():
            unit.end()
    done(storing)


def backward(fast, tl, rc, dt, di, weights, gains, saved, norms):
    n, m = weights[0].shape[1], weights[10].shape[1]
    f, fi = weights[6].shape[1], weights[8].shape[1]
    tg, _, ig, _ = gains
    co_w, cf_w, sa_w, sf_w = weight_groups(list(weights))
    text_cols = (4 * n, 2 * f, 4 * m, 2 * f)
    image_cols = (4 * n, 2 * fi, 4 * n, 2 * fi)
    rt, ri = DT // 8, DV // 8
    dw_shapes = [s for i in range(4) for s in ((4, 2, rt, text_cols[i]), (4, 2, ri, image_cols[i]))]
    text, image = (2, 4, LT, DT), (2, 4, RP, DV)
    outs = [sds((2, LT, DT), BF16), sds((2 * RG, DV), BF16), sds((8, DT)), sds((8, DV))]
    blocks = {
        "sf1": (rt, f), "sf2": (rt, f), "sfi": (ri, 2 * fi), "sa1": (rt, 4 * m), "sai": (ri, 4 * n),
        "cf1": (rt, f), "cf2": (rt, f), "cfi": (ri, 2 * fi), "coi": (ri, 4 * n), "co1": (rt, 4 * n),
    }
    outs += [sds(blocks[u], BF16) for u in UNITS] if fast else [sds(s, BF16) for s in dw_shapes]
    sums = []
    if fast:
        tc = max(4 * n, 4 * m)
        shapes = [
            (4, rt, f), (4, rt, f), (4, ri, 2 * fi), (2, 3, rt, f), (2, 3, rt, f), (2, 3, ri, 2 * fi),
            (4, rt, tc), (4, ri, 4 * n), (2, 3, rt, tc), (2, 3, 2, ri, 4 * n), (ri, 4 * n),
        ]
        k = len(UNITS)
        sums = (
            [pltpu.VMEM(s, BF16) for s in shapes]
            + [pltpu.SemaphoreType.DMA((2, k)), pltpu.SemaphoreType.DMA((2, k, 2, 3)),
               pltpu.SemaphoreType.REGULAR((k,)), pltpu.SemaphoreType.REGULAR((k,))]
            + [pltpu.VMEM((6, 8, w), F32) for w in (DT, DV)]
            + [pltpu.VMEM((5, 8, w), F32) for w in (DT, DV)]
            + [pltpu.SemaphoreType.DMA((2, 2, 5))]
        )
    buffers = (
        [w.shape for w in cf_w] + [w.shape for w in sa_w] + [w.shape for w in co_w]
        + [x.shape for x in saved[1][2:]] + [x.shape for x in saved[0][2:]]
        + [text, image]
    )
    scratch = (
        [pltpu.VMEM(s, BF16) for s in buffers]
        + [pltpu.VMEM(s, F32) for s in NORM_SAVED]
        + [pltpu.VMEM(s, BF16) for s in (text, image, text, image)]
        + [pltpu.VMEM(s, BF16) for s in ((2, 4, LT, 3 * n), (2, 4, RP, 3 * n), (2, 4, RP, fi))]
        + [pltpu.VMEM((2, LT, DT), F32), pltpu.VMEM((2, RP, DV), F32)]
        + [pltpu.VMEM(s, BF16) for s in dw_shapes]
        + [pltpu.SemaphoreType.DMA((72,)), pltpu.SemaphoreType.DMA((40,))]
        + sums
        + COMM
    )
    got = pl.pallas_call(
        functools.partial(bwd_kernel, fast),
        out_shape=outs,
        in_specs=[SM] * 2 + [VM] * 4 + [ANY] * (18 + sum(SAVED) + 16),
        out_specs=[VM] * 4 + [ANY] * (len(outs) - 4),
        scratch_shapes=scratch,
        compiler_params=pltpu.CompilerParams(
            collective_id=2, has_side_effects=True, vmem_limit_bytes=VMEM_LIMIT
        ),
        cost_estimate=pl.CostEstimate(flops=2 * 10**10, bytes_accessed=60 << 20, transcendentals=0),
        name="backward",
    )(tl, rc, dt, di, tg, ig, *weights, *[x for g in saved for x in g], *[x for g in norms for x in g])
    return got[0:4], got[4:]


def last_kernel(yt, yi, gt, gi, nt, ni, *refs):
    block = dict(zip(UNITS, refs))
    outs = list(refs[len(UNITS) :])

    def out():
        return outs.pop(0)

    for x in (yt, yi, gt, gi):
        out()[...] = x[...]
    rt, ri = block["co1"].shape[0], block["coi"].shape[0]
    n, m = block["coi"].shape[1] // 4, block["sa1"].shape[1] // 4

    def part(name, i, size):
        return block[name][:, i * size : (i + 1) * size].astype(F32)

    def one(name, i, size, turn=False):
        value = part(name, i, size)
        out()[...] = value.T if turn else value

    def stack(name, first, count, size):
        ref = out()
        for i in range(count):
            ref[i] = part(name, first + i, size)

    one("co1", 0, n)
    stack("coi", 1, 2, n)
    one("co1", 3, n)
    one("coi", 0, n)
    stack("co1", 1, 2, n)
    one("coi", 3, n, True)
    one("cf1", 0, block["cf1"].shape[1])
    one("cf2", 0, block["cf2"].shape[1])
    one("cfi", 0, n)
    one("cfi", 1, n, True)
    stack("sa1", 0, 3, m)
    one("sa1", 3, m, True)
    one("sf1", 0, block["sf1"].shape[1])
    one("sf2", 0, block["sf2"].shape[1])
    stack("sai", 0, 3, n)
    one("sai", 3, n, True)
    one("sfi", 0, n)
    one("sfi", 1, n, True)
    for x in (nt, ni):
        out()[...] = x[0:4]
        out()[...] = x[4:8]


def last(yt, yi, gt, gi, nt, ni, blocks):
    shape = {u: b.shape for u, b in zip(UNITS, blocks)}
    rt, ri = shape["co1"][0], shape["coi"][0]
    n, m, f = shape["coi"][1] // 4, shape["sa1"][1] // 4, shape["sf1"][1]
    final = [
        (rt, n), (2, ri, n), (rt, n), (ri, n), (2, rt, n), (n, ri),
        (rt, f), (rt, f), (ri, n), (n, ri),
        (3, rt, m), (m, rt), (rt, f), (rt, f), (3, ri, n), (n, ri), (ri, n), (n, ri),
        (4, DT), (4, DT), (4, DV), (4, DV),
    ]
    outs = [sds(x.shape, BF16) for x in (yt, yi, gt, gi)] + [sds(s) for s in final]
    return pl.pallas_call(
        last_kernel,
        out_shape=outs,
        in_specs=[VM] * (6 + len(blocks)),
        out_specs=[VM] * len(outs),
        compiler_params=pltpu.CompilerParams(vmem_limit_bytes=VMEM_LIMIT),
        name="last",
    )(yt, yi, gt, gi, nt, ni, *blocks)


def local(dp, text_in, image_in, tl, rc, *rest):
    weights, gains, (text_cot, image_cot) = list(rest[:18]), rest[18:22], rest[22:]
    n, m, f = weights[0].shape[1], weights[10].shape[2], weights[6].shape[1]
    weights[10] = jnp.swapaxes(weights[10], 1, 2)
    rows, fast = (2, LT, DT), dp == 8
    yt, yi, saved, norms = forward(tl, rc, text_in.reshape(rows), image_in, weights, gains)
    (gt, gi, tgb, igb), grads = backward(
        fast, tl, rc, text_cot.reshape(rows), image_cot, weights, gains, saved, norms
    )
    if fast:
        yt, yi, gt, gi, *rest = last(yt, yi, gt, gi, tgb, igb, grads)
        grads, norm_grads = rest[:18], rest[18:]
        grads = [g.T if i in (2, 7, 13) else g for i, g in enumerate(grads)]
    else:
        tgb, igb = lax.psum((tgb, igb), ("dp", "tensor"))
        parts = []
        for g in grads:
            g = g.reshape(-1, g.shape[3])
            parts.append(lax.psum_scatter(g, "dp", scatter_dimension=0, tiled=True).astype(F32))
        ct, ci, ft, fi, st, si, ht, hi = parts
        grads = [
            ct[:, :n],
            jnp.stack([ci[:, n : 2 * n], ci[:, 2 * n : 3 * n]]),
            ct[:, 3 * n :].T,
            ci[:, :n],
            jnp.stack([ct[:, n : 2 * n], ct[:, 2 * n : 3 * n]]),
            ci[:, 3 * n :].T,
            ft[:, :f], ft[:, f:].T, fi[:, :n], fi[:, n:].T,
            jnp.stack([st[:, i * m : (i + 1) * m] for i in range(3)]),
            st[:, 3 * m :].T,
            ht[:, :f], ht[:, f:].T,
            jnp.stack([si[:, i * n : (i + 1) * n] for i in range(3)]),
            si[:, 3 * n :].T,
            hi[:, :n], hi[:, n:].T,
        ]
        norm_grads = tgb[0:4], tgb[4:8], igb[0:4], igb[4:8]
    return (
        yt.reshape(2 * LT, DT), yi, gt.reshape(2 * LT, DT), gi, *grads,
        *norm_grads,
    )


def solution(mesh):
    rows, pairs = P(("dp", "tensor"), None), P("dp")
    wide, tall, stack = P(None, "tensor"), P("tensor", None), P(None, None, "tensor")
    g_wide, g_tall, g_stack = P("dp", "tensor"), P("tensor", "dp"), P(None, "dp", "tensor")
    return jax.shard_map(
        functools.partial(local, mesh.shape["dp"]),
        mesh=mesh,
        in_specs=(
            rows, rows, pairs, pairs,
            wide, stack, tall, wide, stack, tall,
            wide, tall, wide, tall,
            stack, tall, wide, tall,
            stack, tall, wide, tall,
            P(), P(), P(), P(),
            rows, rows,
        ),
        out_specs=(
            rows, rows, rows, rows,
            g_wide, g_stack, g_tall, g_wide, g_stack, g_tall,
            g_wide, g_tall, g_wide, g_tall,
            g_stack, g_tall, g_wide, g_tall,
            g_stack, g_tall, g_wide, g_tall,
            P(), P(), P(), P(),
        ),
        check_vma=False,
    )
```
